32 devices in a mesh: doc: 4 (over y, x), seq: 8 (over z, core).
Axes of the slice: x: 2, y: 2, z: 4, core: 2. Of those that a mesh axis runs over, the one named last changes fastest.
Arguments:
- queries: bfloat16 [12288, 2048], P(('doc', 'seq')), parts along dimension 0, may hold values from -120 to 120
- keys: bfloat16 [12288, 2048], P(('doc', 'seq')), parts along dimension 0, may hold values from -4.1 to 4.1
- values: bfloat16 [12288, 2048], P(('doc', 'seq')), parts along dimension 0, may hold values from -6 to 6
- global_positions: int32 [256], P('doc'), parts along dimension 0, may hold values from 0 to 3070, as said below
- score_weight: float32 [2048], replicated, may hold values from -0.125 to 0.125
Outputs:
- token_scores: float32 [12288], P(('doc', 'seq')), parts along dimension 0
The draws below stay inside these ranges and needn't reach their ends.
There are 4 independent parts, one for each index of `doc`. The reference program is written for one: setup_inputs(seed, part) draws one part's arguments, and reference() takes and returns one part's arrays. A program takes and returns all parts, laid end to end along the dimension named above; an argument that names none is the same for every part. Nothing has to cross between parts.
Inputs may be any that keep to these rules, and one draw needn't show every extreme that they name: `global_positions`: 64 distinct positions in increasing order; the first is 0 and the last is 3070.
All inputs are finite; a program needn't handle non-finite values.
Results may differ from the reference program's by a relative error of at most 0.0023.
Values may be sent and summed in bfloat16 or wider, within the bound.
No kernel may reach another device: no remote copies, remote signals or barrier semaphores. Data moves between devices by JAX's collectives and lax.ppermute only.
A program may use at most 64 MiB of HBM per device.

```python
import jax
import jax.numpy as jnp
from jax import lax

D = 2048
HEADS = 16
BLK = 64
G = 64
TOK_DEV = 384
TOKENS = 3072
N_SEQ = 8


def positions_of(key):
    inner = jax.random.permutation(jax.random.fold_in(key, 7), TOKENS - 3)[:G - 2] + 1
    joined = jnp.concatenate([jnp.zeros((1,), jnp.int32), inner.astype(jnp.int32), jnp.full((1,), TOKENS - 2, jnp.int32)])
    return jnp.sort(joined)


def keys_of(key):
    base_keys = jnp.clip(jax.random.normal(jax.random.fold_in(key, 17), (TOKENS, D), jnp.float32), -4.0, 4.0)
    return base_keys


def draw_global_positions(key, part):
    return positions_of(key)


def draw_keys(key, part):
    return keys_of(key).astype(jnp.bfloat16)


def draw_queries(key, part):
    base_queries = jnp.clip(jax.random.normal(jax.random.fold_in(key, 19), (TOKENS, D), jnp.float32), -4.0, 4.0)
    loud_rows = jax.random.randint(jax.random.fold_in(key, 23), (TOKENS,), 0, 4) == 0
    base_queries = jnp.where(loud_rows[:, None], 30.0 * base_queries, base_queries)
    return base_queries.astype(jnp.bfloat16)


def steps_of(key, shape, pieces, least, top_value):
    gain = 1.0
    for position, shards_of in pieces:
        draws = jax.random.uniform(jax.random.fold_in(jax.random.fold_in(key, 6), position), (shards_of,), jnp.float32, least / len(pieces), top_value / len(pieces))
        gain = gain * jnp.repeat(jnp.exp(draws), shape[position] // shards_of).reshape((-1,) + (1,) * (len(shape) - 1 - position))
    return gain


def gaussian(key, shape, spread, most, split=(), kind=jnp.bfloat16):
    array = jax.random.normal(key, shape, jnp.float32) * spread
    if len(split) > 0:
        array = steps_of(key, shape, split, -0.22, 0.18) * array
    return jnp.clip(array, min=-most, max=most).astype(kind)


def setup_inputs(seed: int = 0, part: int = 0) -> dict:
    streams_of = jax.random.split(jax.random.key(seed), 6)
    part_splits = jax.random.split(jax.random.fold_in(streams_of[5], part), 6)
    queries = draw_queries(jax.random.fold_in(jax.random.fold_in(streams_of[5], part), 71), part)
    keys = draw_keys(jax.random.fold_in(jax.random.fold_in(streams_of[5], part), 71), part)
    values = gaussian(part_splits[2], (TOKENS, D), 1.0, 6.0, ((0, 8),))
    global_positions = draw_global_positions(jax.random.fold_in(jax.random.fold_in(streams_of[5], part), 71), part)
    score_weight = gaussian(streams_of[4], (D,), D ** -0.5, 0.125, (), jnp.float32)
    return {"queries": queries, "keys": keys, "values": values, "global_positions": global_positions, "score_weight": score_weight}


def token_score(attended, score_weight):
    mean_square = lax.optimization_barrier(jnp.mean(attended * attended, axis=-1))
    return lax.optimization_barrier(jnp.sum(attended * score_weight, axis=-1)) * lax.rsqrt(mean_square + 1e-06)

def reference(queries, keys, values, global_positions, score_weight):
    head_size = D // HEADS
    score_scale = head_size ** (-0.5)
    block_count = TOKENS // BLK
    glob_queries = jnp.take(queries, global_positions, axis=0).astype(jnp.float32).reshape(G, HEADS, head_size)
    glob_keys = jnp.take(keys, global_positions, axis=0).astype(jnp.float32).reshape(G, HEADS, head_size)
    glob_values = jnp.take(values, global_positions, axis=0).astype(jnp.float32).reshape(G, HEADS, head_size)
    glob_block = (global_positions // BLK).astype(jnp.int32)
    query_blocks = queries.reshape(block_count, BLK, HEADS, head_size)
    zero_block = jnp.zeros((1, BLK, HEADS, head_size), keys.dtype)
    key_blocks = jnp.concatenate([zero_block, keys.reshape(block_count, BLK, HEADS, head_size), zero_block], axis=0)
    value_blocks = jnp.concatenate([zero_block, values.reshape(block_count, BLK, HEADS, head_size), zero_block], axis=0)

    def window_block(block_index):
        query_f = query_blocks[block_index].astype(jnp.float32)
        near_keys = lax.dynamic_slice_in_dim(key_blocks, block_index, 3, 0).reshape(3 * BLK, HEADS, head_size).astype(jnp.float32)
        near_values = lax.dynamic_slice_in_dim(value_blocks, block_index, 3, 0).reshape(3 * BLK, HEADS, head_size).astype(jnp.float32)
        near_scores = jnp.einsum('qhd,khd->hqk', query_f, near_keys) * score_scale
        far_scores = jnp.einsum('qhd,ghd->hqg', query_f, glob_keys) * score_scale
        key_block = block_index - 1 + jnp.arange(3 * BLK, dtype=jnp.int32) // BLK
        near_valid = (key_block >= 0) & (key_block < block_count)
        far_valid = jnp.abs(glob_block - block_index) > 1
        all_scores = jnp.concatenate([near_scores, far_scores], axis=-1)
        key_valid = jnp.concatenate([near_valid, far_valid], axis=0)
        all_scores = jnp.where(key_valid, all_scores, -jnp.inf)
        row_max = lax.optimization_barrier(jnp.max(all_scores, axis=-1, keepdims=True))
        exp_scores = jnp.exp(all_scores - row_max)
        row_total = lax.optimization_barrier(jnp.sum(exp_scores, axis=-1))
        rounded = lax.optimization_barrier(exp_scores.astype(jnp.bfloat16)).astype(jnp.float32)
        mixture = jnp.einsum('hqk,khd->qhd', rounded[..., :3 * BLK], near_values)
        mixture = mixture + jnp.einsum('hqg,ghd->qhd', rounded[..., 3 * BLK:], glob_values)
        return mixture / jnp.transpose(row_total)[:, :, None]
    window_out = lax.map(window_block, jnp.arange(block_count, dtype=jnp.int32)).reshape(TOKENS, D)
    all_keys = keys.astype(jnp.float32).reshape(TOKENS, HEADS, head_size)
    seg_values = values.astype(jnp.float32).reshape(N_SEQ, TOK_DEV, HEADS, head_size)
    glob_scores = jnp.einsum('ghd,khd->hgk', glob_queries, all_keys) * score_scale
    seg_scores = glob_scores.reshape(HEADS, G, N_SEQ, TOK_DEV)
    seg_max = lax.optimization_barrier(jnp.max(seg_scores, axis=-1, keepdims=True))
    seg_exp = jnp.exp(seg_scores - seg_max)
    seg_total = lax.optimization_barrier(jnp.sum(seg_exp, axis=-1))
    seg_rounded = lax.optimization_barrier(seg_exp.astype(jnp.bfloat16)).astype(jnp.float32)
    seg_acc = jnp.einsum('hgsk,skhd->hgsd', seg_rounded, seg_values)
    seg_peak = seg_max[..., 0]
    glob_max = lax.optimization_barrier(jnp.max(seg_peak, axis=-1, keepdims=True))
    rescale = jnp.exp(seg_peak - glob_max)
    glob_acc = lax.optimization_barrier(jnp.sum(seg_acc * rescale[..., None], axis=2))
    glob_total = lax.optimization_barrier(jnp.sum(seg_total * rescale, axis=2))
    glob_out = jnp.transpose(glob_acc / glob_total[..., None], (1, 0, 2))
    attended = window_out.at[global_positions].set(glob_out.reshape(G, D))
    return token_score(attended, score_weight)
```

```python
import functools
import math

import jax
import jax.numpy as jnp
from jax import lax
from jax.experimental import pallas as pl
from jax.experimental.pallas import tpu as pltpu
from jax.sharding import PartitionSpec as P

HEADS = 16
BLK = 64
CORES = 2
LANES = 128
NEG = -1e30
LOG2E = math.log2(math.e)
STAT_ROWS = 16


def pieces(x):
    hi = x.astype(jnp.bfloat16)
    rest = x - hi.astype(jnp.float32)
    mid = rest.astype(jnp.bfloat16)
    low = (rest - mid.astype(jnp.float32)).astype(jnp.bfloat16)
    return hi, mid, low


def dot_t(a, b):
    return lax.dot_general(a, b, (((1,), (1,)), ((), ())), preferred_element_type=jnp.float32)


def dot_n(a, b):
    return lax.dot_general(a, b, (((1,), (0,)), ((), ())), preferred_element_type=jnp.float32)


def put_message(out_ref, pair, out, peak, total):
    rows = out.shape[0]
    out_ref[pair, :rows, :] = out.astype(jnp.bfloat16)
    stats = [p.astype(jnp.float32) for p in (*pieces(peak), *pieces(total))]
    row = lax.broadcasted_iota(jnp.int32, (STAT_ROWS, LANES), 0)
    block = jnp.zeros((STAT_ROWS, LANES), jnp.float32)
    for i, stat in enumerate(stats):
        block = jnp.where(row == i, jnp.broadcast_to(stat, block.shape), block)
    out_ref[pair, rows:, :] = block.astype(jnp.bfloat16)


def get_message(ref, pair, head_size):
    out = ref[pair, :head_size, :].astype(jnp.float32)
    stats = ref[pair, head_size:, :].astype(jnp.float32)
    peak = stats[0:1] + stats[1:2] + stats[2:3]
    total = stats[3:4] + stats[4:5] + stats[5:6]
    return out, peak, total


def merged(a, b, scale2):
    out_a, peak_a, total_a = a
    out_b, peak_b, total_b = b
    peak = jnp.maximum(peak_a, peak_b)
    weight_a = jnp.exp2((peak_a - peak) * scale2) * total_a
    weight_b = jnp.exp2((peak_b - peak) * scale2) * total_b
    total = weight_a + weight_b
    inv = 1.0 / total
    return out_a * (weight_a * inv) + out_b * (weight_b * inv), peak, total


def global_kernel(scale2, info_ref, q_ref, k_own_ref, k_sib_ref, v_own_ref, v_sib_ref, out_ref):
    glob, width = q_ref.shape
    head_size = width // 2
    q = q_ref[...]
    doubled = jnp.concatenate([q, q], axis=0)
    row = lax.broadcasted_iota(jnp.int32, doubled.shape, 0)
    col = lax.broadcasted_iota(jnp.int32, doubled.shape, 1)
    diag = jnp.where((row < glob) == (col < head_size), doubled, jnp.zeros_like(doubled))
    s_own = dot_t(k_own_ref[...], diag)
    s_sib = dot_t(k_sib_ref[...], diag)
    peak = jnp.maximum(jnp.max(s_own, axis=0, keepdims=True), jnp.max(s_sib, axis=0, keepdims=True))
    e_own = jnp.exp2((s_own - peak) * scale2)
    e_sib = jnp.exp2((s_sib - peak) * scale2)
    total = jnp.sum(e_own, axis=0, keepdims=True) + jnp.sum(e_sib, axis=0, keepdims=True)
    contract = (((0,), (0,)), ((), ()))
    acc = lax.dot_general(
        v_own_ref[...], e_own.astype(jnp.bfloat16), contract, preferred_element_type=jnp.float32
    ) + lax.dot_general(
        v_sib_ref[...], e_sib.astype(jnp.bfloat16), contract, preferred_element_type=jnp.float32
    )
    lane = lax.broadcasted_iota(jnp.int32, (head_size, LANES), 1)
    out = jnp.where(lane < glob, acc[:head_size], acc[head_size:]) / total
    put_message(out_ref, 0, out, peak, total)


def merge_kernel(scale2, a_ref, b_ref, out_ref):
    head_size = a_ref.shape[1] - STAT_ROWS
    for pair in range(a_ref.shape[0]):
        a = get_message(a_ref, pair, head_size)
        b = get_message(b_ref, pair, head_size)
        put_message(out_ref, pair, *merged(a, b, scale2))


def final_kernel(scale2, info_ref, a_ref, b_ref, w_ref, pos_ref, win_ref, out_ref):
    pairs = a_ref.shape[0]
    head_size = a_ref.shape[1] - STAT_ROWS
    glob = pos_ref.shape[0]
    lane = lax.broadcasted_iota(jnp.int32, (head_size, LANES), 1)
    lin = jnp.zeros((1, LANES), jnp.float32)
    sq = jnp.zeros((1, LANES), jnp.float32)
    for pair in range(pairs):
        a = get_message(a_ref, pair, head_size)
        b = get_message(b_ref, pair, head_size)
        out, _, _ = merged(a, b, scale2)
        w = jnp.where(lane < glob, w_ref[:, 2 * pair : 2 * pair + 1], w_ref[:, 2 * pair + 1 : 2 * pair + 2])
        lin = lin + jnp.sum(out * w, axis=0, keepdims=True)
        sq = sq + jnp.sum(out * out, axis=0, keepdims=True)
    lin = lin + pltpu.roll(lin, glob, 1)
    sq = sq + pltpu.roll(sq, glob, 1)
    parts = [p.astype(jnp.float32) for p in (*pieces(lin), *pieces(sq))] + [jnp.ones((1, LANES), jnp.float32)]
    row = lax.broadcasted_iota(jnp.int32, (16, LANES), 0)
    table = jnp.zeros((16, LANES), jnp.float32)
    for i, part in enumerate(parts):
        table = jnp.where(row == i, jnp.broadcast_to(part, table.shape), table)
    table = table.astype(jnp.bfloat16)[:, :glob]
    pos = pos_ref[...]
    n_pairs = win_ref.shape[1]
    base = info_ref[1]
    for j in range(n_pairs):
        token = base + j * LANES + lax.broadcasted_iota(jnp.int32, (glob, LANES), 1)
        hit = jnp.where(pos == token, 1.0, 0.0).astype(jnp.bfloat16)
        placed = dot_n(table, hit)
        is_glob = placed[6:7] > 0.5
        out_ref[j // (n_pairs // CORES), 0:1, (j % (n_pairs // CORES)) * LANES : (j % (n_pairs // CORES) + 1) * LANES] = (
            jnp.where(is_glob, placed[0:1] + placed[1:2] + placed[2:3], win_ref[0, j : j + 1, :])
        )
        out_ref[j // (n_pairs // CORES), 1:2, (j % (n_pairs // CORES)) * LANES : (j % (n_pairs // CORES) + 1) * LANES] = (
            jnp.where(is_glob, placed[3:4] + placed[4:5] + placed[5:6], win_ref[1, j : j + 1, :])
        )


def window_kernel(
    scale2,
    info_ref,
    q_own_ref,
    q_sib_ref,
    k_own_ref,
    k_sib_ref,
    v_own_ref,
    v_sib_ref,
    k_low_ref,
    k_high_ref,
    v_low_ref,
    v_high_ref,
    kg_ref,
    vg_ref,
    w_ref,
    pos_ref,
    out_ref,
    q_all,
    k_all,
    v_all,
    bias,
):
    step = pl.program_id(0)
    rows, width = q_own_ref.shape
    glob = kg_ref.shape[0]
    head_size = LANES
    n_pairs = CORES * rows // LANES
    core = info_ref[0]
    base = info_ref[1]
    lane = lax.broadcasted_iota(jnp.int32, (BLK, LANES), 1)
    left = lane < BLK

    @pl.when(step == 0)
    def _():
        out_ref[...] = jnp.zeros_like(out_ref)
        glob_block = pos_ref[...] // BLK
        for j in range(n_pairs):
            block = (base + j * LANES) // BLK + lax.broadcasted_iota(jnp.int32, (glob, LANES), 1) // BLK
            bias[j] = jnp.where(jnp.abs(glob_block - block) > 1, 0.0, NEG)

    own = pl.multiple_of(core * rows, BLK)
    sib = pl.multiple_of((1 - core) * rows, BLK)
    q_all[pl.ds(own, rows), :] = q_own_ref[...]
    q_all[pl.ds(sib, rows), :] = q_sib_ref[...]
    k_all[pl.ds(pl.multiple_of(own + BLK, BLK), rows), :] = k_own_ref[...]
    k_all[pl.ds(pl.multiple_of(sib + BLK, BLK), rows), :] = k_sib_ref[...]
    k_all[:BLK, :] = k_low_ref[...]
    k_all[BLK + CORES * rows :, :] = k_high_ref[...]
    v_all[pl.ds(pl.multiple_of(own + BLK, BLK), rows), :] = v_own_ref[...]
    v_all[pl.ds(pl.multiple_of(sib + BLK, BLK), rows), :] = v_sib_ref[...]
    v_all[:BLK, :] = v_low_ref[...]
    v_all[BLK + CORES * rows :, :] = v_high_ref[...]
    first_bias = jnp.where(left & (info_ref[2] == 1), NEG, 0.0)
    last_bias = jnp.where((~left) & (info_ref[3] == 1), NEG, 0.0)
    for head in range(width // head_size):
        cols = slice(head * head_size, (head + 1) * head_size)
        v_t = jnp.transpose(v_all[:, cols])
        vg_t = jnp.transpose(vg_ref[:, cols])
        kg = kg_ref[:, cols]
        w = jnp.broadcast_to(w_ref[0, :, head : head + 1], (head_size, LANES))
        for j in range(n_pairs):
            q = q_all[j * LANES : (j + 1) * LANES, cols]
            near = dot_t(k_all[j * LANES : (j + 2) * LANES, cols], q)
            far = dot_t(kg, q) + bias[j]
            ends = jnp.where(left, near[:BLK], near[3 * BLK :])
            if j == 0:
                ends = ends + first_bias
            if j == n_pairs - 1:
                ends = ends + last_bias
            mid = near[BLK : 3 * BLK]
            peak = jnp.max(jnp.maximum(jnp.maximum(ends, far), jnp.maximum(mid[:BLK], mid[BLK:])), axis=0, keepdims=True)
            e_ends = jnp.exp2((ends - peak) * scale2)
            e_mid = jnp.exp2((mid - peak) * scale2)
            e_far = jnp.exp2((far - peak) * scale2)
            total = jnp.sum(e_ends + e_far + e_mid[:BLK] + e_mid[BLK:], axis=0, keepdims=True)
            zero = jnp.zeros_like(e_ends)
            weights = jnp.concatenate(
                [jnp.where(left, e_ends, zero), e_mid, jnp.where(left, zero, e_ends)], axis=0
            ).astype(jnp.bfloat16)
            acc = dot_n(v_t[:, j * LANES : (j + 2) * LANES], weights) + dot_n(vg_t, e_far.astype(jnp.bfloat16))
            inv = 1.0 / total
            out_ref[0, j : j + 1, :] += jnp.sum(acc * w, axis=0, keepdims=True) * inv
            out_ref[1, j : j + 1, :] += jnp.sum(acc * acc, axis=0, keepdims=True) * (inv * inv)


def on_device(queries, keys, values, global_positions, score_weight):
    rows, model_width = queries.shape
    head_size = model_width // HEADS
    half = model_width // CORES
    half_heads = HEADS // CORES
    glob = global_positions.shape[0]
    seq_index = lax.axis_index("seq")
    seq_count = lax.axis_size("seq")
    chips = seq_count // CORES
    core = seq_index % CORES
    chip = seq_index // CORES
    scale2 = head_size ** (-0.5) * LOG2E
    bf16 = jnp.bfloat16
    f32 = jnp.float32

    def swap(x, mask):
        return lax.ppermute(x, "seq", [(i, i ^ mask) for i in range(seq_count)])

    def columns(x, which):
        return lax.dynamic_slice_in_dim(x, which * half, half, axis=1)

    row_ids = seq_index * rows + jnp.arange(rows, dtype=jnp.int32)
    select = (global_positions[:, None] == row_ids[None, :]).astype(bf16)
    chosen = [jnp.dot(select, x, preferred_element_type=f32).astype(bf16) for x in (queries, keys, values)]
    sib_sel = swap(jnp.concatenate([columns(x, 1 - core) for x in chosen], axis=0), 1)
    own_sel = jnp.concatenate([columns(x, core) for x in chosen], axis=0)
    chip_sel = own_sel + sib_sel
    q_glob = chip_sel[:glob]
    kv_glob = chip_sel[glob:]

    q_sib = swap(columns(queries, 1 - core), 1)
    kv_sib = swap(jnp.concatenate([columns(keys, 1 - core), columns(values, 1 - core)], axis=0), 1)

    for r in range(1, int(math.log2(chips)) + 1):
        q_glob = q_glob + swap(q_glob, 1 << r)
    for r in range(1, int(math.log2(chips)) + 1):
        kv_glob = kv_glob + swap(kv_glob, 1 << r)

    k_mine = columns(keys, core)
    v_mine = columns(values, core)
    k_sib, v_sib = kv_sib[:rows], kv_sib[rows:]
    is_low = core == 0
    top = jnp.concatenate(
        [jnp.where(is_low, k_mine[:BLK], k_sib[:BLK]), jnp.where(is_low, v_mine[:BLK], v_sib[:BLK])], axis=0
    )
    bottom = jnp.concatenate(
        [jnp.where(is_low, k_sib[-BLK:], k_mine[-BLK:]), jnp.where(is_low, v_sib[-BLK:], v_mine[-BLK:])], axis=0
    )
    low = lax.ppermute(bottom, "seq", [(i, i + CORES) for i in range(seq_count - CORES)])
    high = lax.ppermute(top, "seq", [(i + CORES, i) for i in range(seq_count - CORES)])

    info = jnp.stack(
        [core, chip * (CORES * rows), (chip == 0).astype(jnp.int32), (chip == chips - 1).astype(jnp.int32)]
    ).astype(jnp.int32)
    pair_width = 2 * head_size
    n_steps = half // pair_width
    own_spec = pl.BlockSpec((rows, pair_width), lambda p, info: (0, info[0] * n_steps + p))

    def part_spec(count, block=0):
        return pl.BlockSpec((count, pair_width), lambda p, info: (block, p))

    message = pl.pallas_call(
        functools.partial(global_kernel, scale2),
        grid_spec=pltpu.PrefetchScalarGridSpec(
            num_scalar_prefetch=1,
            grid=(n_steps,),
            in_specs=[part_spec(glob), own_spec, part_spec(rows), own_spec, part_spec(rows, 1)],
            out_specs=pl.BlockSpec((1, head_size + STAT_ROWS, LANES), lambda p, info: (p, 0, 0)),
        ),
        out_shape=jax.ShapeDtypeStruct((n_steps, head_size + STAT_ROWS, LANES), bf16),
        compiler_params=pltpu.CompilerParams(vmem_limit_bytes=16 * 1024 * 1024),
        name="global_partial",
    )(info, q_glob, keys, kv_sib, values, kv_sib)

    rounds = int(math.log2(chips))
    for r in range(1, rounds):
        message = pl.pallas_call(
            functools.partial(merge_kernel, scale2),
            out_shape=jax.ShapeDtypeStruct(message.shape, bf16),
            name="merge_partial",
        )(message, swap(message, 1 << r))
    message_far = swap(message, 1 << rounds)

    weight_cols = lax.dynamic_slice_in_dim(score_weight.reshape(HEADS, head_size), core * half_heads, half_heads, 0)
    weight_cols = weight_cols.reshape(n_steps, 2, head_size)
    positions = global_positions.reshape(glob, 1)
    n_pairs = CORES * rows // LANES
    whole = pl.BlockSpec((glob, 1), lambda p, info: (0, 0))
    window = pl.pallas_call(
        functools.partial(window_kernel, scale2),
        grid_spec=pltpu.PrefetchScalarGridSpec(
            num_scalar_prefetch=1,
            grid=(n_steps,),
            in_specs=[
                own_spec,
                part_spec(rows),
                own_spec,
                part_spec(rows),
                own_spec,
                part_spec(rows, 1),
                part_spec(BLK),
                part_spec(BLK),
                part_spec(BLK, 1),
                part_spec(BLK, 1),
                part_spec(glob),
                part_spec(glob, 1),
                pl.BlockSpec((1, head_size, 2), lambda p, info: (p, 0, 0)),
                whole,
            ],
            out_specs=pl.BlockSpec((2, n_pairs, LANES), lambda p, info: (0, 0, 0)),
            scratch_shapes=[
                pltpu.VMEM((CORES * rows, pair_width), bf16),
                pltpu.VMEM((CORES * rows + 2 * BLK, pair_width), bf16),
                pltpu.VMEM((CORES * rows + 2 * BLK, pair_width), bf16),
                pltpu.VMEM((n_pairs, glob, LANES), f32),
            ],
        ),
        out_shape=jax.ShapeDtypeStruct((2, n_pairs, LANES), f32),
        compiler_params=pltpu.CompilerParams(vmem_limit_bytes=24 * 1024 * 1024),
        name="window_attention",
    )(
        info,
        queries,
        q_sib,
        keys,
        kv_sib,
        values,
        kv_sib,
        low,
        high,
        low,
        high,
        kv_glob,
        kv_glob,
        jnp.transpose(weight_cols, (0, 2, 1)),
        positions,
    )

    vmem = pl.BlockSpec(memory_space=pltpu.VMEM)
    sums = pl.pallas_call(
        functools.partial(final_kernel, scale2),
        in_specs=[pl.BlockSpec(memory_space=pltpu.SMEM), vmem, vmem, vmem, vmem, vmem],
        out_specs=vmem,
        out_shape=jax.ShapeDtypeStruct((CORES, 2, rows), f32),
        name="place_global",
    )(info, message, message_far, jnp.transpose(weight_cols.reshape(half_heads, head_size)), positions, window)
    mine = lax.dynamic_index_in_dim(sums, core, 0, keepdims=False)
    theirs = swap(lax.dynamic_index_in_dim(sums, 1 - core, 0, keepdims=False), 1)
    both = mine + theirs
    return both[0] * lax.rsqrt(both[1] * (1.0 / model_width) + 1e-06)


def solution(mesh):
    placed = (
        P(("doc", "seq"), None),
        P(("doc", "seq"), None),
        P(("doc", "seq"), None),
        P("doc"),
        P(),
    )
    return jax.shard_map(
        on_device, mesh=mesh, in_specs=placed, out_specs=P(("doc", "seq")), check_vma=False
    )
```

```python
import functools
import math

import jax
import jax.numpy as jnp
from jax import lax
from jax.experimental import pallas as pl
from jax.experimental.pallas import tpu as pltpu
from jax.sharding import PartitionSpec as P

HEADS = 16
BLK = 64
CORES = 2
LANES = 128
NEG = -1e30
LOG2E = math.log2(math.e)
STAT_ROWS = 16


def pieces(x):
    hi = x.astype(jnp.bfloat16)
    rest = x - hi.astype(jnp.float32)
    mid = rest.astype(jnp.bfloat16)
    low = (rest - mid.astype(jnp.float32)).astype(jnp.bfloat16)
    return hi, mid, low


def dot_t(a, b):
    return lax.dot_general(a, b, (((1,), (1,)), ((), ())), preferred_element_type=jnp.float32)


def dot_n(a, b):
    return lax.dot_general(a, b, (((1,), (0,)), ((), ())), preferred_element_type=jnp.float32)


def put_message(out_ref, pair, out, peak, total):
    rows = out.shape[0]
    out_ref[pair, :rows, :] = out.astype(jnp.bfloat16)
    stats = [p.astype(jnp.float32) for p in (*pieces(peak), *pieces(total))]
    row = lax.broadcasted_iota(jnp.int32, (STAT_ROWS, LANES), 0)
    block = jnp.zeros((STAT_ROWS, LANES), jnp.float32)
    for i, stat in enumerate(stats):
        block = jnp.where(row == i, jnp.broadcast_to(stat, block.shape), block)
    out_ref[pair, rows:, :] = block.astype(jnp.bfloat16)


def get_message(ref, pair, head_size):
    out = ref[pair, :head_size, :].astype(jnp.float32)
    stats = ref[pair, head_size:, :].astype(jnp.float32)
    peak = stats[0:1] + stats[1:2] + stats[2:3]
    total = stats[3:4] + stats[4:5] + stats[5:6]
    return out, peak, total


def merged(a, b, scale2):
    out_a, peak_a, total_a = a
    out_b, peak_b, total_b = b
    peak = jnp.maximum(peak_a, peak_b)
    weight_a = jnp.exp2((peak_a - peak) * scale2) * total_a
    weight_b = jnp.exp2((peak_b - peak) * scale2) * total_b
    total = weight_a + weight_b
    inv = 1.0 / total
    return out_a * (weight_a * inv) + out_b * (weight_b * inv), peak, total


def device_place():
    index = lax.axis_index("seq")
    return index % CORES, index // CORES


def select_kernel(base_of, half, pos_ref, *refs):
    count = (len(refs) - 2) if len(refs) < 4 else (len(refs) - 2)
    x_refs, own_ref, sib_ref = refs[:count], refs[count], refs[count + 1]
    rows = x_refs[0].shape[0]
    glob = pos_ref.shape[1]
    core, chip = device_place()
    base = (chip * CORES + core) * rows
    row = base + lax.broadcasted_iota(jnp.int32, (rows, glob), 0)
    hit = jnp.where(row == pos_ref[...], 1.0, 0.0).astype(jnp.bfloat16)
    contract = (((0,), (0,)), ((), ()))
    for i, x_ref in enumerate(x_refs):
        for out_ref, which in ((own_ref, core), (sib_ref, 1 - core)):
            x = x_ref[:, pl.ds(pl.multiple_of(which * half, half), half)]
            picked = lax.dot_general(hit, x, contract, preferred_element_type=jnp.float32)
            out_ref[i * glob : (i + 1) * glob, :] = picked.astype(jnp.bfloat16)
            if len(x_refs) > 1:
                edge = pl.multiple_of(core * (rows - BLK), BLK)
                out_ref[(2 + i) * glob : (2 + i) * glob + BLK, :] = x_ref[
                    pl.ds(edge, BLK), pl.ds(pl.multiple_of(which * half, half), half)
                ]


def prepare_kernel(q_own_ref, q_sib_ref, k_own_ref, k_sib_ref, v_own_ref, v_sib_ref, q_t_ref, k_ref, v_t_ref, v_all):
    rows = q_own_ref.shape[0]
    half = k_ref.shape[1]
    core, _ = device_place()
    cols = pl.ds(pl.multiple_of(core * half, half), half)
    zero = jnp.zeros((BLK, half), jnp.bfloat16)
    for ref in (k_ref, v_all):
        ref[:BLK, :] = zero
        ref[BLK + CORES * rows :, :] = zero
    for which, k_from, v_from in ((core, k_own_ref, v_own_ref), (1 - core, k_sib_ref, v_sib_ref)):
        at = pl.ds(pl.multiple_of(which * rows + BLK, BLK), rows)
        k_ref[at, :] = k_from[:, cols]
        v_all[at, :] = v_from[:, cols]

    def turn(head, carry):
        lanes = pl.ds(pl.multiple_of(head * LANES, LANES), LANES)
        source = pl.ds(pl.multiple_of(core * half + head * LANES, LANES), LANES)
        v_t_ref[lanes, :] = jnp.transpose(v_all[:, lanes])
        q_t_ref[lanes, pl.ds(pl.multiple_of(core * rows, LANES), rows)] = jnp.transpose(q_own_ref[:, source])
        q_t_ref[lanes, pl.ds(pl.multiple_of((1 - core) * rows, LANES), rows)] = jnp.transpose(q_sib_ref[:, source])
        return carry

    lax.fori_loop(0, half // LANES, turn, 0)


def global_kernel(scale2, q_a_ref, q_b_ref, k_ref, v_t_ref, out_ref, s_buf, e_buf):
    glob, half = q_a_ref.shape
    head_size = LANES
    pairs = half // (2 * head_size)
    tokens = k_ref.shape[0] - 2 * BLK
    row = lax.broadcasted_iota(jnp.int32, (2 * glob, 2 * head_size), 0)
    col = lax.broadcasted_iota(jnp.int32, (2 * glob, 2 * head_size), 1)
    keep = (row < glob) == (col < head_size)
    lane = lax.broadcasted_iota(jnp.int32, (head_size, LANES), 1)
    for pair in range(pairs):
        cols = slice(2 * pair * head_size, 2 * (pair + 1) * head_size)
        q = q_a_ref[:, cols] + q_b_ref[:, cols]
        doubled = jnp.concatenate([q, q], axis=0)
        diag = jnp.where(keep, doubled, jnp.zeros_like(doubled))
        s_buf[pair] = dot_t(k_ref[BLK : BLK + tokens, cols], diag)
    stats = []
    for pair in range(pairs):
        s = s_buf[pair]
        peak = jnp.max(s, axis=0, keepdims=True)
        e = jnp.exp2((s - peak) * scale2)
        stats.append((peak, jnp.sum(e, axis=0, keepdims=True)))
        zero = jnp.zeros((BLK, LANES), jnp.bfloat16)
        e_buf[pair, :BLK] = zero
        e_buf[pair, BLK + tokens :] = zero
        e_buf[pair, BLK : BLK + tokens] = e.astype(jnp.bfloat16)
    for pair in range(pairs):
        rows = slice(2 * pair * head_size, 2 * (pair + 1) * head_size)
        acc = dot_n(v_t_ref[rows, :], e_buf[pair])
        peak, total = stats[pair]
        out = jnp.where(lane < glob, acc[:head_size], acc[head_size:]) / total
        put_message(out_ref, pair, out, peak, total)


def merge_kernel(scale2, a_ref, b_ref, out_ref):
    head_size = a_ref.shape[1] - STAT_ROWS
    for pair in range(a_ref.shape[0]):
        a = get_message(a_ref, pair, head_size)
        b = get_message(b_ref, pair, head_size)
        put_message(out_ref, pair, *merged(a, b, scale2))


def final_kernel(scale2, a_ref, b_ref, w_ref, pos_ref, win_ref, own_ref, sib_ref):
    pairs = a_ref.shape[0]
    head_size = a_ref.shape[1] - STAT_ROWS
    glob = pos_ref.shape[0]
    core, chip = device_place()
    lane = lax.broadcasted_iota(jnp.int32, (head_size, LANES), 1)
    lin = jnp.zeros((1, LANES), jnp.float32)
    sq = jnp.zeros((1, LANES), jnp.float32)
    for pair in range(pairs):
        a = get_message(a_ref, pair, head_size)
        b = get_message(b_ref, pair, head_size)
        out, _, _ = merged(a, b, scale2)
        w = jnp.where(lane < glob, w_ref[:, 2 * pair : 2 * pair + 1], w_ref[:, 2 * pair + 1 : 2 * pair + 2])
        lin = lin + jnp.sum(out * w, axis=0, keepdims=True)
        sq = sq + jnp.sum(out * out, axis=0, keepdims=True)
    lin = lin + pltpu.roll(lin, glob, 1)
    sq = sq + pltpu.roll(sq, glob, 1)
    parts = [p.astype(jnp.float32) for p in (*pieces(lin), *pieces(sq))] + [jnp.ones((1, LANES), jnp.float32)]
    row = lax.broadcasted_iota(jnp.int32, (16, LANES), 0)
    table = jnp.zeros((16, LANES), jnp.float32)
    for i, part in enumerate(parts):
        table = jnp.where(row == i, jnp.broadcast_to(part, table.shape), table)
    table = table.astype(jnp.bfloat16)[:, :glob]
    pos = pos_ref[...]
    n_pairs = win_ref.shape[1]
    each = n_pairs // CORES
    for out_ref, which in ((own_ref, core), (sib_ref, 1 - core)):
        for j in range(each):
            pair = which * each + j
            token = (chip * n_pairs + pair) * LANES + lax.broadcasted_iota(jnp.int32, (glob, LANES), 1)
            hit = jnp.where(pos == token, 1.0, 0.0).astype(jnp.bfloat16)
            placed = dot_n(table, hit)
            is_glob = placed[6:7] > 0.5
            for i in (0, 1):
                value = placed[3 * i : 3 * i + 1] + placed[3 * i + 1 : 3 * i + 2] + placed[3 * i + 2 : 3 * i + 3]
                out_ref[i, j : j + 1, :] = jnp.where(is_glob, value, win_ref[i, pl.ds(pair, 1), :])


def window_kernel(
    scale2,
    q_t_ref,
    k_ref,
    v_t_ref,
    edge_a_ref,
    edge_b_ref,
    kv_a_ref,
    kv_b_ref,
    w_ref,
    pos_ref,
    out_ref,
    s_buf,
    e_buf,
    bias,
    edges,
    v_glob_t,
):
    half, tokens = q_t_ref.shape
    glob = pos_ref.shape[0]
    n_pairs = tokens // LANES
    core, chip = device_place()
    chips = lax.axis_size("seq") // CORES
    lane = lax.broadcasted_iota(jnp.int32, (BLK, LANES), 1)
    left = lane < BLK
    wide_left = lax.broadcasted_iota(jnp.int32, (LANES, LANES), 1) < BLK
    glob_block = pos_ref[...] // BLK
    for j in range(n_pairs):
        block = (chip * n_pairs + j) * (LANES // BLK) + lax.broadcasted_iota(jnp.int32, (glob, LANES), 1) // BLK
        bias[j] = jnp.where(jnp.abs(glob_block - block) > 1, 0.0, NEG)
    first_bias = jnp.where(left & (chip == 0), NEG, 0.0)
    last_bias = jnp.where((~left) & (chip == chips - 1), NEG, 0.0)

    @pl.when(core == 1)
    def _():
        edges[0] = edge_a_ref[...]
        edges[1] = edge_b_ref[...]

    @pl.when(core == 0)
    def _():
        edges[0] = edge_b_ref[...]
        edges[1] = edge_a_ref[...]

    def one_head(head, carry):
        cols = pl.ds(pl.multiple_of(head * LANES, LANES), LANES)
        kg = kv_a_ref[:glob, cols] + kv_b_ref[:glob, cols]
        for j in range(n_pairs):
            q = q_t_ref[cols, j * LANES : (j + 1) * LANES]
            if j == 0:
                k = jnp.concatenate([edges[0, :BLK, cols], k_ref[BLK : 4 * BLK, cols]], axis=0)
            elif j == n_pairs - 1:
                k = jnp.concatenate([k_ref[j * LANES : j * LANES + 3 * BLK, cols], edges[1, :BLK, cols]], axis=0)
            else:
                k = k_ref[j * LANES : (j + 2) * LANES, cols]
            s_buf[j, : 4 * BLK] = dot_n(k, q)
            s_buf[j, 4 * BLK :] = dot_n(kg, q)
        inverses = []
        for j in range(n_pairs):
            far = s_buf[j, 4 * BLK :] + bias[j]
            ends = jnp.where(left, s_buf[j, :BLK], s_buf[j, 3 * BLK : 4 * BLK])
            if j == 0:
                ends = ends + first_bias
            if j == n_pairs - 1:
                ends = ends + last_bias
            mid = s_buf[j, BLK : 3 * BLK]
            peak = jnp.maximum(jnp.maximum(ends, far), jnp.maximum(mid[:BLK], mid[BLK:]))
            peak = jnp.max(peak, axis=0, keepdims=True)
            e_ends = jnp.exp2((ends - peak) * scale2)
            e_mid = jnp.exp2((mid - peak) * scale2)
            e_far = jnp.exp2((far - peak) * scale2)
            total = jnp.sum(e_ends + e_far + e_mid[:BLK] + e_mid[BLK:], axis=0, keepdims=True)
            zero = jnp.zeros_like(e_ends)
            e_buf[j, :BLK] = jnp.where(left, e_ends, zero).astype(jnp.bfloat16)
            e_buf[j, BLK : 3 * BLK] = e_mid.astype(jnp.bfloat16)
            e_buf[j, 3 * BLK : 4 * BLK] = jnp.where(left, zero, e_ends).astype(jnp.bfloat16)
            e_buf[j, 4 * BLK :] = e_far.astype(jnp.bfloat16)
            inverses.append(1.0 / total)
        vg = kv_a_ref[glob:, cols] + kv_b_ref[glob:, cols]
        vg_t = jnp.transpose(vg)
        turned = jnp.transpose(jnp.concatenate([edges[0, BLK:, cols], edges[1, BLK:, cols]], axis=0))
        w = jnp.broadcast_to(w_ref[head], (LANES, LANES))
        lins, sqs = [], []
        for j in range(n_pairs):
            v_0 = v_t_ref[cols, j * LANES : (j + 1) * LANES]
            v_1 = v_t_ref[cols, (j + 1) * LANES : (j + 2) * LANES]
            if j == 0:
                v_0 = jnp.where(wide_left, turned, v_0)
            if j == n_pairs - 1:
                v_1 = jnp.where(wide_left, v_1, turned)
            acc = dot_n(jnp.concatenate([v_0, v_1], axis=1), e_buf[j, : 4 * BLK]) + dot_n(vg_t, e_buf[j, 4 * BLK :])
            lins.append(jnp.sum(acc * w, axis=0, keepdims=True) * inverses[j])
            sqs.append(jnp.sum(acc * acc, axis=0, keepdims=True) * (inverses[j] * inverses[j]))
        lin, sq = carry
        return lin + jnp.concatenate(lins, axis=0), sq + jnp.concatenate(sqs, axis=0)

    none = jnp.zeros((n_pairs, LANES), jnp.float32)
    lin, sq = lax.fori_loop(0, half // LANES, one_head, (none, none))
    out_ref[0] = lin
    out_ref[1] = sq


def call(kernel, name, outs, args, scratch=()):
    spec = pl.BlockSpec(memory_space=pltpu.VMEM)
    single = not isinstance(outs, list)
    shapes = [outs] if single else outs
    result = pl.pallas_call(
        kernel,
        in_specs=[spec] * len(args),
        out_specs=[spec] * len(shapes),
        out_shape=[pltpu.VMEM(shape, dtype) for shape, dtype in shapes],
        scratch_shapes=[pltpu.VMEM(shape, dtype) for shape, dtype in scratch],
        compiler_params=pltpu.CompilerParams(vmem_limit_bytes=16 * 1024 * 1024),
        name=name,
    )(*[pltpu.with_memory_space_constraint(x, pltpu.VMEM) for x in args])
    return result[0] if single else result


def on_device(queries, keys, values, global_positions, score_weight):
    rows, model_width = queries.shape
    head_size = model_width // HEADS
    half = model_width // CORES
    half_heads = HEADS // CORES
    glob = global_positions.shape[0]
    seq_count = lax.axis_size("seq")
    chips = seq_count // CORES
    core = lax.axis_index("seq") % CORES
    scale2 = head_size ** (-0.5) * LOG2E
    bf16 = jnp.bfloat16
    f32 = jnp.float32
    rounds = int(math.log2(chips))
    tokens = CORES * rows
    n_pairs = tokens // LANES

    def swap(x, mask):
        return lax.ppermute(x, "seq", [(i, i ^ mask) for i in range(seq_count)])

    def shift(x, even, odd):
        moves = [(i, i + (odd if i % CORES else even) * CORES) for i in range(seq_count)]
        return lax.ppermute(x, "seq", [(i, to) for i, to in moves if 0 <= to < seq_count])

    row_positions = global_positions.reshape(1, glob)
    positions = global_positions.reshape(glob, 1)
    small = ((glob, half), bf16)
    big = ((2 * glob + 2 * BLK, half), bf16)
    q_own, q_sib = call(
        functools.partial(select_kernel, None, half), "select_queries", [small, small], [row_positions, queries]
    )
    kv_own, kv_sib = call(
        functools.partial(select_kernel, None, half), "select_keys_values", [big, big], [row_positions, keys, values]
    )
    q_near = q_own + swap(q_sib, 1)
    kv_recv = swap(kv_sib, 1)
    for r in range(1, rounds):
        q_near = q_near + swap(q_near, 1 << r)
    q_far = swap(q_near, 1 << rounds)

    k_other, v_other, q_other = swap(keys, 1), swap(values, 1), swap(queries, 1)
    kv_near = kv_own[: 2 * glob] + kv_recv[: 2 * glob]
    edge_a = shift(kv_own[2 * glob :], -1, 1)
    edge_b = shift(kv_recv[2 * glob :], 1, -1)
    for r in range(1, rounds):
        kv_near = kv_near + swap(kv_near, 1 << r)
    kv_far = swap(kv_near, 1 << rounds)

    q_t, k_all, v_t = call(
        prepare_kernel,
        "prepare",
        [((half, tokens), bf16), ((tokens + 2 * BLK, half), bf16), ((half, tokens + 2 * BLK), bf16)],
        [queries, q_other, keys, k_other, values, v_other],
        [((tokens + 2 * BLK, half), bf16)],
    )
    part = ((half_heads // 2, head_size + STAT_ROWS, LANES), bf16)
    message = call(
        functools.partial(global_kernel, scale2),
        "global_partial",
        part,
        [q_near, q_far, k_all, v_t],
        [((half_heads // 2, tokens, LANES), f32), ((half_heads // 2, tokens + 2 * BLK, LANES), bf16)],
    )
    for r in range(1, rounds):
        message = call(
            functools.partial(merge_kernel, scale2), "merge_partial", part, [message, swap(message, 1 << r)]
        )
    message_far = swap(message, 1 << rounds)

    weight_rows = lax.dynamic_slice_in_dim(score_weight.reshape(HEADS, head_size), core * half_heads, half_heads, 0)
    window = call(
        functools.partial(window_kernel, scale2),
        "window_attention",
        ((2, n_pairs, LANES), f32),
        [q_t, k_all, v_t, edge_a, edge_b, kv_near, kv_far, weight_rows.reshape(half_heads, head_size, 1), positions],
        [
            ((n_pairs, 4 * BLK + glob, LANES), f32),
            ((n_pairs, 4 * BLK + glob, LANES), bf16),
            ((n_pairs, glob, LANES), f32),
            ((2, 2 * BLK, half), bf16),
            ((LANES, glob), bf16),
        ],
    )
    share = ((2, n_pairs // CORES, LANES), f32)
    mine, theirs = call(
        functools.partial(final_kernel, scale2),
        "place_global",
        [share, share],
        [message, message_far, jnp.transpose(weight_rows), positions, window],
    )
    theirs = swap(theirs, 1)
    lin = mine[0] + theirs[0]
    sq = mine[1] + theirs[1]
    return (lin * lax.rsqrt(sq * (1.0 / model_width) + 1e-06)).reshape(rows)


def solution(mesh):
    placed = (
        P(("doc", "seq"), None),
        P(("doc", "seq"), None),
        P(("doc", "seq"), None),
        P("doc"),
        P(),
    )
    return jax.shard_map(
        on_device, mesh=mesh, in_specs=placed, out_specs=P(("doc", "seq")), check_vma=False
    )
```

```python
import functools
import math

import jax
import jax.numpy as jnp
from jax import lax
from jax.experimental import pallas as pl
from jax.experimental.pallas import tpu as pltpu
from jax.sharding import PartitionSpec as P

HEADS = 16
BLK = 64
CORES = 2
LANES = 128
NEG = -1e30
LOG2E = math.log2(math.e)
STAT_ROWS = 16


def pieces(x):
    hi = x.astype(jnp.bfloat16)
    rest = x - hi.astype(jnp.float32)
    mid = rest.astype(jnp.bfloat16)
    low = (rest - mid.astype(jnp.float32)).astype(jnp.bfloat16)
    return hi, mid, low


def dot_t(a, b):
    return lax.dot_general(a, b, (((1,), (1,)), ((), ())), preferred_element_type=jnp.float32)


def dot_n(a, b):
    return lax.dot_general(a, b, (((1,), (0,)), ((), ())), preferred_element_type=jnp.float32)


def put_message(out_ref, pair, out, peak, total):
    rows = out.shape[0]
    out_ref[pair, :rows, :] = out.astype(jnp.bfloat16)
    stats = [p.astype(jnp.float32) for p in (*pieces(peak), *pieces(total))]
    row = lax.broadcasted_iota(jnp.int32, (STAT_ROWS, LANES), 0)
    block = jnp.zeros((STAT_ROWS, LANES), jnp.float32)
    for i, stat in enumerate(stats):
        block = jnp.where(row == i, jnp.broadcast_to(stat, block.shape), block)
    out_ref[pair, rows:, :] = block.astype(jnp.bfloat16)


def get_message(ref, pair, head_size):
    out = ref[pair, :head_size, :].astype(jnp.float32)
    stats = ref[pair, head_size:, :].astype(jnp.float32)
    peak = stats[0:1] + stats[1:2] + stats[2:3]
    total = stats[3:4] + stats[4:5] + stats[5:6]
    return out, peak, total


def merged(a, b, scale2):
    out_a, peak_a, total_a = a
    out_b, peak_b, total_b = b
    peak = jnp.maximum(peak_a, peak_b)
    weight_a = jnp.exp2((peak_a - peak) * scale2) * total_a
    weight_b = jnp.exp2((peak_b - peak) * scale2) * total_b
    total = weight_a + weight_b
    inv = 1.0 / total
    return out_a * (weight_a * inv) + out_b * (weight_b * inv), peak, total


def device_place():
    index = lax.axis_index("seq")
    return index % CORES, index // CORES


def column_of(row):
    wide = jnp.concatenate([row, row], axis=1).astype(jnp.float32)
    return jnp.transpose(jnp.broadcast_to(wide, (LANES, LANES)))[: row.shape[1]]


def pick(x_ref, hit, out_ref, at, cols):
    contract = (((0,), (0,)), ((), ()))
    picked = lax.dot_general(hit, x_ref[:, cols], contract, preferred_element_type=jnp.float32)
    out_ref[at : at + hit.shape[1], :] = picked.astype(jnp.bfloat16)


def own_positions(pos_ref, rows):
    core, chip = device_place()
    row = (chip * CORES + core) * rows + lax.broadcasted_iota(jnp.int32, (rows, pos_ref.shape[1]), 0)
    return jnp.where(row == pos_ref[...], 1.0, 0.0).astype(jnp.bfloat16)


def select_q_kernel(half, pos_ref, q_ref, own_ref, sib_ref):
    hit = own_positions(pos_ref, q_ref.shape[0])
    core, _ = device_place()
    for out_ref, which in ((sib_ref, 1 - core), (own_ref, core)):
        pick(q_ref, hit, out_ref, 0, pl.ds(pl.multiple_of(which * half, half), half))


def select_kv_kernel(half, pos_ref, k_ref, v_ref, q_ref, own_ref, edge_ref, sib_ref):
    rows = k_ref.shape[0]
    glob = pos_ref.shape[1]
    hit = own_positions(pos_ref, rows)
    core, _ = device_place()
    block = pl.ds(pl.multiple_of(core * (rows - BLK), BLK), BLK)
    mine = pl.ds(pl.multiple_of(core * half, half), half)
    theirs = pl.ds(pl.multiple_of((1 - core) * half, half), half)
    start = 2 * glob + 2 * BLK
    for i, x_ref in enumerate((k_ref, v_ref)):
        pick(x_ref, hit, sib_ref, i * glob, theirs)
        sib_ref[2 * glob + i * BLK : 2 * glob + (i + 1) * BLK, :] = x_ref[block, theirs]
        sib_ref[start + i * rows : start + (i + 1) * rows, :] = x_ref[:, theirs]
        pick(x_ref, hit, own_ref, i * glob, mine)
        edge_ref[i * BLK : (i + 1) * BLK, :] = x_ref[block, mine]
    sib_ref[start + 2 * rows :, :] = q_ref[:, theirs]


def split_kernel(a_ref, b_ref, sum_ref, rest_ref):
    count = sum_ref.shape[0]
    sum_ref[...] = a_ref[...] + b_ref[:count, :]
    rest_ref[...] = b_ref[count : count + rest_ref.shape[0], :]


def add_kernel(a_ref, b_ref, out_ref):
    count = out_ref.shape[0]
    out_ref[...] = a_ref[:count, :] + b_ref[:count, :]


def prepare_kernel(q_own_ref, k_own_ref, v_own_ref, sib_ref, k_ref, v_t_ref, q_t_ref, v_all):
    rows = k_own_ref.shape[0]
    half = k_ref.shape[1]
    core, _ = device_place()
    cols = pl.ds(pl.multiple_of(core * half, half), half)
    own = pl.multiple_of(core * rows, BLK)
    sib = pl.multiple_of((1 - core) * rows, BLK)
    start = sib_ref.shape[0] - 3 * rows
    zero = jnp.zeros((BLK, half), jnp.bfloat16)
    for i, (ref, own_ref) in enumerate(((k_ref, k_own_ref), (v_all, v_own_ref))):
        ref[:BLK, :] = zero
        ref[BLK + CORES * rows :, :] = zero
        ref[pl.ds(pl.multiple_of(own + BLK, BLK), rows), :] = own_ref[:, cols]
        ref[pl.ds(pl.multiple_of(sib + BLK, BLK), rows), :] = sib_ref[start + i * rows : start + (i + 1) * rows, :]

    def turn(head, carry):
        lanes = pl.ds(pl.multiple_of(head * LANES, LANES), LANES)
        v_t_ref[lanes, :] = jnp.transpose(v_all[:, lanes])
        source = pl.ds(pl.multiple_of(core * half + head * LANES, LANES), LANES)
        q_t_ref[lanes, pl.ds(pl.multiple_of(own, LANES), rows)] = jnp.transpose(q_own_ref[:, source])
        q_t_ref[lanes, pl.ds(pl.multiple_of(sib, LANES), rows)] = jnp.transpose(sib_ref[start + 2 * rows :, lanes])
        return carry

    lax.fori_loop(0, half // LANES, turn, 0)


def global_kernel(scale2, q_a_ref, q_b_ref, k_ref, v_t_ref, out_ref, s_buf, e_buf):
    glob, half = q_a_ref.shape
    head_size = LANES
    pairs = half // (2 * head_size)
    tokens = k_ref.shape[0] - 2 * BLK
    row = lax.broadcasted_iota(jnp.int32, (2 * glob, 2 * head_size), 0)
    col = lax.broadcasted_iota(jnp.int32, (2 * glob, 2 * head_size), 1)
    keep = (row < glob) == (col < head_size)
    lane = lax.broadcasted_iota(jnp.int32, (head_size, LANES), 1)
    for pair in range(pairs):
        cols = slice(2 * pair * head_size, 2 * (pair + 1) * head_size)
        q = q_a_ref[:, cols] + q_b_ref[:, cols]
        doubled = jnp.concatenate([q, q], axis=0)
        diag = jnp.where(keep, doubled, jnp.zeros_like(doubled))
        s_buf[pair] = dot_t(k_ref[BLK : BLK + tokens, cols], diag)
    stats = []
    for pair in range(pairs):
        s = s_buf[pair]
        peak = jnp.max(s, axis=0, keepdims=True)
        e = jnp.exp2((s - peak) * scale2)
        stats.append((peak, jnp.sum(e, axis=0, keepdims=True)))
        zero = jnp.zeros((BLK, LANES), jnp.bfloat16)
        e_buf[pair, :BLK] = zero
        e_buf[pair, BLK + tokens :] = zero
        e_buf[pair, BLK : BLK + tokens] = e.astype(jnp.bfloat16)
    for pair in range(pairs):
        rows = slice(2 * pair * head_size, 2 * (pair + 1) * head_size)
        acc = dot_n(v_t_ref[rows, :], e_buf[pair])
        peak, total = stats[pair]
        out = jnp.where(lane < glob, acc[:head_size], acc[head_size:]) / total
        put_message(out_ref, pair, out, peak, total)


def merge_kernel(scale2, a_ref, b_ref, out_ref):
    head_size = a_ref.shape[1] - STAT_ROWS
    for pair in range(a_ref.shape[0]):
        a = get_message(a_ref, pair, head_size)
        b = get_message(b_ref, pair, head_size)
        put_message(out_ref, pair, *merged(a, b, scale2))


def final_kernel(scale2, a_ref, b_ref, w_ref, pos_ref, win_ref, own_ref, sib_ref):
    pairs = a_ref.shape[0]
    head_size = a_ref.shape[1] - STAT_ROWS
    glob = pos_ref.shape[1]
    core, chip = device_place()
    upper = lax.broadcasted_iota(jnp.int32, (LANES, head_size), 0) < glob
    lin = jnp.zeros((1, LANES), jnp.float32)
    sq = jnp.zeros((1, LANES), jnp.float32)
    for pair in range(pairs):
        a = get_message(a_ref, pair, head_size)
        b = get_message(b_ref, pair, head_size)
        out, _, _ = merged(a, b, scale2)
        w_a = w_ref[pl.ds(core * 2 * pairs + 2 * pair, 1), :]
        w_b = w_ref[pl.ds(core * 2 * pairs + 2 * pair + 1, 1), :]
        w = jnp.transpose(jnp.where(upper, w_a, w_b))
        lin = lin + jnp.sum(out * w, axis=0, keepdims=True)
        sq = sq + jnp.sum(out * out, axis=0, keepdims=True)
    lin = lin + pltpu.roll(lin, glob, 1)
    sq = sq + pltpu.roll(sq, glob, 1)
    parts = [p.astype(jnp.float32) for p in (*pieces(lin), *pieces(sq))] + [jnp.ones((1, LANES), jnp.float32)]
    row = lax.broadcasted_iota(jnp.int32, (16, LANES), 0)
    table = jnp.zeros((16, LANES), jnp.float32)
    for i, part in enumerate(parts):
        table = jnp.where(row == i, jnp.broadcast_to(part, table.shape), table)
    table = table.astype(jnp.bfloat16)[:, :glob]
    pos = column_of(pos_ref[...])
    n_pairs = win_ref.shape[1]
    each = n_pairs // CORES
    for out_ref, which in ((own_ref, core), (sib_ref, 1 - core)):
        for j in range(each):
            pair = which * each + j
            token = (chip * n_pairs + pair) * LANES + lax.broadcasted_iota(jnp.int32, (glob, LANES), 1)
            hit = jnp.where(pos == token.astype(jnp.float32), 1.0, 0.0).astype(jnp.bfloat16)
            placed = dot_n(table, hit)
            is_glob = placed[6:7] > 0.5
            for i in (0, 1):
                value = placed[3 * i : 3 * i + 1] + placed[3 * i + 1 : 3 * i + 2] + placed[3 * i + 2 : 3 * i + 3]
                out_ref[i, j : j + 1, :] = jnp.where(is_glob, value, win_ref[i, pl.ds(pair, 1), :])


def window_kernel(
    scale2,
    q_t_ref,
    k_ref,
    v_t_ref,
    edge_a_ref,
    edge_b_ref,
    kv_a_ref,
    kv_b_ref,
    w_ref,
    pos_ref,
    out_ref,
    s_buf,
    e_buf,
    bias,
    w_cols,
    edges,
):
    half, tokens = q_t_ref.shape
    glob = pos_ref.shape[1]
    heads = half // LANES
    n_pairs = tokens // LANES
    core, chip = device_place()
    chips = lax.axis_size("seq") // CORES
    left = lax.broadcasted_iota(jnp.int32, (BLK, LANES), 1) < BLK
    glob_block = column_of(pos_ref[...] // BLK)
    for j in range(n_pairs):
        block = (chip * n_pairs + j) * (LANES // BLK) + lax.broadcasted_iota(jnp.int32, (glob, LANES), 1) // BLK
        bias[j] = jnp.where(jnp.abs(glob_block - block.astype(jnp.float32)) > 1.5, 0.0, NEG)
    first_bias = jnp.where(left & (chip == 0), NEG, 0.0)
    last_bias = jnp.where((~left) & (chip == chips - 1), NEG, 0.0)
    for head in range(heads):
        row = w_ref[pl.ds(core * heads + head, 1), :]
        w_cols[head] = jnp.transpose(jnp.broadcast_to(row, (LANES, LANES)))

    wide_left = lax.broadcasted_iota(jnp.int32, (LANES, LANES), 1) < BLK

    @pl.when(core == 1)
    def _():
        edges[0] = edge_a_ref[...]
        edges[1] = edge_b_ref[...]

    @pl.when(core == 0)
    def _():
        edges[0] = edge_b_ref[...]
        edges[1] = edge_a_ref[...]

    def one_head(head, carry):
        cols = pl.ds(pl.multiple_of(head * LANES, LANES), LANES)
        kg = kv_a_ref[:glob, cols] + kv_b_ref[:glob, cols]
        for j in range(n_pairs):
            q = q_t_ref[cols, j * LANES : (j + 1) * LANES]
            if j == 0:
                k = jnp.concatenate([edges[0, :BLK, cols], k_ref[BLK : 4 * BLK, cols]], axis=0)
            elif j == n_pairs - 1:
                k = jnp.concatenate([k_ref[j * LANES : j * LANES + 3 * BLK, cols], edges[1, :BLK, cols]], axis=0)
            else:
                k = k_ref[j * LANES : (j + 2) * LANES, cols]
            s_buf[j, : 4 * BLK] = dot_n(k, q)
            s_buf[j, 4 * BLK :] = dot_n(kg, q)
        inverses = []
        for j in range(n_pairs):
            far = s_buf[j, 4 * BLK :] + bias[j]
            ends = jnp.where(left, s_buf[j, :BLK], s_buf[j, 3 * BLK : 4 * BLK])
            if j == 0:
                ends = ends + first_bias
            if j == n_pairs - 1:
                ends = ends + last_bias
            mid = s_buf[j, BLK : 3 * BLK]
            peak = jnp.maximum(jnp.maximum(ends, far), jnp.maximum(mid[:BLK], mid[BLK:]))
            peak = jnp.max(peak, axis=0, keepdims=True)
            e_ends = jnp.exp2((ends - peak) * scale2)
            e_mid = jnp.exp2((mid - peak) * scale2)
            e_far = jnp.exp2((far - peak) * scale2)
            total = jnp.sum(e_ends + e_far + e_mid[:BLK] + e_mid[BLK:], axis=0, keepdims=True)
            zero = jnp.zeros_like(e_ends)
            e_buf[j, :BLK] = jnp.where(left, e_ends, zero).astype(jnp.bfloat16)
            e_buf[j, BLK : 3 * BLK] = e_mid.astype(jnp.bfloat16)
            e_buf[j, 3 * BLK : 4 * BLK] = jnp.where(left, zero, e_ends).astype(jnp.bfloat16)
            e_buf[j, 4 * BLK :] = e_far.astype(jnp.bfloat16)
            inverses.append(1.0 / total)
        vg_t = jnp.transpose(kv_a_ref[glob:, cols] + kv_b_ref[glob:, cols])
        turned = jnp.transpose(jnp.concatenate([edges[0, BLK:, cols], edges[1, BLK:, cols]], axis=0))
        w = w_cols[head]
        lins, sqs = [], []
        for j in range(n_pairs):
            v_0 = v_t_ref[cols, j * LANES : (j + 1) * LANES]
            v_1 = v_t_ref[cols, (j + 1) * LANES : (j + 2) * LANES]
            if j == 0:
                v_0 = jnp.where(wide_left, turned, v_0)
            if j == n_pairs - 1:
                v_1 = jnp.where(wide_left, v_1, turned)
            near = dot_n(jnp.concatenate([v_0, v_1], axis=1), e_buf[j, : 4 * BLK])
            acc = near + dot_n(vg_t, e_buf[j, 4 * BLK :])
            lins.append(jnp.sum(acc * w, axis=0, keepdims=True) * inverses[j])
            sqs.append(jnp.sum(acc * acc, axis=0, keepdims=True) * (inverses[j] * inverses[j]))
        lin, sq = carry
        return lin + jnp.concatenate(lins, axis=0), sq + jnp.concatenate(sqs, axis=0)

    none = jnp.zeros((n_pairs, LANES), jnp.float32)
    lin, sq = lax.fori_loop(0, half // LANES, one_head, (none, none))
    out_ref[0] = lin
    out_ref[1] = sq


def call(kernel, name, outs, args, scratch=()):
    spec = pl.BlockSpec(memory_space=pltpu.VMEM)
    single = not isinstance(outs, list)
    shapes = [outs] if single else outs
    result = pl.pallas_call(
        kernel,
        in_specs=[spec] * len(args),
        out_specs=[spec] * len(shapes),
        out_shape=[pltpu.VMEM(shape, dtype) for shape, dtype in shapes],
        scratch_shapes=[pltpu.VMEM(shape, dtype) for shape, dtype in scratch],
        compiler_params=pltpu.CompilerParams(vmem_limit_bytes=16 * 1024 * 1024),
        cost_estimate=pl.CostEstimate(flops=1, transcendentals=0, bytes_accessed=1),
        name=name,
    )(*[pltpu.with_memory_space_constraint(x, pltpu.VMEM) for x in args])
    return result[0] if single else result


def on_device(queries, keys, values, global_positions, score_weight):
    rows, model_width = queries.shape
    head_size = model_width // HEADS
    half = model_width // CORES
    half_heads = HEADS // CORES
    glob = global_positions.shape[0]
    seq_count = lax.axis_size("seq")
    chips = seq_count // CORES
    scale2 = head_size ** (-0.5) * LOG2E
    bf16 = jnp.bfloat16
    f32 = jnp.float32
    rounds = int(math.log2(chips))
    tokens = CORES * rows
    n_pairs = tokens // LANES

    def swap(x, mask):
        return lax.ppermute(x, "seq", [(i, i ^ mask) for i in range(seq_count)])

    def shift(x, even, odd):
        moves = [(i, i + (odd if i % CORES else even) * CORES) for i in range(seq_count)]
        return lax.ppermute(x, "seq", [(i, to) for i, to in moves if 0 <= to < seq_count])

    def after(arrays, *others):
        return lax.optimization_barrier((*arrays, *others))[: len(arrays)]

    row_positions = global_positions.reshape(1, glob)
    small = ((glob, half), bf16)
    pair_of = ((2 * glob, half), bf16)
    edge = ((2 * BLK, half), bf16)
    q_own, q_sib = call(
        functools.partial(select_q_kernel, half), "select_queries", [small, small], [row_positions, queries]
    )
    keys, values, queries = after((keys, values, queries), q_sib)
    kv_own, edge_own, kv_sib = call(
        functools.partial(select_kv_kernel, half),
        "select_keys_values",
        [pair_of, edge, ((2 * glob + 2 * BLK + 3 * rows, half), bf16)],
        [row_positions, keys, values, queries],
    )
    sib_recv = swap(kv_sib, 1)
    q_near = call(add_kernel, "add_queries", small, [q_own, swap(q_sib, 1)])
    edge_own = after((edge_own,), q_near)[0]
    edge_a = shift(edge_own, -1, 1)
    for r in range(1, rounds):
        q_near = call(add_kernel, "add_queries", small, [q_near, swap(q_near, 1 << r)])
    q_far = swap(q_near, 1 << rounds)

    kv_near, edge_recv = call(split_kernel, "join_keys_values", [pair_of, edge], [kv_own, sib_recv])
    edge_b = shift(edge_recv, 1, -1)
    for r in range(1, rounds):
        kv_near = call(add_kernel, "add_keys_values", pair_of, [kv_near, swap(kv_near, 1 << r)])
    kv_far = swap(kv_near, 1 << rounds)

    k_all, v_t, q_t = call(
        prepare_kernel,
        "prepare",
        [((tokens + 2 * BLK, half), bf16), ((half, tokens + 2 * BLK), bf16), ((half, tokens), bf16)],
        [queries, keys, values, sib_recv],
        [((tokens + 2 * BLK, half), bf16)],
    )
    k_all, v_t = after((k_all, v_t), edge_a, edge_b, kv_near)
    part = ((half_heads // 2, head_size + STAT_ROWS, LANES), bf16)
    message = call(
        functools.partial(global_kernel, scale2),
        "global_partial",
        part,
        [q_near, q_far, k_all, v_t],
        [((half_heads // 2, tokens, LANES), f32), ((half_heads // 2, tokens + 2 * BLK, LANES), bf16)],
    )
    for r in range(1, rounds):
        message = call(
            functools.partial(merge_kernel, scale2), "merge_partial", part, [message, swap(message, 1 << r)]
        )
    message_far = swap(message, 1 << rounds)

    weights = score_weight.reshape(HEADS, head_size)
    window = call(
        functools.partial(window_kernel, scale2),
        "window_attention",
        ((2, n_pairs, LANES), f32),
        [q_t, k_all, v_t, edge_a, edge_b, kv_near, kv_far, weights, row_positions],
        [
            ((n_pairs, 4 * BLK + glob, LANES), f32),
            ((n_pairs, 4 * BLK + glob, LANES), bf16),
            ((n_pairs, glob, LANES), f32),
            ((half_heads, LANES, LANES), f32),
            ((2, 2 * BLK, half), bf16),
        ],
    )
    share = ((2, n_pairs // CORES, LANES), f32)
    mine, theirs = call(
        functools.partial(final_kernel, scale2),
        "place_global",
        [share, share],
        [message, message_far, weights, row_positions, window],
    )
    theirs = swap(theirs, 1)
    lin = mine[0] + theirs[0]
    sq = mine[1] + theirs[1]
    return (lin * lax.rsqrt(sq * (1.0 / model_width) + 1e-06)).reshape(rows)


def solution(mesh):
    placed = (
        P(("doc", "seq"), None),
        P(("doc", "seq"), None),
        P(("doc", "seq"), None),
        P("doc"),
        P(),
    )
    return jax.shard_map(
        on_device, mesh=mesh, in_specs=placed, out_specs=P(("doc", "seq")), check_vma=False
    )
```

```python
import functools
import math

import jax
import jax.numpy as jnp
from jax import lax
from jax.experimental import pallas as pl
from jax.experimental.pallas import tpu as pltpu
from jax.sharding import PartitionSpec as P

HEADS = 16
BLK = 64
CORES = 2
LANES = 128
NEG = -1e30
LOG2E = math.log2(math.e)
STAT_ROWS = 16


def pieces(x):
    hi = x.astype(jnp.bfloat16)
    rest = x - hi.astype(jnp.float32)
    mid = rest.astype(jnp.bfloat16)
    low = (rest - mid.astype(jnp.float32)).astype(jnp.bfloat16)
    return hi, mid, low


def dot_t(a, b):
    return lax.dot_general(a, b, (((1,), (1,)), ((), ())), preferred_element_type=jnp.float32)


def dot_n(a, b):
    return lax.dot_general(a, b, (((1,), (0,)), ((), ())), preferred_element_type=jnp.float32)


def put_message(out_ref, pair, out, peak, total):
    rows = out.shape[0]
    out_ref[pair, :rows, :] = out.astype(jnp.bfloat16)
    stats = [p.astype(jnp.float32) for p in (*pieces(peak), *pieces(total))]
    row = lax.broadcasted_iota(jnp.int32, (STAT_ROWS, LANES), 0)
    block = jnp.zeros((STAT_ROWS, LANES), jnp.float32)
    for i, stat in enumerate(stats):
        block = jnp.where(row == i, jnp.broadcast_to(stat, block.shape), block)
    out_ref[pair, rows:, :] = block.astype(jnp.bfloat16)


def get_message(ref, pair, head_size):
    out = ref[pair, :head_size, :].astype(jnp.float32)
    stats = ref[pair, head_size:, :].astype(jnp.float32)
    peak = stats[0:1] + stats[1:2] + stats[2:3]
    total = stats[3:4] + stats[4:5] + stats[5:6]
    return out, peak, total


def merged(a, b, scale2):
    out_a, peak_a, total_a = a
    out_b, peak_b, total_b = b
    peak = jnp.maximum(peak_a, peak_b)
    weight_a = jnp.exp2((peak_a - peak) * scale2) * total_a
    weight_b = jnp.exp2((peak_b - peak) * scale2) * total_b
    total = weight_a + weight_b
    inv = 1.0 / total
    return out_a * (weight_a * inv) + out_b * (weight_b * inv), peak, total


def device_place():
    index = lax.axis_index("seq")
    return index % CORES, index // CORES


def column_of(row):
    wide = jnp.concatenate([row, row], axis=1).astype(jnp.float32)
    return jnp.transpose(jnp.broadcast_to(wide, (LANES, LANES)))[: row.shape[1]]


def pick(x_ref, hit, out_ref, at, cols):
    contract = (((0,), (0,)), ((), ()))
    picked = lax.dot_general(hit, x_ref[:, cols], contract, preferred_element_type=jnp.float32)
    out_ref[at : at + hit.shape[1], :] = picked.astype(jnp.bfloat16)


def own_positions(pos_ref, rows):
    core, chip = device_place()
    row = (chip * CORES + core) * rows + lax.broadcasted_iota(jnp.int32, (rows, pos_ref.shape[1]), 0)
    return jnp.where(row == pos_ref[...], 1.0, 0.0).astype(jnp.bfloat16)


def select_q_kernel(half, pos_hbm, q_hbm, own_ref, sib_ref, pos_ref, q_ref, sems):
    core, _ = device_place()
    copies = [pltpu.make_async_copy(pos_hbm, pos_ref, sems.at[2])]
    for slot, which in ((0, 1 - core), (1, core)):
        cols = pl.ds(pl.multiple_of(which * half, half), half)
        copies.append(pltpu.make_async_copy(q_hbm.at[:, cols], q_ref.at[slot], sems.at[slot]))
    for copy in copies:
        copy.start()
    copies[0].wait()
    hit = own_positions(pos_ref, q_ref.shape[1])
    for slot, out_ref in ((0, sib_ref), (1, own_ref)):
        copies[1 + slot].wait()
        pick(q_ref.at[slot], hit, out_ref, 0, slice(None))


def select_kv_kernel(half, pos_ref, k_ref, v_ref, q_ref, own_ref, edge_ref, sib_ref):
    rows = k_ref.shape[0]
    glob = pos_ref.shape[1]
    hit = own_positions(pos_ref, rows)
    core, _ = device_place()
    block = pl.ds(pl.multiple_of(core * (rows - BLK), BLK), BLK)
    mine = pl.ds(pl.multiple_of(core * half, half), half)
    theirs = pl.ds(pl.multiple_of((1 - core) * half, half), half)
    start = 2 * glob + 2 * BLK
    for i, x_ref in enumerate((k_ref, v_ref)):
        pick(x_ref, hit, sib_ref, i * glob, theirs)
        sib_ref[2 * glob + i * BLK : 2 * glob + (i + 1) * BLK, :] = x_ref[block, theirs]
        sib_ref[start + i * rows : start + (i + 1) * rows, :] = x_ref[:, theirs]
        pick(x_ref, hit, own_ref, i * glob, mine)
        edge_ref[i * BLK : (i + 1) * BLK, :] = x_ref[block, mine]
    sib_ref[start + 2 * rows :, :] = q_ref[:, theirs]


def split_kernel(a_ref, b_ref, sum_ref, rest_ref):
    count = sum_ref.shape[0]
    sum_ref[...] = a_ref[...] + b_ref[:count, :]
    rest_ref[...] = b_ref[count : count + rest_ref.shape[0], :]


def add_kernel(a_ref, b_ref, out_ref):
    count = out_ref.shape[0]
    out_ref[...] = a_ref[:count, :] + b_ref[:count, :]


def prepare_kernel(q_own_ref, k_own_ref, v_own_ref, sib_ref, k_ref, v_t_ref, q_t_ref, v_all):
    rows = k_own_ref.shape[0]
    half = k_ref.shape[1]
    core, _ = device_place()
    cols = pl.ds(pl.multiple_of(core * half, half), half)
    own = pl.multiple_of(core * rows, BLK)
    sib = pl.multiple_of((1 - core) * rows, BLK)
    start = sib_ref.shape[0] - 3 * rows
    zero = jnp.zeros((BLK, half), jnp.bfloat16)
    for i, (ref, own_ref) in enumerate(((k_ref, k_own_ref), (v_all, v_own_ref))):
        ref[:BLK, :] = zero
        ref[BLK + CORES * rows :, :] = zero
        ref[pl.ds(pl.multiple_of(own + BLK, BLK), rows), :] = own_ref[:, cols]
        ref[pl.ds(pl.multiple_of(sib + BLK, BLK), rows), :] = sib_ref[start + i * rows : start + (i + 1) * rows, :]

    def turn(head, carry):
        lanes = pl.ds(pl.multiple_of(head * LANES, LANES), LANES)
        v_t_ref[lanes, :] = jnp.transpose(v_all[:, lanes])
        source = pl.ds(pl.multiple_of(core * half + head * LANES, LANES), LANES)
        q_t_ref[lanes, pl.ds(pl.multiple_of(own, LANES), rows)] = jnp.transpose(q_own_ref[:, source])
        q_t_ref[lanes, pl.ds(pl.multiple_of(sib, LANES), rows)] = jnp.transpose(sib_ref[start + 2 * rows :, lanes])
        return carry

    lax.fori_loop(0, half // LANES, turn, 0)


def global_kernel(scale2, q_a_ref, q_b_ref, k_ref, v_t_ref, out_ref, s_buf, e_buf):
    glob, half = q_a_ref.shape
    head_size = LANES
    pairs = half // (2 * head_size)
    tokens = k_ref.shape[0] - 2 * BLK
    row = lax.broadcasted_iota(jnp.int32, (2 * glob, 2 * head_size), 0)
    col = lax.broadcasted_iota(jnp.int32, (2 * glob, 2 * head_size), 1)
    keep = (row < glob) == (col < head_size)
    lane = lax.broadcasted_iota(jnp.int32, (head_size, LANES), 1)
    for pair in range(pairs):
        cols = slice(2 * pair * head_size, 2 * (pair + 1) * head_size)
        q = q_a_ref[:, cols] + q_b_ref[:, cols]
        doubled = jnp.concatenate([q, q], axis=0)
        diag = jnp.where(keep, doubled, jnp.zeros_like(doubled))
        s_buf[pair] = dot_t(k_ref[BLK : BLK + tokens, cols], diag)
    stats = []
    for pair in range(pairs):
        s = s_buf[pair]
        peak = jnp.max(s, axis=0, keepdims=True)
        e = jnp.exp2((s - peak) * scale2)
        stats.append((peak, jnp.sum(e, axis=0, keepdims=True)))
        zero = jnp.zeros((BLK, LANES), jnp.bfloat16)
        e_buf[pair, :BLK] = zero
        e_buf[pair, BLK + tokens :] = zero
        e_buf[pair, BLK : BLK + tokens] = e.astype(jnp.bfloat16)
    for pair in range(pairs):
        rows = slice(2 * pair * head_size, 2 * (pair + 1) * head_size)
        acc = dot_n(v_t_ref[rows, :], e_buf[pair])
        peak, total = stats[pair]
        out = jnp.where(lane < glob, acc[:head_size], acc[head_size:]) / total
        put_message(out_ref, pair, out, peak, total)


def merge_kernel(scale2, a_ref, b_ref, out_ref):
    head_size = a_ref.shape[1] - STAT_ROWS
    for pair in range(a_ref.shape[0]):
        a = get_message(a_ref, pair, head_size)
        b = get_message(b_ref, pair, head_size)
        put_message(out_ref, pair, *merged(a, b, scale2))


def final_kernel(scale2, a_ref, b_ref, w_ref, pos_ref, win_ref, own_ref, sib_ref):
    pairs = a_ref.shape[0]
    head_size = a_ref.shape[1] - STAT_ROWS
    glob = pos_ref.shape[1]
    core, chip = device_place()
    upper = lax.broadcasted_iota(jnp.int32, (LANES, head_size), 0) < glob
    lin = jnp.zeros((1, LANES), jnp.float32)
    sq = jnp.zeros((1, LANES), jnp.float32)
    for pair in range(pairs):
        a = get_message(a_ref, pair, head_size)
        b = get_message(b_ref, pair, head_size)
        out, _, _ = merged(a, b, scale2)
        w_a = w_ref[pl.ds(core * 2 * pairs + 2 * pair, 1), :]
        w_b = w_ref[pl.ds(core * 2 * pairs + 2 * pair + 1, 1), :]
        w = jnp.transpose(jnp.where(upper, w_a, w_b))
        lin = lin + jnp.sum(out * w, axis=0, keepdims=True)
        sq = sq + jnp.sum(out * out, axis=0, keepdims=True)
    lin = lin + pltpu.roll(lin, glob, 1)
    sq = sq + pltpu.roll(sq, glob, 1)
    parts = [p.astype(jnp.float32) for p in (*pieces(lin), *pieces(sq))] + [jnp.ones((1, LANES), jnp.float32)]
    row = lax.broadcasted_iota(jnp.int32, (16, LANES), 0)
    table = jnp.zeros((16, LANES), jnp.float32)
    for i, part in enumerate(parts):
        table = jnp.where(row == i, jnp.broadcast_to(part, table.shape), table)
    table = table.astype(jnp.bfloat16)[:, :glob]
    pos = column_of(pos_ref[...])
    n_pairs = win_ref.shape[1]
    each = n_pairs // CORES
    for out_ref, which in ((own_ref, core), (sib_ref, 1 - core)):
        for j in range(each):
            pair = which * each + j
            token = (chip * n_pairs + pair) * LANES + lax.broadcasted_iota(jnp.int32, (glob, LANES), 1)
            hit = jnp.where(pos == token.astype(jnp.float32), 1.0, 0.0).astype(jnp.bfloat16)
            placed = dot_n(table, hit)
            is_glob = placed[6:7] > 0.5
            for i in (0, 1):
                value = placed[3 * i : 3 * i + 1] + placed[3 * i + 1 : 3 * i + 2] + placed[3 * i + 2 : 3 * i + 3]
                out_ref[i, j : j + 1, :] = jnp.where(is_glob, value, win_ref[i, pl.ds(pair, 1), :])


def near_kernel(scale2, q_t_ref, k_ref, v_t_ref, edge_a_ref, edge_b_ref, acc_ref, stat_ref, s_buf, e_buf, edges):
    half, tokens = q_t_ref.shape
    n_pairs = tokens // LANES
    core, chip = device_place()
    chips = lax.axis_size("seq") // CORES
    left = lax.broadcasted_iota(jnp.int32, (BLK, LANES), 1) < BLK
    wide_left = lax.broadcasted_iota(jnp.int32, (LANES, LANES), 1) < BLK
    first_bias = jnp.where(left & (chip == 0), NEG, 0.0)
    last_bias = jnp.where((~left) & (chip == chips - 1), NEG, 0.0)

    @pl.when(core == 1)
    def _():
        edges[0] = edge_a_ref[...]
        edges[1] = edge_b_ref[...]

    @pl.when(core == 0)
    def _():
        edges[0] = edge_b_ref[...]
        edges[1] = edge_a_ref[...]

    def one_head(head, carry):
        cols = pl.ds(pl.multiple_of(head * LANES, LANES), LANES)
        for j in range(n_pairs):
            if j == 0:
                k = jnp.concatenate([edges[0, :BLK, cols], k_ref[BLK : 4 * BLK, cols]], axis=0)
            elif j == n_pairs - 1:
                k = jnp.concatenate([k_ref[j * LANES : j * LANES + 3 * BLK, cols], edges[1, :BLK, cols]], axis=0)
            else:
                k = k_ref[j * LANES : (j + 2) * LANES, cols]
            s_buf[j] = dot_n(k, q_t_ref[cols, j * LANES : (j + 1) * LANES])
        peaks, totals = [], []
        for j in range(n_pairs):
            ends = jnp.where(left, s_buf[j, :BLK], s_buf[j, 3 * BLK :])
            if j == 0:
                ends = ends + first_bias
            if j == n_pairs - 1:
                ends = ends + last_bias
            mid = s_buf[j, BLK : 3 * BLK]
            peak = jnp.max(jnp.maximum(ends, jnp.maximum(mid[:BLK], mid[BLK:])), axis=0, keepdims=True)
            e_ends = jnp.exp2((ends - peak) * scale2)
            e_mid = jnp.exp2((mid - peak) * scale2)
            zero = jnp.zeros_like(e_ends)
            e_buf[j, :BLK] = jnp.where(left, e_ends, zero).astype(jnp.bfloat16)
            e_buf[j, BLK : 3 * BLK] = e_mid.astype(jnp.bfloat16)
            e_buf[j, 3 * BLK :] = jnp.where(left, zero, e_ends).astype(jnp.bfloat16)
            peaks.append(peak)
            totals.append(jnp.sum(e_ends + e_mid[:BLK] + e_mid[BLK:], axis=0, keepdims=True))
        stat_ref[head, 0] = jnp.concatenate(peaks, axis=0)
        stat_ref[head, 1] = jnp.concatenate(totals, axis=0)
        turned = jnp.transpose(jnp.concatenate([edges[0, BLK:, cols], edges[1, BLK:, cols]], axis=0))
        for j in range(n_pairs):
            v_0 = v_t_ref[cols, j * LANES : (j + 1) * LANES]
            v_1 = v_t_ref[cols, (j + 1) * LANES : (j + 2) * LANES]
            if j == 0:
                v_0 = jnp.where(wide_left, turned, v_0)
            if j == n_pairs - 1:
                v_1 = jnp.where(wide_left, v_1, turned)
            acc_ref[head, j] = dot_n(jnp.concatenate([v_0, v_1], axis=1), e_buf[j])
        return carry

    lax.fori_loop(0, half // LANES, one_head, 0)


def far_kernel(
    scale2, q_t_ref, acc_ref, stat_ref, kv_a_ref, kv_b_ref, w_ref, pos_ref, out_ref, s_buf, e_buf, bias, w_cols
):
    half, tokens = q_t_ref.shape
    glob = pos_ref.shape[1]
    heads = half // LANES
    n_pairs = tokens // LANES
    core, chip = device_place()
    glob_block = column_of(pos_ref[...] // BLK)
    for j in range(n_pairs):
        block = (chip * n_pairs + j) * (LANES // BLK) + lax.broadcasted_iota(jnp.int32, (glob, LANES), 1) // BLK
        bias[j] = jnp.where(jnp.abs(glob_block - block.astype(jnp.float32)) > 1.5, 0.0, NEG)
    for head in range(heads):
        row = w_ref[pl.ds(core * heads + head, 1), :]
        w_cols[head] = jnp.transpose(jnp.broadcast_to(row, (LANES, LANES)))

    def one_head(head, carry):
        cols = pl.ds(pl.multiple_of(head * LANES, LANES), LANES)
        kg = kv_a_ref[:glob, cols] + kv_b_ref[:glob, cols]
        for j in range(n_pairs):
            s_buf[j] = dot_n(kg, q_t_ref[cols, j * LANES : (j + 1) * LANES])
        near_peaks = stat_ref[head, 0]
        near_totals = stat_ref[head, 1]
        near_weights, inverses = [], []
        for j in range(n_pairs):
            far = s_buf[j] + bias[j]
            near_peak = near_peaks[j : j + 1]
            peak = jnp.maximum(jnp.max(far, axis=0, keepdims=True), near_peak)
            e_far = jnp.exp2((far - peak) * scale2)
            e_buf[j] = e_far.astype(jnp.bfloat16)
            near_weight = jnp.exp2((near_peak - peak) * scale2)
            total = near_totals[j : j + 1] * near_weight + jnp.sum(e_far, axis=0, keepdims=True)
            near_weights.append(near_weight)
            inverses.append(1.0 / total)
        vg_t = jnp.transpose(kv_a_ref[glob:, cols] + kv_b_ref[glob:, cols])
        w = w_cols[head]
        lins, sqs = [], []
        for j in range(n_pairs):
            acc = acc_ref[head, j] * near_weights[j] + dot_n(vg_t, e_buf[j])
            lins.append(jnp.sum(acc * w, axis=0, keepdims=True) * inverses[j])
            sqs.append(jnp.sum(acc * acc, axis=0, keepdims=True) * (inverses[j] * inverses[j]))
        lin, sq = carry
        return lin + jnp.concatenate(lins, axis=0), sq + jnp.concatenate(sqs, axis=0)

    none = jnp.zeros((n_pairs, LANES), jnp.float32)
    lin, sq = lax.fori_loop(0, heads, one_head, (none, none))
    out_ref[0] = lin
    out_ref[1] = sq


def call(kernel, name, outs, args, scratch=(), micros=0.0, from_hbm=False):
    spec = pl.BlockSpec(memory_space=pltpu.VMEM)
    source = pltpu.HBM if from_hbm else pltpu.VMEM
    single = not isinstance(outs, list)
    shapes = [outs] if single else outs
    result = pl.pallas_call(
        kernel,
        in_specs=[pl.BlockSpec(memory_space=source)] * len(args),
        out_specs=[spec] * len(shapes),
        out_shape=[pltpu.VMEM(shape, dtype) for shape, dtype in shapes],
        scratch_shapes=[pltpu.VMEM(*x) if isinstance(x, tuple) else x for x in scratch],
        compiler_params=pltpu.CompilerParams(vmem_limit_bytes=16 * 1024 * 1024),
        cost_estimate=pl.CostEstimate(flops=int(micros * 1e9) + 1, transcendentals=0, bytes_accessed=1),
        name=name,
    )(*[pltpu.with_memory_space_constraint(x, source) for x in args])
    return result[0] if single else result


def on_device(queries, keys, values, global_positions, score_weight):
    rows, model_width = queries.shape
    head_size = model_width // HEADS
    half = model_width // CORES
    half_heads = HEADS // CORES
    glob = global_positions.shape[0]
    seq_count = lax.axis_size("seq")
    chips = seq_count // CORES
    scale2 = head_size ** (-0.5) * LOG2E
    bf16 = jnp.bfloat16
    f32 = jnp.float32
    rounds = int(math.log2(chips))
    tokens = CORES * rows
    n_pairs = tokens // LANES

    def swap(x, mask):
        return lax.ppermute(x, "seq", [(i, i ^ mask) for i in range(seq_count)])

    def shift(x, even, odd):
        moves = [(i, i + (odd if i % CORES else even) * CORES) for i in range(seq_count)]
        return lax.ppermute(x, "seq", [(i, to) for i, to in moves if 0 <= to < seq_count])

    def after(arrays, *others):
        return lax.optimization_barrier((*arrays, *others))[: len(arrays)]

    row_positions = global_positions.reshape(1, glob)
    small = ((glob, half), bf16)
    pair_of = ((2 * glob, half), bf16)
    edge = ((2 * BLK, half), bf16)
    q_own, q_sib = call(
        functools.partial(select_q_kernel, half),
        "select_queries",
        [small, small],
        [row_positions, queries],
        [((1, glob), jnp.int32), ((CORES, rows, half), bf16), pltpu.SemaphoreType.DMA((3,))],
        from_hbm=True,
    )
    keys, values, queries = after((keys, values, queries), q_sib)
    kv_own, edge_own, kv_sib = call(
        functools.partial(select_kv_kernel, half),
        "select_keys_values",
        [pair_of, edge, ((2 * glob + 2 * BLK + 3 * rows, half), bf16)],
        [row_positions, keys, values, queries],
    )
    q_near = call(add_kernel, "add_queries", small, [q_own, swap(q_sib, 1)])
    kv_sib = after((kv_sib,), q_near)[0]
    sib_recv = swap(kv_sib, 1)
    for r in range(1, rounds):
        q_near = call(add_kernel, "add_queries", small, [q_near, swap(q_near, 1 << r)])
    q_far = swap(q_near, 1 << rounds)

    k_all, v_t, q_t = call(
        prepare_kernel,
        "prepare",
        [((tokens + 2 * BLK, half), bf16), ((half, tokens + 2 * BLK), bf16), ((half, tokens), bf16)],
        [queries, keys, values, sib_recv],
        [((tokens + 2 * BLK, half), bf16)],
        micros=1.6,
    )
    kv_own, edge_own, sib_recv = after((kv_own, edge_own, sib_recv), k_all, q_near)
    edge_a = shift(edge_own, -1, 1)
    kv_near, edge_recv = call(split_kernel, "join_keys_values", [pair_of, edge], [kv_own, sib_recv])
    edge_b = shift(edge_recv, 1, -1)
    for r in range(1, rounds):
        kv_near = call(add_kernel, "add_keys_values", pair_of, [kv_near, swap(kv_near, 1 << r)])
    kv_far = swap(kv_near, 1 << rounds)

    part = ((half_heads // 2, head_size + STAT_ROWS, LANES), bf16)
    message = call(
        functools.partial(global_kernel, scale2),
        "global_partial",
        part,
        [q_near, q_far, k_all, v_t],
        [((half_heads // 2, tokens, LANES), f32), ((half_heads // 2, tokens + 2 * BLK, LANES), bf16)],
    )
    for r in range(1, rounds):
        message = call(
            functools.partial(merge_kernel, scale2), "merge_partial", part, [message, swap(message, 1 << r)]
        )
    message_far = swap(message, 1 << rounds)

    weights = score_weight.reshape(HEADS, head_size)
    near_acc, near_stat = call(
        functools.partial(near_kernel, scale2),
        "near_attention",
        [((half_heads, n_pairs, head_size, LANES), f32), ((half_heads, 2, n_pairs, LANES), f32)],
        [q_t, k_all, v_t, edge_a, edge_b],
        [((n_pairs, 4 * BLK, LANES), f32), ((n_pairs, 4 * BLK, LANES), bf16), ((2, 2 * BLK, half), bf16)],
        micros=4.0,
    )
    window = call(
        functools.partial(far_kernel, scale2),
        "far_attention",
        ((2, n_pairs, LANES), f32),
        [q_t, near_acc, near_stat, kv_near, kv_far, weights, row_positions],
        [
            ((n_pairs, glob, LANES), f32),
            ((n_pairs, glob, LANES), bf16),
            ((n_pairs, glob, LANES), f32),
            ((half_heads, LANES, LANES), f32),
        ],
        micros=2.0,
    )
    share = ((2, n_pairs // CORES, LANES), f32)
    mine, theirs = call(
        functools.partial(final_kernel, scale2),
        "place_global",
        [share, share],
        [message, message_far, weights, row_positions, window],
    )
    theirs = swap(theirs, 1)
    lin = mine[0] + theirs[0]
    sq = mine[1] + theirs[1]
    return (lin * lax.rsqrt(sq * (1.0 / model_width) + 1e-06)).reshape(rows)


def solution(mesh):
    placed = (
        P(("doc", "seq"), None),
        P(("doc", "seq"), None),
        P(("doc", "seq"), None),
        P("doc"),
        P(),
    )
    return jax.shard_map(
        on_device, mesh=mesh, in_specs=placed, out_specs=P(("doc", "seq")), check_vma=False
    )
```

```python
import functools
import math

import jax
import jax.numpy as jnp
from jax import lax
from jax.experimental import pallas as pl
from jax.experimental.pallas import tpu as pltpu
from jax.sharding import PartitionSpec as P

HEADS = 16
BLK = 64
CORES = 2
LANES = 128
NEG = -1e30
LOG2E = math.log2(math.e)
STAT_ROWS = 16


def pieces(x):
    hi = x.astype(jnp.bfloat16)
    rest = x - hi.astype(jnp.float32)
    mid = rest.astype(jnp.bfloat16)
    low = (rest - mid.astype(jnp.float32)).astype(jnp.bfloat16)
    return hi, mid, low


def dot_t(a, b):
    return lax.dot_general(a, b, (((1,), (1,)), ((), ())), preferred_element_type=jnp.float32)


def dot_n(a, b):
    return lax.dot_general(a, b, (((1,), (0,)), ((), ())), preferred_element_type=jnp.float32)


def put_message(out_ref, pair, out, peak, total):
    rows = out.shape[0]
    out_ref[pair, :rows, :] = out.astype(jnp.bfloat16)
    stats = [p.astype(jnp.float32) for p in (*pieces(peak), *pieces(total))]
    row = lax.broadcasted_iota(jnp.int32, (STAT_ROWS, LANES), 0)
    block = jnp.zeros((STAT_ROWS, LANES), jnp.float32)
    for i, stat in enumerate(stats):
        block = jnp.where(row == i, jnp.broadcast_to(stat, block.shape), block)
    out_ref[pair, rows:, :] = block.astype(jnp.bfloat16)


def get_message(ref, pair, head_size):
    out = ref[pair, :head_size, :].astype(jnp.float32)
    stats = ref[pair, head_size:, :].astype(jnp.float32)
    peak = stats[0:1] + stats[1:2] + stats[2:3]
    total = stats[3:4] + stats[4:5] + stats[5:6]
    return out, peak, total


def merged(a, b, scale2):
    out_a, peak_a, total_a = a
    out_b, peak_b, total_b = b
    peak = jnp.maximum(peak_a, peak_b)
    weight_a = jnp.exp2((peak_a - peak) * scale2) * total_a
    weight_b = jnp.exp2((peak_b - peak) * scale2) * total_b
    total = weight_a + weight_b
    inv = 1.0 / total
    return out_a * (weight_a * inv) + out_b * (weight_b * inv), peak, total


def device_place():
    index = lax.axis_index("seq")
    return index % CORES, index // CORES


def column_of(row):
    wide = jnp.concatenate([row, row], axis=1).astype(jnp.float32)
    return jnp.transpose(jnp.broadcast_to(wide, (LANES, LANES)))[: row.shape[1]]


def pick(x_ref, hit, out_ref, at, cols):
    contract = (((0,), (0,)), ((), ()))
    picked = lax.dot_general(hit, x_ref[:, cols], contract, preferred_element_type=jnp.float32)
    out_ref[at : at + hit.shape[1], :] = picked.astype(jnp.bfloat16)


def own_positions(pos_ref, rows):
    core, chip = device_place()
    row = (chip * CORES + core) * rows + lax.broadcasted_iota(jnp.int32, (rows, pos_ref.shape[1]), 0)
    return jnp.where(row == pos_ref[...], 1.0, 0.0).astype(jnp.bfloat16)


def select_q_kernel(half, pos_hbm, q_hbm, own_ref, sib_ref, pos_ref, q_ref, sems):
    core, _ = device_place()
    copies = [pltpu.make_async_copy(pos_hbm, pos_ref, sems.at[2])]
    for slot, which in ((0, 1 - core), (1, core)):
        cols = pl.ds(pl.multiple_of(which * half, half), half)
        copies.append(pltpu.make_async_copy(q_hbm.at[:, cols], q_ref.at[slot], sems.at[slot]))
    for copy in copies:
        copy.start()
    copies[0].wait()
    hit = own_positions(pos_ref, q_ref.shape[1])
    for slot, out_ref in ((0, sib_ref), (1, own_ref)):
        copies[1 + slot].wait()
        pick(q_ref.at[slot], hit, out_ref, 0, slice(None))


def select_kv_kernel(half, pos_ref, k_ref, v_ref, q_ref, own_ref, edge_ref, sib_ref, bulk_ref):
    rows = k_ref.shape[0]
    glob = pos_ref.shape[1]
    hit = own_positions(pos_ref, rows)
    core, _ = device_place()
    block = pl.ds(pl.multiple_of(core * (rows - BLK), BLK), BLK)
    mine = pl.ds(pl.multiple_of(core * half, half), half)
    theirs = pl.ds(pl.multiple_of((1 - core) * half, half), half)
    for i, x_ref in enumerate((k_ref, v_ref)):
        pick(x_ref, hit, sib_ref, i * glob, theirs)
        sib_ref[2 * glob + i * BLK : 2 * glob + (i + 1) * BLK, :] = x_ref[block, theirs]
        bulk_ref[i * rows : (i + 1) * rows, :] = x_ref[:, theirs]
        pick(x_ref, hit, own_ref, i * glob, mine)
        edge_ref[i * BLK : (i + 1) * BLK, :] = x_ref[block, mine]
    bulk_ref[2 * rows :, :] = q_ref[:, theirs]


def split_kernel(a_ref, b_ref, sum_ref, rest_ref):
    count = sum_ref.shape[0]
    sum_ref[...] = a_ref[...] + b_ref[:count, :]
    rest_ref[...] = b_ref[count:, :]


def add_kernel(a_ref, b_ref, out_ref):
    out_ref[...] = a_ref[...] + b_ref[...]


def on_line():
    return lax.axis_size("seq") // CORES == 4


def is_inner(chip):
    return (chip == 1) | (chip == 2)


def prepare_kernel(q_own_ref, k_own_ref, v_own_ref, sib_ref, k_ref, v_t_ref, q_t_ref, v_all):
    rows = k_own_ref.shape[0]
    half = k_ref.shape[1]
    core, _ = device_place()
    cols = pl.ds(pl.multiple_of(core * half, half), half)
    own = pl.multiple_of(core * rows, BLK)
    sib = pl.multiple_of((1 - core) * rows, BLK)
    zero = jnp.zeros((BLK, half), jnp.bfloat16)
    for i, (ref, own_ref) in enumerate(((k_ref, k_own_ref), (v_all, v_own_ref))):
        ref[:BLK, :] = zero
        ref[BLK + CORES * rows :, :] = zero
        ref[pl.ds(pl.multiple_of(own + BLK, BLK), rows), :] = own_ref[:, cols]
        ref[pl.ds(pl.multiple_of(sib + BLK, BLK), rows), :] = sib_ref[i * rows : (i + 1) * rows, :]

    def turn(head, carry):
        lanes = pl.ds(pl.multiple_of(head * LANES, LANES), LANES)
        v_t_ref[lanes, :] = jnp.transpose(v_all[:, lanes])
        source = pl.ds(pl.multiple_of(core * half + head * LANES, LANES), LANES)
        q_t_ref[lanes, pl.ds(pl.multiple_of(own, LANES), rows)] = jnp.transpose(q_own_ref[:, source])
        q_t_ref[lanes, pl.ds(pl.multiple_of(sib, LANES), rows)] = jnp.transpose(sib_ref[2 * rows :, lanes])
        return carry

    lax.fori_loop(0, half // LANES, turn, 0)


def global_kernel(scale2, q_a_ref, q_b_ref, k_ref, v_t_ref, out_ref, s_buf, e_buf):
    glob, half = q_a_ref.shape
    head_size = LANES
    pairs = half // (2 * head_size)
    tokens = k_ref.shape[0] - 2 * BLK
    row = lax.broadcasted_iota(jnp.int32, (2 * glob, 2 * head_size), 0)
    col = lax.broadcasted_iota(jnp.int32, (2 * glob, 2 * head_size), 1)
    keep = (row < glob) == (col < head_size)
    lane = lax.broadcasted_iota(jnp.int32, (head_size, LANES), 1)
    for pair in range(pairs):
        cols = slice(2 * pair * head_size, 2 * (pair + 1) * head_size)
        q = q_a_ref[:, cols] + q_b_ref[:, cols]
        doubled = jnp.concatenate([q, q], axis=0)
        diag = jnp.where(keep, doubled, jnp.zeros_like(doubled))
        s_buf[pair] = dot_t(k_ref[BLK : BLK + tokens, cols], diag)
    stats = []
    for pair in range(pairs):
        s = s_buf[pair]
        peak = jnp.max(s, axis=0, keepdims=True)
        e = jnp.exp2((s - peak) * scale2)
        stats.append((peak, jnp.sum(e, axis=0, keepdims=True)))
        zero = jnp.zeros((BLK, LANES), jnp.bfloat16)
        e_buf[pair, :BLK] = zero
        e_buf[pair, BLK + tokens :] = zero
        e_buf[pair, BLK : BLK + tokens] = e.astype(jnp.bfloat16)
    for pair in range(pairs):
        rows = slice(2 * pair * head_size, 2 * (pair + 1) * head_size)
        acc = dot_n(v_t_ref[rows, :], e_buf[pair])
        peak, total = stats[pair]
        out = jnp.where(lane < glob, acc[:head_size], acc[head_size:]) / total
        put_message(out_ref, pair, out, peak, total)


def merge_kernel(scale2, a_ref, b_ref, out_ref):
    head_size = a_ref.shape[1] - STAT_ROWS
    for pair in range(a_ref.shape[0]):
        a = get_message(a_ref, pair, head_size)
        b = get_message(b_ref, pair, head_size)
        put_message(out_ref, pair, *merged(a, b, scale2))


def inward_kernel(scale2, a_ref, b_ref, out_ref):
    _, chip = device_place()

    @pl.when(is_inner(chip))
    def _():
        merge_kernel(scale2, a_ref, b_ref, out_ref)

    @pl.when(jnp.logical_not(is_inner(chip)))
    def _():
        out_ref[...] = a_ref[...]


def sums_kernel(scale2, a_ref, b_ref, w_ref, out_ref):
    pairs = a_ref.shape[0]
    head_size = a_ref.shape[1] - STAT_ROWS
    glob = LANES // 2
    core, chip = device_place()
    upper = lax.broadcasted_iota(jnp.int32, (LANES, head_size), 0) < glob
    lin = jnp.zeros((1, LANES), jnp.float32)
    sq = jnp.zeros((1, LANES), jnp.float32)
    for pair in range(pairs):
        a = get_message(a_ref, pair, head_size)
        b = get_message(b_ref, pair, head_size)
        if on_line():
            b = tuple(jnp.where(is_inner(chip), y, x) for x, y in zip(a, b))
        out, _, _ = merged(a, b, scale2)
        w_a = w_ref[pl.ds(core * 2 * pairs + 2 * pair, 1), :]
        w_b = w_ref[pl.ds(core * 2 * pairs + 2 * pair + 1, 1), :]
        w = jnp.transpose(jnp.where(upper, w_a, w_b))
        lin = lin + jnp.sum(out * w, axis=0, keepdims=True)
        sq = sq + jnp.sum(out * out, axis=0, keepdims=True)
    out_ref[...] = jnp.zeros_like(out_ref)
    out_ref[0:1, :] = lin + pltpu.roll(lin, glob, 1)
    out_ref[1:2, :] = sq + pltpu.roll(sq, glob, 1)


def place_kernel(own_sums_ref, far_sums_ref, pos_ref, win_ref, own_ref, sib_ref):
    glob = pos_ref.shape[1]
    core, chip = device_place()
    sums = own_sums_ref[...]
    if on_line():
        sums = jnp.where(is_inner(chip), sums, far_sums_ref[...])
    parts = [p.astype(jnp.float32) for p in (*pieces(sums[0:1]), *pieces(sums[1:2]))] + [jnp.ones((1, LANES), jnp.float32)]
    row = lax.broadcasted_iota(jnp.int32, (16, LANES), 0)
    table = jnp.zeros((16, LANES), jnp.float32)
    for i, part in enumerate(parts):
        table = jnp.where(row == i, jnp.broadcast_to(part, table.shape), table)
    table = table.astype(jnp.bfloat16)[:, :glob]
    pos = column_of(pos_ref[...])
    n_pairs = win_ref.shape[1]
    each = n_pairs // CORES
    for out_ref, which in ((sib_ref, 1 - core), (own_ref, core)):
        for j in range(each):
            pair = which * each + j
            token = (chip * n_pairs + pair) * LANES + lax.broadcasted_iota(jnp.int32, (glob, LANES), 1)
            hit = jnp.where(pos == token.astype(jnp.float32), 1.0, 0.0).astype(jnp.bfloat16)
            placed = dot_n(table, hit)
            is_glob = placed[6:7] > 0.5
            for i in (0, 1):
                value = placed[3 * i : 3 * i + 1] + placed[3 * i + 1 : 3 * i + 2] + placed[3 * i + 2 : 3 * i + 3]
                out_ref[i, j : j + 1, :] = jnp.where(is_glob, value, win_ref[i, pl.ds(pair, 1), :])


def near_kernel(scale2, q_t_ref, k_ref, v_t_ref, edge_a_ref, edge_b_ref, acc_ref, stat_ref, s_buf, e_buf, edges):
    half, tokens = q_t_ref.shape
    n_pairs = tokens // LANES
    core, chip = device_place()
    chips = lax.axis_size("seq") // CORES
    left = lax.broadcasted_iota(jnp.int32, (BLK, LANES), 1) < BLK
    wide_left = lax.broadcasted_iota(jnp.int32, (LANES, LANES), 1) < BLK
    first_bias = jnp.where(left & (chip == 0), NEG, 0.0)
    last_bias = jnp.where((~left) & (chip == chips - 1), NEG, 0.0)

    @pl.when(core == 1)
    def _():
        edges[0] = edge_a_ref[...]
        edges[1] = edge_b_ref[...]

    @pl.when(core == 0)
    def _():
        edges[0] = edge_b_ref[...]
        edges[1] = edge_a_ref[...]

    def one_head(head, carry):
        cols = pl.ds(pl.multiple_of(head * LANES, LANES), LANES)
        for j in range(n_pairs):
            if j == 0:
                k = jnp.concatenate([edges[0, :BLK, cols], k_ref[BLK : 4 * BLK, cols]], axis=0)
            elif j == n_pairs - 1:
                k = jnp.concatenate([k_ref[j * LANES : j * LANES + 3 * BLK, cols], edges[1, :BLK, cols]], axis=0)
            else:
                k = k_ref[j * LANES : (j + 2) * LANES, cols]
            s_buf[j] = dot_n(k, q_t_ref[cols, j * LANES : (j + 1) * LANES])
        peaks, totals = [], []
        for j in range(n_pairs):
            ends = jnp.where(left, s_buf[j, :BLK], s_buf[j, 3 * BLK :])
            if j == 0:
                ends = ends + first_bias
            if j == n_pairs - 1:
                ends = ends + last_bias
            mid = s_buf[j, BLK : 3 * BLK]
            peak = jnp.max(jnp.maximum(ends, jnp.maximum(mid[:BLK], mid[BLK:])), axis=0, keepdims=True)
            e_ends = jnp.exp2((ends - peak) * scale2)
            e_mid = jnp.exp2((mid - peak) * scale2)
            zero = jnp.zeros_like(e_ends)
            e_buf[j, :BLK] = jnp.where(left, e_ends, zero).astype(jnp.bfloat16)
            e_buf[j, BLK : 3 * BLK] = e_mid.astype(jnp.bfloat16)
            e_buf[j, 3 * BLK :] = jnp.where(left, zero, e_ends).astype(jnp.bfloat16)
            peaks.append(peak)
            totals.append(jnp.sum(e_ends + e_mid[:BLK] + e_mid[BLK:], axis=0, keepdims=True))
        stat_ref[head, 0] = jnp.concatenate(peaks, axis=0)
        stat_ref[head, 1] = jnp.concatenate(totals, axis=0)
        turned = jnp.transpose(jnp.concatenate([edges[0, BLK:, cols], edges[1, BLK:, cols]], axis=0))
        for j in range(n_pairs):
            v_0 = v_t_ref[cols, j * LANES : (j + 1) * LANES]
            v_1 = v_t_ref[cols, (j + 1) * LANES : (j + 2) * LANES]
            if j == 0:
                v_0 = jnp.where(wide_left, turned, v_0)
            if j == n_pairs - 1:
                v_1 = jnp.where(wide_left, v_1, turned)
            acc_ref[head, j] = dot_n(jnp.concatenate([v_0, v_1], axis=1), e_buf[j])
        return carry

    lax.fori_loop(0, half // LANES, one_head, 0)


def far_kernel(
    scale2, q_t_ref, acc_ref, stat_ref, kv_a_ref, kv_b_ref, w_ref, pos_ref, out_ref, s_buf, e_buf, bias, w_cols
):
    half, tokens = q_t_ref.shape
    glob = pos_ref.shape[1]
    heads = half // LANES
    n_pairs = tokens // LANES
    core, chip = device_place()
    glob_block = column_of(pos_ref[...] // BLK)
    for j in range(n_pairs):
        block = (chip * n_pairs + j) * (LANES // BLK) + lax.broadcasted_iota(jnp.int32, (glob, LANES), 1) // BLK
        bias[j] = jnp.where(jnp.abs(glob_block - block.astype(jnp.float32)) > 1.5, 0.0, NEG)
    for head in range(heads):
        row = w_ref[pl.ds(core * heads + head, 1), :]
        w_cols[head] = jnp.transpose(jnp.broadcast_to(row, (LANES, LANES)))

    def one_head(head, carry):
        cols = pl.ds(pl.multiple_of(head * LANES, LANES), LANES)
        kv_a = kv_a_ref[:, cols]
        if on_line():
            kv_a = jnp.where(is_inner(chip), kv_a, jnp.zeros_like(kv_a))
        kv = kv_a + kv_b_ref[:, cols]
        kg = kv[:glob]
        for j in range(n_pairs):
            s_buf[j] = dot_n(kg, q_t_ref[cols, j * LANES : (j + 1) * LANES])
        near_peaks = stat_ref[head, 0]
        near_totals = stat_ref[head, 1]
        near_weights, inverses = [], []
        for j in range(n_pairs):
            far = s_buf[j] + bias[j]
            near_peak = near_peaks[j : j + 1]
            peak = jnp.maximum(jnp.max(far, axis=0, keepdims=True), near_peak)
            e_far = jnp.exp2((far - peak) * scale2)
            e_buf[j] = e_far.astype(jnp.bfloat16)
            near_weight = jnp.exp2((near_peak - peak) * scale2)
            total = near_totals[j : j + 1] * near_weight + jnp.sum(e_far, axis=0, keepdims=True)
            near_weights.append(near_weight)
            inverses.append(1.0 / total)
        vg_t = jnp.transpose(kv[glob:])
        w = w_cols[head]
        lins, sqs = [], []
        for j in range(n_pairs):
            acc = acc_ref[head, j] * near_weights[j] + dot_n(vg_t, e_buf[j])
            lins.append(jnp.sum(acc * w, axis=0, keepdims=True) * inverses[j])
            sqs.append(jnp.sum(acc * acc, axis=0, keepdims=True) * (inverses[j] * inverses[j]))
        lin, sq = carry
        return lin + jnp.concatenate(lins, axis=0), sq + jnp.concatenate(sqs, axis=0)

    none = jnp.zeros((n_pairs, LANES), jnp.float32)
    lin, sq = lax.fori_loop(0, heads, one_head, (none, none))
    out_ref[0] = lin
    out_ref[1] = sq


def call(kernel, name, outs, args, scratch=(), micros=0.0, from_hbm=False):
    spec = pl.BlockSpec(memory_space=pltpu.VMEM)
    source = pltpu.HBM if from_hbm else pltpu.VMEM
    single = not isinstance(outs, list)
    shapes = [outs] if single else outs
    result = pl.pallas_call(
        kernel,
        in_specs=[pl.BlockSpec(memory_space=source)] * len(args),
        out_specs=[spec] * len(shapes),
        out_shape=[pltpu.VMEM(shape, dtype) for shape, dtype in shapes],
        scratch_shapes=[pltpu.VMEM(*x) if isinstance(x, tuple) else x for x in scratch],
        compiler_params=pltpu.CompilerParams(vmem_limit_bytes=16 * 1024 * 1024),
        cost_estimate=pl.CostEstimate(flops=int(micros * 1e9) + 1, transcendentals=0, bytes_accessed=1),
        name=name,
    )(*[pltpu.with_memory_space_constraint(x, source) for x in args])
    return result[0] if single else result


def on_device(queries, keys, values, global_positions, score_weight):
    rows, model_width = queries.shape
    head_size = model_width // HEADS
    half = model_width // CORES
    half_heads = HEADS // CORES
    glob = global_positions.shape[0]
    seq_count = lax.axis_size("seq")
    chips = seq_count // CORES
    scale2 = head_size ** (-0.5) * LOG2E
    bf16 = jnp.bfloat16
    f32 = jnp.float32
    rounds = int(math.log2(chips))
    tokens = CORES * rows
    n_pairs = tokens // LANES

    def swap(x, mask):
        return lax.ppermute(x, "seq", [(i, i ^ mask) for i in range(seq_count)])

    def shift(x, even, odd):
        moves = [(i, i + (odd if i % CORES else even) * CORES) for i in range(seq_count)]
        return lax.ppermute(x, "seq", [(i, to) for i, to in moves if 0 <= to < seq_count])

    def move(x, pairs):
        return lax.ppermute(x, "seq", [(a * CORES + c, b * CORES + c) for a, b in pairs for c in range(CORES)])

    inward = ((0, 1), (3, 2))
    across = ((1, 2), (2, 1))
    outward = ((1, 0), (2, 3))

    def after(arrays, *others):
        return lax.optimization_barrier((*arrays, *others))[: len(arrays)]

    row_positions = global_positions.reshape(1, glob)
    small = ((glob, half), bf16)
    pair_of = ((2 * glob, half), bf16)
    edge = ((2 * BLK, half), bf16)
    q_own, q_sib = call(
        functools.partial(select_q_kernel, half),
        "select_queries",
        [small, small],
        [row_positions, queries],
        [((1, glob), jnp.int32), ((CORES, rows, half), bf16), pltpu.SemaphoreType.DMA((3,))],
        from_hbm=True,
    )
    later_positions = after((row_positions,), q_sib)[0]
    kv_own, edge_own, kv_sib, bulk_sib = call(
        functools.partial(select_kv_kernel, half),
        "select_keys_values",
        [pair_of, edge, ((2 * glob + 2 * BLK, half), bf16), ((3 * rows, half), bf16)],
        [later_positions, keys, values, queries],
    )
    q_near = call(add_kernel, "add_queries", small, [q_own, swap(q_sib, 1)])
    kv_near, edge_recv = call(split_kernel, "join_keys_values", [pair_of, edge], [kv_own, swap(kv_sib, 1)])
    bulk_sib = after((bulk_sib,), q_near, kv_near)[0]
    bulk_recv = swap(bulk_sib, 1)
    kv_near = after((kv_near,), q_near)[0]
    for r in range(1, rounds):
        q_near = call(add_kernel, "add_queries", small, [q_near, swap(q_near, 1 << r)])
    q_far = swap(q_near, 1 << rounds)

    edge_own, edge_recv = after((edge_own, edge_recv), q_near)
    edge_a = shift(edge_own, -1, 1)
    edge_b = shift(edge_recv, 1, -1)
    if chips == 4:
        kv_near = call(add_kernel, "add_keys_values", pair_of, [kv_near, move(kv_near, inward)])
        kv_near = call(add_kernel, "add_keys_values", pair_of, [kv_near, move(kv_near, across)])
        kv_far = move(kv_near, outward)
    else:
        for r in range(1, rounds):
            kv_near = call(add_kernel, "add_keys_values", pair_of, [kv_near, swap(kv_near, 1 << r)])
        kv_far = swap(kv_near, 1 << rounds)

    k_all, v_t, q_t = call(
        prepare_kernel,
        "prepare",
        [((tokens + 2 * BLK, half), bf16), ((half, tokens + 2 * BLK), bf16), ((half, tokens), bf16)],
        [queries, keys, values, bulk_recv],
        [((tokens + 2 * BLK, half), bf16)],
        micros=1.6,
    )
    part = ((half_heads // 2, head_size + STAT_ROWS, LANES), bf16)
    message = call(
        functools.partial(global_kernel, scale2),
        "global_partial",
        part,
        [q_near, q_far, k_all, v_t],
        [((half_heads // 2, tokens, LANES), f32), ((half_heads // 2, tokens + 2 * BLK, LANES), bf16)],
    )
    weights = score_weight.reshape(HEADS, head_size)
    if chips == 4:
        message = call(
            functools.partial(inward_kernel, scale2), "merge_partial", part, [message, move(message, inward)]
        )
        message_far = move(message, across)
    else:
        for r in range(1, rounds):
            message = call(
                functools.partial(merge_kernel, scale2), "merge_partial", part, [message, swap(message, 1 << r)]
            )
        message_far = swap(message, 1 << rounds)
    sums = call(
        functools.partial(sums_kernel, scale2), "global_sums", ((8, LANES), f32), [message, message_far, weights]
    )
    sums_far = move(sums, outward) if chips == 4 else sums

    near_acc, near_stat = call(
        functools.partial(near_kernel, scale2),
        "near_attention",
        [((half_heads, n_pairs, head_size, LANES), f32), ((half_heads, 2, n_pairs, LANES), f32)],
        [q_t, k_all, v_t, edge_a, edge_b],
        [((n_pairs, 4 * BLK, LANES), f32), ((n_pairs, 4 * BLK, LANES), bf16), ((2, 2 * BLK, half), bf16)],
        micros=4.0,
    )
    window = call(
        functools.partial(far_kernel, scale2),
        "far_attention",
        ((2, n_pairs, LANES), f32),
        [q_t, near_acc, near_stat, kv_near, kv_far, weights, row_positions],
        [
            ((n_pairs, glob, LANES), f32),
            ((n_pairs, glob, LANES), bf16),
            ((n_pairs, glob, LANES), f32),
            ((half_heads, LANES, LANES), f32),
        ],
        micros=2.0,
    )
    share = ((2, n_pairs // CORES, LANES), f32)
    mine, theirs = call(
        place_kernel, "place_global", [share, share], [sums, sums_far, row_positions, window]
    )
    theirs = swap(theirs, 1)
    lin = mine[0] + theirs[0]
    sq = mine[1] + theirs[1]
    return (lin * lax.rsqrt(sq * (1.0 / model_width) + 1e-06)).reshape(rows)


def solution(mesh):
    placed = (
        P(("doc", "seq"), None),
        P(("doc", "seq"), None),
        P(("doc", "seq"), None),
        P("doc"),
        P(),
    )
    return jax.shard_map(
        on_device, mesh=mesh, in_specs=placed, out_specs=P(("doc", "seq")), check_vma=False
    )
```

```python
import functools
import math

import jax
import jax.numpy as jnp
from jax import lax
from jax.experimental import pallas as pl
from jax.experimental.pallas import tpu as pltpu
from jax.sharding import PartitionSpec as P

HEADS = 16
BLK = 64
CORES = 2
LANES = 128
NEG = -1e30
LOG2E = math.log2(math.e)
STAT_ROWS = 16


def pieces(x):
    hi = x.astype(jnp.bfloat16)
    rest = x - hi.astype(jnp.float32)
    mid = rest.astype(jnp.bfloat16)
    low = (rest - mid.astype(jnp.float32)).astype(jnp.bfloat16)
    return hi, mid, low


def dot_t(a, b):
    return lax.dot_general(a, b, (((1,), (1,)), ((), ())), preferred_element_type=jnp.float32)


def dot_n(a, b):
    return lax.dot_general(a, b, (((1,), (0,)), ((), ())), preferred_element_type=jnp.float32)


def put_message(out_ref, pair, out, peak, total):
    rows = out.shape[0]
    out_ref[pair, :rows, :] = out.astype(jnp.bfloat16)
    stats = [p.astype(jnp.float32) for p in (*pieces(peak), *pieces(total))]
    row = lax.broadcasted_iota(jnp.int32, (STAT_ROWS, LANES), 0)
    block = jnp.zeros((STAT_ROWS, LANES), jnp.float32)
    for i, stat in enumerate(stats):
        block = jnp.where(row == i, jnp.broadcast_to(stat, block.shape), block)
    out_ref[pair, rows:, :] = block.astype(jnp.bfloat16)


def get_message(ref, pair, head_size):
    out = ref[pair, :head_size, :].astype(jnp.float32)
    stats = ref[pair, head_size:, :].astype(jnp.float32)
    peak = stats[0:1] + stats[1:2] + stats[2:3]
    total = stats[3:4] + stats[4:5] + stats[5:6]
    return out, peak, total


def merged(a, b, scale2):
    out_a, peak_a, total_a = a
    out_b, peak_b, total_b = b
    peak = jnp.maximum(peak_a, peak_b)
    weight_a = jnp.exp2((peak_a - peak) * scale2) * total_a
    weight_b = jnp.exp2((peak_b - peak) * scale2) * total_b
    total = weight_a + weight_b
    inv = 1.0 / total
    return out_a * (weight_a * inv) + out_b * (weight_b * inv), peak, total


def device_place():
    index = lax.axis_index("seq")
    return index % CORES, index // CORES


def column_of(row):
    wide = jnp.concatenate([row, row], axis=1).astype(jnp.float32)
    return jnp.transpose(jnp.broadcast_to(wide, (LANES, LANES)))[: row.shape[1]]


def pick(x_ref, hit, out_ref, at, cols):
    contract = (((0,), (0,)), ((), ()))
    picked = lax.dot_general(hit, x_ref[:, cols], contract, preferred_element_type=jnp.float32)
    out_ref[at : at + hit.shape[1], :] = picked.astype(jnp.bfloat16)


def own_positions(pos_ref, rows):
    core, chip = device_place()
    row = (chip * CORES + core) * rows + lax.broadcasted_iota(jnp.int32, (rows, pos_ref.shape[1]), 0)
    return jnp.where(row == pos_ref[...], 1.0, 0.0).astype(jnp.bfloat16)


def select_q_kernel(half, pos_hbm, q_hbm, own_ref, sib_ref, pos_ref, q_ref, sems):
    core, _ = device_place()
    copies = [pltpu.make_async_copy(pos_hbm, pos_ref, sems.at[2])]
    for slot, which in ((0, 1 - core), (1, core)):
        cols = pl.ds(pl.multiple_of(which * half, half), half)
        copies.append(pltpu.make_async_copy(q_hbm.at[:, cols], q_ref.at[slot], sems.at[slot]))
    for copy in copies:
        copy.start()
    copies[0].wait()
    hit = own_positions(pos_ref, q_ref.shape[1])
    for slot, out_ref in ((0, sib_ref), (1, own_ref)):
        copies[1 + slot].wait()
        pick(q_ref.at[slot], hit, out_ref, 0, slice(None))


def select_kv_kernel(half, pos_ref, k_ref, v_ref, q_ref, own_ref, edge_ref, sib_ref, bulk_ref):
    rows = k_ref.shape[0]
    glob = pos_ref.shape[1]
    hit = own_positions(pos_ref, rows)
    core, _ = device_place()
    block = pl.ds(pl.multiple_of(core * (rows - BLK), BLK), BLK)
    mine = pl.ds(pl.multiple_of(core * half, half), half)
    theirs = pl.ds(pl.multiple_of((1 - core) * half, half), half)
    for i, x_ref in enumerate((k_ref, v_ref)):
        pick(x_ref, hit, sib_ref, i * glob, theirs)
        sib_ref[2 * glob + i * BLK : 2 * glob + (i + 1) * BLK, :] = x_ref[block, theirs]
        bulk_ref[i * rows : (i + 1) * rows, :] = x_ref[:, theirs]
        pick(x_ref, hit, own_ref, i * glob, mine)
        edge_ref[i * BLK : (i + 1) * BLK, :] = x_ref[block, mine]
    bulk_ref[2 * rows :, :] = q_ref[:, theirs]


def split_kernel(a_ref, b_ref, sum_ref, rest_ref):
    count = sum_ref.shape[0]
    sum_ref[...] = a_ref[...] + b_ref[:count, :]
    rest_ref[...] = b_ref[count:, :]


def add_kernel(a_ref, b_ref, out_ref):
    out_ref[...] = a_ref[...] + b_ref[...]


def on_line():
    return lax.axis_size("seq") // CORES == 4


def is_inner(chip):
    return (chip == 1) | (chip == 2)


def prepare_kernel(q_own_ref, k_own_ref, v_own_ref, sib_ref, k_ref, v_t_ref, q_t_ref, v_all):
    rows = k_own_ref.shape[0]
    half = k_ref.shape[1]
    core, _ = device_place()
    cols = pl.ds(pl.multiple_of(core * half, half), half)
    own = pl.multiple_of(core * rows, BLK)
    sib = pl.multiple_of((1 - core) * rows, BLK)
    zero = jnp.zeros((BLK, half), jnp.bfloat16)
    for i, (ref, own_ref) in enumerate(((k_ref, k_own_ref), (v_all, v_own_ref))):
        ref[:BLK, :] = zero
        ref[BLK + CORES * rows :, :] = zero
        ref[pl.ds(pl.multiple_of(own + BLK, BLK), rows), :] = own_ref[:, cols]
        ref[pl.ds(pl.multiple_of(sib + BLK, BLK), rows), :] = sib_ref[i * rows : (i + 1) * rows, :]

    def turn(head, carry):
        lanes = pl.ds(pl.multiple_of(head * LANES, LANES), LANES)
        v_t_ref[lanes, :] = jnp.transpose(v_all[:, lanes])
        source = pl.ds(pl.multiple_of(core * half + head * LANES, LANES), LANES)
        q_t_ref[lanes, pl.ds(pl.multiple_of(own, LANES), rows)] = jnp.transpose(q_own_ref[:, source])
        q_t_ref[lanes, pl.ds(pl.multiple_of(sib, LANES), rows)] = jnp.transpose(sib_ref[2 * rows :, lanes])
        return carry

    lax.fori_loop(0, half // LANES, turn, 0)


def global_kernel(scale2, q_a_ref, q_b_ref, k_ref, v_t_ref, out_ref, s_buf, e_buf):
    glob, half = q_a_ref.shape
    head_size = LANES
    pairs = half // (2 * head_size)
    tokens = k_ref.shape[0] - 2 * BLK
    row = lax.broadcasted_iota(jnp.int32, (2 * glob, 2 * head_size), 0)
    col = lax.broadcasted_iota(jnp.int32, (2 * glob, 2 * head_size), 1)
    keep = (row < glob) == (col < head_size)
    lane = lax.broadcasted_iota(jnp.int32, (head_size, LANES), 1)
    for pair in range(pairs):
        cols = slice(2 * pair * head_size, 2 * (pair + 1) * head_size)
        q = q_a_ref[:, cols] + q_b_ref[:, cols]
        doubled = jnp.concatenate([q, q], axis=0)
        diag = jnp.where(keep, doubled, jnp.zeros_like(doubled))
        s_buf[pair] = dot_t(k_ref[BLK : BLK + tokens, cols], diag)
    stats = []
    for pair in range(pairs):
        s = s_buf[pair]
        peak = jnp.max(s, axis=0, keepdims=True)
        e = jnp.exp2((s - peak) * scale2)
        stats.append((peak, jnp.sum(e, axis=0, keepdims=True)))
        zero = jnp.zeros((BLK, LANES), jnp.bfloat16)
        e_buf[pair, :BLK] = zero
        e_buf[pair, BLK + tokens :] = zero
        e_buf[pair, BLK : BLK + tokens] = e.astype(jnp.bfloat16)
    for pair in range(pairs):
        rows = slice(2 * pair * head_size, 2 * (pair + 1) * head_size)
        acc = dot_n(v_t_ref[rows, :], e_buf[pair])
        peak, total = stats[pair]
        out = jnp.where(lane < glob, acc[:head_size], acc[head_size:]) / total
        put_message(out_ref, pair, out, peak, total)


def merge_kernel(scale2, a_ref, b_ref, out_ref):
    head_size = a_ref.shape[1] - STAT_ROWS
    for pair in range(a_ref.shape[0]):
        a = get_message(a_ref, pair, head_size)
        b = get_message(b_ref, pair, head_size)
        put_message(out_ref, pair, *merged(a, b, scale2))


def inward_kernel(scale2, a_ref, b_ref, out_ref):
    _, chip = device_place()

    @pl.when(is_inner(chip))
    def _():
        merge_kernel(scale2, a_ref, b_ref, out_ref)

    @pl.when(jnp.logical_not(is_inner(chip)))
    def _():
        out_ref[...] = a_ref[...]


def sums_kernel(scale2, a_ref, b_ref, w_ref, out_ref):
    pairs = a_ref.shape[0]
    head_size = a_ref.shape[1] - STAT_ROWS
    glob = LANES // 2
    core, chip = device_place()
    upper = lax.broadcasted_iota(jnp.int32, (LANES, head_size), 0) < glob
    lin = jnp.zeros((1, LANES), jnp.float32)
    sq = jnp.zeros((1, LANES), jnp.float32)
    for pair in range(pairs):
        a = get_message(a_ref, pair, head_size)
        b = get_message(b_ref, pair, head_size)
        if on_line():
            b = tuple(jnp.where(is_inner(chip), y, x) for x, y in zip(a, b))
        out, _, _ = merged(a, b, scale2)
        w_a = w_ref[pl.ds(core * 2 * pairs + 2 * pair, 1), :]
        w_b = w_ref[pl.ds(core * 2 * pairs + 2 * pair + 1, 1), :]
        w = jnp.transpose(jnp.where(upper, w_a, w_b))
        lin = lin + jnp.sum(out * w, axis=0, keepdims=True)
        sq = sq + jnp.sum(out * out, axis=0, keepdims=True)
    out_ref[...] = jnp.zeros_like(out_ref)
    out_ref[0:1, :] = lin + pltpu.roll(lin, glob, 1)
    out_ref[1:2, :] = sq + pltpu.roll(sq, glob, 1)


def place_kernel(own_sums_ref, far_sums_ref, pos_ref, win_ref, own_ref, sib_ref):
    glob = pos_ref.shape[1]
    core, chip = device_place()
    sums = own_sums_ref[...]
    if on_line():
        sums = jnp.where(is_inner(chip), sums, far_sums_ref[...])
    parts = [p.astype(jnp.float32) for p in (*pieces(sums[0:1]), *pieces(sums[1:2]))] + [jnp.ones((1, LANES), jnp.float32)]
    row = lax.broadcasted_iota(jnp.int32, (16, LANES), 0)
    table = jnp.zeros((16, LANES), jnp.float32)
    for i, part in enumerate(parts):
        table = jnp.where(row == i, jnp.broadcast_to(part, table.shape), table)
    table = table.astype(jnp.bfloat16)[:, :glob]
    pos = column_of(pos_ref[...])
    n_pairs = win_ref.shape[1]
    each = n_pairs // CORES
    for out_ref, which in ((sib_ref, 1 - core), (own_ref, core)):
        for j in range(each):
            pair = which * each + j
            token = (chip * n_pairs + pair) * LANES + lax.broadcasted_iota(jnp.int32, (glob, LANES), 1)
            hit = jnp.where(pos == token.astype(jnp.float32), 1.0, 0.0).astype(jnp.bfloat16)
            placed = dot_n(table, hit)
            is_glob = placed[6:7] > 0.5
            for i in (0, 1):
                value = placed[3 * i : 3 * i + 1] + placed[3 * i + 1 : 3 * i + 2] + placed[3 * i + 2 : 3 * i + 3]
                out_ref[i, j : j + 1, :] = jnp.where(is_glob, value, win_ref[i, pl.ds(pair, 1), :])


def near_kernel(scale2, q_t_ref, k_ref, v_t_ref, edge_a_ref, edge_b_ref, acc_ref, stat_ref, s_buf, e_buf, edges):
    half, tokens = q_t_ref.shape
    n_pairs = tokens // LANES
    core, chip = device_place()
    chips = lax.axis_size("seq") // CORES
    left = lax.broadcasted_iota(jnp.int32, (BLK, LANES), 1) < BLK
    wide_left = lax.broadcasted_iota(jnp.int32, (LANES, LANES), 1) < BLK
    first_bias = jnp.where(left & (chip == 0), NEG, 0.0)
    last_bias = jnp.where((~left) & (chip == chips - 1), NEG, 0.0)

    @pl.when(core == 1)
    def _():
        edges[0] = edge_a_ref[...]
        edges[1] = edge_b_ref[...]

    @pl.when(core == 0)
    def _():
        edges[0] = edge_b_ref[...]
        edges[1] = edge_a_ref[...]

    def one_head(head, carry):
        cols = pl.ds(pl.multiple_of(head * LANES, LANES), LANES)
        for j in range(n_pairs):
            if j == 0:
                k = jnp.concatenate([edges[0, :BLK, cols], k_ref[BLK : 4 * BLK, cols]], axis=0)
            elif j == n_pairs - 1:
                k = jnp.concatenate([k_ref[j * LANES : j * LANES + 3 * BLK, cols], edges[1, :BLK, cols]], axis=0)
            else:
                k = k_ref[j * LANES : (j + 2) * LANES, cols]
            s_buf[j] = dot_n(k, q_t_ref[cols, j * LANES : (j + 1) * LANES])
        peaks, totals = [], []
        for j in range(n_pairs):
            ends = jnp.where(left, s_buf[j, :BLK], s_buf[j, 3 * BLK :])
            if j == 0:
                ends = ends + first_bias
            if j == n_pairs - 1:
                ends = ends + last_bias
            mid = s_buf[j, BLK : 3 * BLK]
            peak = jnp.max(jnp.maximum(ends, jnp.maximum(mid[:BLK], mid[BLK:])), axis=0, keepdims=True)
            e_ends = jnp.exp2((ends - peak) * scale2)
            e_mid = jnp.exp2((mid - peak) * scale2)
            zero = jnp.zeros_like(e_ends)
            e_buf[j, :BLK] = jnp.where(left, e_ends, zero).astype(jnp.bfloat16)
            e_buf[j, BLK : 3 * BLK] = e_mid.astype(jnp.bfloat16)
            e_buf[j, 3 * BLK :] = jnp.where(left, zero, e_ends).astype(jnp.bfloat16)
            peaks.append(peak)
            totals.append(jnp.sum(e_ends + e_mid[:BLK] + e_mid[BLK:], axis=0, keepdims=True))
        stat_ref[head, 0] = jnp.concatenate(peaks, axis=0)
        stat_ref[head, 1] = jnp.concatenate(totals, axis=0)
        turned = jnp.transpose(jnp.concatenate([edges[0, BLK:, cols], edges[1, BLK:, cols]], axis=0))
        for j in range(n_pairs):
            v_0 = v_t_ref[cols, j * LANES : (j + 1) * LANES]
            v_1 = v_t_ref[cols, (j + 1) * LANES : (j + 2) * LANES]
            if j == 0:
                v_0 = jnp.where(wide_left, turned, v_0)
            if j == n_pairs - 1:
                v_1 = jnp.where(wide_left, v_1, turned)
            acc_ref[head, j] = dot_n(jnp.concatenate([v_0, v_1], axis=1), e_buf[j])
        return carry

    lax.fori_loop(0, half // LANES, one_head, 0)


def far_kernel(
    scale2, q_t_ref, acc_ref, stat_ref, kv_a_ref, kv_b_ref, w_ref, pos_ref, out_ref, s_buf, e_buf, bias, w_cols
):
    half, tokens = q_t_ref.shape
    glob = pos_ref.shape[1]
    heads = half // LANES
    n_pairs = tokens // LANES
    core, chip = device_place()
    glob_block = column_of(pos_ref[...] // BLK)
    for j in range(n_pairs):
        block = (chip * n_pairs + j) * (LANES // BLK) + lax.broadcasted_iota(jnp.int32, (glob, LANES), 1) // BLK
        bias[j] = jnp.where(jnp.abs(glob_block - block.astype(jnp.float32)) > 1.5, 0.0, NEG)
    for head in range(heads):
        row = w_ref[pl.ds(core * heads + head, 1), :]
        w_cols[head] = jnp.transpose(jnp.broadcast_to(row, (LANES, LANES)))

    def one_head(head, carry):
        cols = pl.ds(pl.multiple_of(head * LANES, LANES), LANES)
        kv_a = kv_a_ref[:, cols]
        if on_line():
            kv_a = jnp.where(is_inner(chip), kv_a, jnp.zeros_like(kv_a))
        kv = kv_a + kv_b_ref[:, cols]
        kg = kv[:glob]
        for j in range(n_pairs):
            s_buf[j] = dot_n(kg, q_t_ref[cols, j * LANES : (j + 1) * LANES])
        near_peaks = stat_ref[head, 0]
        near_totals = stat_ref[head, 1]
        near_weights, inverses = [], []
        for j in range(n_pairs):
            far = s_buf[j] + bias[j]
            near_peak = near_peaks[j : j + 1]
            peak = jnp.maximum(jnp.max(far, axis=0, keepdims=True), near_peak)
            e_far = jnp.exp2((far - peak) * scale2)
            e_buf[j] = e_far.astype(jnp.bfloat16)
            near_weight = jnp.exp2((near_peak - peak) * scale2)
            total = near_totals[j : j + 1] * near_weight + jnp.sum(e_far, axis=0, keepdims=True)
            near_weights.append(near_weight)
            inverses.append(1.0 / total)
        vg_t = jnp.transpose(kv[glob:])
        w = w_cols[head]
        lins, sqs = [], []
        for j in range(n_pairs):
            acc = acc_ref[head, j] * near_weights[j] + dot_n(vg_t, e_buf[j])
            lins.append(jnp.sum(acc * w, axis=0, keepdims=True) * inverses[j])
            sqs.append(jnp.sum(acc * acc, axis=0, keepdims=True) * (inverses[j] * inverses[j]))
        lin, sq = carry
        return lin + jnp.concatenate(lins, axis=0), sq + jnp.concatenate(sqs, axis=0)

    none = jnp.zeros((n_pairs, LANES), jnp.float32)
    lin, sq = lax.fori_loop(0, heads, one_head, (none, none))
    out_ref[0] = lin
    out_ref[1] = sq


def call(kernel, name, outs, args, scratch=(), micros=0.0, from_hbm=False):
    spec = pl.BlockSpec(memory_space=pltpu.VMEM)
    source = pltpu.HBM if from_hbm else pltpu.VMEM
    single = not isinstance(outs, list)
    shapes = [outs] if single else outs
    result = pl.pallas_call(
        kernel,
        in_specs=[pl.BlockSpec(memory_space=source)] * len(args),
        out_specs=[spec] * len(shapes),
        out_shape=[pltpu.VMEM(shape, dtype) for shape, dtype in shapes],
        scratch_shapes=[pltpu.VMEM(*x) if isinstance(x, tuple) else x for x in scratch],
        compiler_params=pltpu.CompilerParams(vmem_limit_bytes=16 * 1024 * 1024),
        cost_estimate=pl.CostEstimate(flops=int(micros * 1e9) + 1, transcendentals=0, bytes_accessed=1),
        name=name,
    )(*[pltpu.with_memory_space_constraint(x, source) for x in args])
    return result[0] if single else result


def on_device(queries, keys, values, global_positions, score_weight):
    rows, model_width = queries.shape
    head_size = model_width // HEADS
    half = model_width // CORES
    half_heads = HEADS // CORES
    glob = global_positions.shape[0]
    seq_count = lax.axis_size("seq")
    chips = seq_count // CORES
    scale2 = head_size ** (-0.5) * LOG2E
    bf16 = jnp.bfloat16
    f32 = jnp.float32
    rounds = int(math.log2(chips))
    tokens = CORES * rows
    n_pairs = tokens // LANES

    def swap(x, mask):
        return lax.ppermute(x, "seq", [(i, i ^ mask) for i in range(seq_count)])

    def shift(x, even, odd):
        moves = [(i, i + (odd if i % CORES else even) * CORES) for i in range(seq_count)]
        return lax.ppermute(x, "seq", [(i, to) for i, to in moves if 0 <= to < seq_count])

    def move(x, pairs):
        return lax.ppermute(x, "seq", [(a * CORES + c, b * CORES + c) for a, b in pairs for c in range(CORES)])

    inward = ((0, 1), (3, 2))
    across = ((1, 2), (2, 1))
    outward = ((1, 0), (2, 3))

    def after(arrays, *others):
        return lax.optimization_barrier((*arrays, *others))[: len(arrays)]

    row_positions = global_positions.reshape(1, glob)
    small = ((glob, half), bf16)
    pair_of = ((2 * glob, half), bf16)
    edge = ((2 * BLK, half), bf16)
    q_own, q_sib = call(
        functools.partial(select_q_kernel, half),
        "select_queries",
        [small, small],
        [row_positions, queries],
        [((1, glob), jnp.int32), ((CORES, rows, half), bf16), pltpu.SemaphoreType.DMA((3,))],
        from_hbm=True,
    )
    q_near = call(add_kernel, "add_queries", small, [q_own, swap(q_sib, 1)])
    later_positions = after((row_positions,), q_near)[0]
    kv_own, edge_own, kv_sib, bulk_sib = call(
        functools.partial(select_kv_kernel, half),
        "select_keys_values",
        [pair_of, edge, ((2 * glob + 2 * BLK, half), bf16), ((3 * rows, half), bf16)],
        [later_positions, keys, values, queries],
    )
    kv_near, edge_recv = call(split_kernel, "join_keys_values", [pair_of, edge], [kv_own, swap(kv_sib, 1)])
    bulk_sib = after((bulk_sib,), kv_near)[0]
    bulk_recv = swap(bulk_sib, 1)
    for r in range(1, rounds):
        q_near = call(add_kernel, "add_queries", small, [q_near, swap(q_near, 1 << r)])
    kv_near = after((kv_near,), q_near)[0]
    q_far = swap(q_near, 1 << rounds)

    edge_own, edge_recv = after((edge_own, edge_recv), q_near)
    edge_a = shift(edge_own, -1, 1)
    edge_b = shift(edge_recv, 1, -1)
    if chips == 4:
        kv_near = call(add_kernel, "add_keys_values", pair_of, [kv_near, move(kv_near, inward)])
        kv_near = call(add_kernel, "add_keys_values", pair_of, [kv_near, move(kv_near, across)])
        kv_far = move(kv_near, outward)
    else:
        for r in range(1, rounds):
            kv_near = call(add_kernel, "add_keys_values", pair_of, [kv_near, swap(kv_near, 1 << r)])
        kv_far = swap(kv_near, 1 << rounds)

    k_all, v_t, q_t = call(
        prepare_kernel,
        "prepare",
        [((tokens + 2 * BLK, half), bf16), ((half, tokens + 2 * BLK), bf16), ((half, tokens), bf16)],
        [queries, keys, values, bulk_recv],
        [((tokens + 2 * BLK, half), bf16)],
        micros=1.6,
    )
    part = ((half_heads // 2, head_size + STAT_ROWS, LANES), bf16)
    message = call(
        functools.partial(global_kernel, scale2),
        "global_partial",
        part,
        [q_near, q_far, k_all, v_t],
        [((half_heads // 2, tokens, LANES), f32), ((half_heads // 2, tokens + 2 * BLK, LANES), bf16)],
    )
    weights = score_weight.reshape(HEADS, head_size)
    if chips == 4:
        message = call(
            functools.partial(inward_kernel, scale2), "merge_partial", part, [message, move(message, inward)]
        )
        message_far = move(message, across)
    else:
        for r in range(1, rounds):
            message = call(
                functools.partial(merge_kernel, scale2), "merge_partial", part, [message, swap(message, 1 << r)]
            )
        message_far = swap(message, 1 << rounds)
    sums = call(
        functools.partial(sums_kernel, scale2), "global_sums", ((8, LANES), f32), [message, message_far, weights]
    )
    sums_far = move(sums, outward) if chips == 4 else sums

    near_acc, near_stat = call(
        functools.partial(near_kernel, scale2),
        "near_attention",
        [((half_heads, n_pairs, head_size, LANES), f32), ((half_heads, 2, n_pairs, LANES), f32)],
        [q_t, k_all, v_t, edge_a, edge_b],
        [((n_pairs, 4 * BLK, LANES), f32), ((n_pairs, 4 * BLK, LANES), bf16), ((2, 2 * BLK, half), bf16)],
        micros=4.0,
    )
    window = call(
        functools.partial(far_kernel, scale2),
        "far_attention",
        ((2, n_pairs, LANES), f32),
        [q_t, near_acc, near_stat, kv_near, kv_far, weights, row_positions],
        [
            ((n_pairs, glob, LANES), f32),
            ((n_pairs, glob, LANES), bf16),
            ((n_pairs, glob, LANES), f32),
            ((half_heads, LANES, LANES), f32),
        ],
        micros=2.0,
    )
    share = ((2, n_pairs // CORES, LANES), f32)
    mine, theirs = call(
        place_kernel, "place_global", [share, share], [sums, sums_far, row_positions, window]
    )
    theirs = swap(theirs, 1)
    lin = mine[0] + theirs[0]
    sq = mine[1] + theirs[1]
    return (lin * lax.rsqrt(sq * (1.0 / model_width) + 1e-06)).reshape(rows)


def solution(mesh):
    placed = (
        P(("doc", "seq"), None),
        P(("doc", "seq"), None),
        P(("doc", "seq"), None),
        P("doc"),
        P(),
    )
    return jax.shard_map(
        on_device, mesh=mesh, in_specs=placed, out_specs=P(("doc", "seq")), check_vma=False
    )
```

```python
import functools
import math

import jax
import jax.numpy as jnp
from jax import lax
from jax.experimental import pallas as pl
from jax.experimental.pallas import tpu as pltpu
from jax.sharding import PartitionSpec as P

HEADS = 16
BLK = 64
CORES = 2
LANES = 128
NEG = -1e30
LOG2E = math.log2(math.e)
STAT_ROWS = 16


def pieces(x):
    hi = x.astype(jnp.bfloat16)
    rest = x - hi.astype(jnp.float32)
    mid = rest.astype(jnp.bfloat16)
    low = (rest - mid.astype(jnp.float32)).astype(jnp.bfloat16)
    return hi, mid, low


def dot_t(a, b):
    return lax.dot_general(a, b, (((1,), (1,)), ((), ())), preferred_element_type=jnp.float32)


def dot_n(a, b):
    return lax.dot_general(a, b, (((1,), (0,)), ((), ())), preferred_element_type=jnp.float32)


def put_message(out_ref, pair, out, peak, total):
    rows = out.shape[0]
    out_ref[pair, :rows, :] = out.astype(jnp.bfloat16)
    stats = [p.astype(jnp.float32) for p in (*pieces(peak), *pieces(total))]
    row = lax.broadcasted_iota(jnp.int32, (STAT_ROWS, LANES), 0)
    block = jnp.zeros((STAT_ROWS, LANES), jnp.float32)
    for i, stat in enumerate(stats):
        block = jnp.where(row == i, jnp.broadcast_to(stat, block.shape), block)
    out_ref[pair, rows:, :] = block.astype(jnp.bfloat16)


def get_message(ref, pair, head_size):
    out = ref[pair, :head_size, :].astype(jnp.float32)
    stats = ref[pair, head_size:, :].astype(jnp.float32)
    peak = stats[0:1] + stats[1:2] + stats[2:3]
    total = stats[3:4] + stats[4:5] + stats[5:6]
    return out, peak, total


def merged(a, b, scale2):
    out_a, peak_a, total_a = a
    out_b, peak_b, total_b = b
    peak = jnp.maximum(peak_a, peak_b)
    weight_a = jnp.exp2((peak_a - peak) * scale2) * total_a
    weight_b = jnp.exp2((peak_b - peak) * scale2) * total_b
    total = weight_a + weight_b
    inv = 1.0 / total
    return out_a * (weight_a * inv) + out_b * (weight_b * inv), peak, total


def device_place():
    index = lax.axis_index("seq")
    return index % CORES, index // CORES


def column_of(row):
    wide = jnp.concatenate([row, row], axis=1).astype(jnp.float32)
    return jnp.transpose(jnp.broadcast_to(wide, (LANES, LANES)))[: row.shape[1]]


def own_positions(pos_ref, rows):
    core, chip = device_place()
    row = (chip * CORES + core) * rows + lax.broadcasted_iota(jnp.int32, (rows, pos_ref.shape[1]), 0)
    return jnp.where(row == pos_ref[...], 1.0, 0.0).astype(jnp.bfloat16)


def select_kernel(half, pos_hbm, q_hbm, k_hbm, v_hbm, sel_ref, sib_ref, edge_ref, mine_ref, bulk_ref, pos_ref, sems):
    rows = q_hbm.shape[0]
    core, _ = device_place()
    block = pl.ds(pl.multiple_of(core * (rows - BLK), BLK), BLK)
    pos_copy = pltpu.make_async_copy(pos_hbm, pos_ref, sems.at[0])
    copies = []
    for i, x_hbm in enumerate((q_hbm, k_hbm, v_hbm)):
        for to_ref, which in ((bulk_ref, 1 - core), (mine_ref, core)):
            cols = pl.ds(pl.multiple_of(which * half, half), half)
            to = to_ref.at[i * rows : (i + 1) * rows, :]
            copies.append(pltpu.make_async_copy(x_hbm.at[:, cols], to, sems.at[1 + len(copies)]))
    edges = [
        pltpu.make_async_copy(x_hbm.at[block, :], edge_ref.at[i * BLK : (i + 1) * BLK, :], sems.at[7 + i])
        for i, x_hbm in enumerate((k_hbm, v_hbm))
    ]
    for copy in (pos_copy, *copies, *edges):
        copy.start()
    pos_copy.wait()
    hit = own_positions(pos_ref, rows)
    glob = hit.shape[1]
    contract = (((0,), (0,)), ((), ()))
    for i in range(3):
        for copy, x_ref, out_ref in ((copies[2 * i], bulk_ref, sib_ref), (copies[2 * i + 1], mine_ref, sel_ref)):
            copy.wait()
            x = x_ref[i * rows : (i + 1) * rows, :]
            picked = lax.dot_general(hit, x, contract, preferred_element_type=jnp.float32)
            out_ref[i * glob : (i + 1) * glob, :] = picked.astype(jnp.bfloat16)
    for copy in edges:
        copy.wait()


def join_kernel(own_ref, recv_ref, q_ref, kv_ref):
    count = q_ref.shape[0]
    q_ref[...] = own_ref[:count, :] + recv_ref[:count, :]
    kv_ref[...] = own_ref[count:, :] + recv_ref[count:, :]


def edge_kernel(full_ref, out_ref):
    half = out_ref.shape[1]
    core, _ = device_place()
    out_ref[...] = full_ref[:, pl.ds(pl.multiple_of((1 - core) * half, half), half)]


def add_kernel(a_ref, b_ref, out_ref):
    out_ref[...] = a_ref[...] + b_ref[...]


def on_line():
    return lax.axis_size("seq") // CORES == 4


def is_inner(chip):
    return (chip == 1) | (chip == 2)


def prepare_kernel(own_ref, sib_ref, k_ref, v_t_ref, q_t_ref, v_all):
    rows = own_ref.shape[0] // 3
    half = k_ref.shape[1]
    core, _ = device_place()
    zero = jnp.zeros((BLK, half), jnp.bfloat16)
    for ref in (k_ref, v_all):
        ref[:BLK, :] = zero
        ref[BLK + CORES * rows :, :] = zero
    for part_ref, which in ((own_ref, core), (sib_ref, 1 - core)):
        at = pl.ds(pl.multiple_of(which * rows + BLK, BLK), rows)
        k_ref[at, :] = part_ref[rows : 2 * rows, :]
        v_all[at, :] = part_ref[2 * rows :, :]

    def turn(head, carry):
        lanes = pl.ds(pl.multiple_of(head * LANES, LANES), LANES)
        v_t_ref[lanes, :] = jnp.transpose(v_all[:, lanes])
        for part_ref, which in ((own_ref, core), (sib_ref, 1 - core)):
            q_t_ref[lanes, pl.ds(pl.multiple_of(which * rows, LANES), rows)] = jnp.transpose(part_ref[:rows, lanes])
        return carry

    lax.fori_loop(0, half // LANES, turn, 0)


def global_kernel(scale2, q_a_ref, q_b_ref, k_ref, v_t_ref, out_ref, s_buf, e_buf):
    glob, half = q_a_ref.shape
    head_size = LANES
    pairs = half // (2 * head_size)
    tokens = k_ref.shape[0] - 2 * BLK
    row = lax.broadcasted_iota(jnp.int32, (2 * glob, 2 * head_size), 0)
    col = lax.broadcasted_iota(jnp.int32, (2 * glob, 2 * head_size), 1)
    keep = (row < glob) == (col < head_size)
    lane = lax.broadcasted_iota(jnp.int32, (head_size, LANES), 1)
    for pair in range(pairs):
        cols = slice(2 * pair * head_size, 2 * (pair + 1) * head_size)
        q = q_a_ref[:, cols] + q_b_ref[:, cols]
        doubled = jnp.concatenate([q, q], axis=0)
        diag = jnp.where(keep, doubled, jnp.zeros_like(doubled))
        s_buf[pair] = dot_t(k_ref[BLK : BLK + tokens, cols], diag)
    stats = []
    for pair in range(pairs):
        s = s_buf[pair]
        peak = jnp.max(s, axis=0, keepdims=True)
        e = jnp.exp2((s - peak) * scale2)
        stats.append((peak, jnp.sum(e, axis=0, keepdims=True)))
        zero = jnp.zeros((BLK, LANES), jnp.bfloat16)
        e_buf[pair, :BLK] = zero
        e_buf[pair, BLK + tokens :] = zero
        e_buf[pair, BLK : BLK + tokens] = e.astype(jnp.bfloat16)
    for pair in range(pairs):
        rows = slice(2 * pair * head_size, 2 * (pair + 1) * head_size)
        acc = dot_n(v_t_ref[rows, :], e_buf[pair])
        peak, total = stats[pair]
        out = jnp.where(lane < glob, acc[:head_size], acc[head_size:]) / total
        put_message(out_ref, pair, out, peak, total)


def merge_kernel(scale2, a_ref, b_ref, out_ref):
    head_size = a_ref.shape[1] - STAT_ROWS
    for pair in range(a_ref.shape[0]):
        a = get_message(a_ref, pair, head_size)
        b = get_message(b_ref, pair, head_size)
        put_message(out_ref, pair, *merged(a, b, scale2))


def inward_kernel(scale2, a_ref, b_ref, out_ref):
    _, chip = device_place()

    @pl.when(is_inner(chip))
    def _():
        merge_kernel(scale2, a_ref, b_ref, out_ref)

    @pl.when(jnp.logical_not(is_inner(chip)))
    def _():
        out_ref[...] = a_ref[...]


def sums_kernel(scale2, a_ref, b_ref, w_ref, out_ref):
    pairs = a_ref.shape[0]
    head_size = a_ref.shape[1] - STAT_ROWS
    glob = LANES // 2
    core, chip = device_place()
    upper = lax.broadcasted_iota(jnp.int32, (LANES, head_size), 0) < glob
    lin = jnp.zeros((1, LANES), jnp.float32)
    sq = jnp.zeros((1, LANES), jnp.float32)
    for pair in range(pairs):
        a = get_message(a_ref, pair, head_size)
        b = get_message(b_ref, pair, head_size)
        if on_line():
            b = tuple(jnp.where(is_inner(chip), y, x) for x, y in zip(a, b))
        out, _, _ = merged(a, b, scale2)
        w_a = w_ref[pl.ds(core * 2 * pairs + 2 * pair, 1), :]
        w_b = w_ref[pl.ds(core * 2 * pairs + 2 * pair + 1, 1), :]
        w = jnp.transpose(jnp.where(upper, w_a, w_b))
        lin = lin + jnp.sum(out * w, axis=0, keepdims=True)
        sq = sq + jnp.sum(out * out, axis=0, keepdims=True)
    out_ref[...] = jnp.zeros_like(out_ref)
    out_ref[0:1, :] = lin + pltpu.roll(lin, glob, 1)
    out_ref[1:2, :] = sq + pltpu.roll(sq, glob, 1)


def place_kernel(own_sums_ref, far_sums_ref, pos_ref, win_ref, own_ref, sib_ref):
    glob = pos_ref.shape[1]
    core, chip = device_place()
    sums = own_sums_ref[...]
    if on_line():
        sums = jnp.where(is_inner(chip), sums, far_sums_ref[...])
    parts = [p.astype(jnp.float32) for p in (*pieces(sums[0:1]), *pieces(sums[1:2]))] + [jnp.ones((1, LANES), jnp.float32)]
    row = lax.broadcasted_iota(jnp.int32, (16, LANES), 0)
    table = jnp.zeros((16, LANES), jnp.float32)
    for i, part in enumerate(parts):
        table = jnp.where(row == i, jnp.broadcast_to(part, table.shape), table)
    table = table.astype(jnp.bfloat16)[:, :glob]
    pos = column_of(pos_ref[...])
    n_pairs = win_ref.shape[1]
    each = n_pairs // CORES
    for out_ref, which in ((sib_ref, 1 - core), (own_ref, core)):
        for j in range(each):
            pair = which * each + j
            token = (chip * n_pairs + pair) * LANES + lax.broadcasted_iota(jnp.int32, (glob, LANES), 1)
            hit = jnp.where(pos == token.astype(jnp.float32), 1.0, 0.0).astype(jnp.bfloat16)
            placed = dot_n(table, hit)
            is_glob = placed[6:7] > 0.5
            for i in (0, 1):
                value = placed[3 * i : 3 * i + 1] + placed[3 * i + 1 : 3 * i + 2] + placed[3 * i + 2 : 3 * i + 3]
                out_ref[i, j : j + 1, :] = jnp.where(is_glob, value, win_ref[i, pl.ds(pair, 1), :])


def near_kernel(scale2, q_t_ref, k_ref, v_t_ref, edge_a_ref, edge_b_ref, acc_ref, stat_ref, s_buf, e_buf, edges):
    half, tokens = q_t_ref.shape
    n_pairs = tokens // LANES
    core, chip = device_place()
    chips = lax.axis_size("seq") // CORES
    left = lax.broadcasted_iota(jnp.int32, (BLK, LANES), 1) < BLK
    wide_left = lax.broadcasted_iota(jnp.int32, (LANES, LANES), 1) < BLK
    first_bias = jnp.where(left & (chip == 0), NEG, 0.0)
    last_bias = jnp.where((~left) & (chip == chips - 1), NEG, 0.0)

    mine = pl.ds(pl.multiple_of(core * half, half), half)

    @pl.when(core == 1)
    def _():
        edges[0] = edge_a_ref[:, mine]
        edges[1] = edge_b_ref[...]

    @pl.when(core == 0)
    def _():
        edges[0] = edge_b_ref[...]
        edges[1] = edge_a_ref[:, mine]

    def one_head(head, carry):
        cols = pl.ds(pl.multiple_of(head * LANES, LANES), LANES)
        for j in range(n_pairs):
            if j == 0:
                k = jnp.concatenate([edges[0, :BLK, cols], k_ref[BLK : 4 * BLK, cols]], axis=0)
            elif j == n_pairs - 1:
                k = jnp.concatenate([k_ref[j * LANES : j * LANES + 3 * BLK, cols], edges[1, :BLK, cols]], axis=0)
            else:
                k = k_ref[j * LANES : (j + 2) * LANES, cols]
            s_buf[j] = dot_n(k, q_t_ref[cols, j * LANES : (j + 1) * LANES])
        peaks, totals = [], []
        for j in range(n_pairs):
            ends = jnp.where(left, s_buf[j, :BLK], s_buf[j, 3 * BLK :])
            if j == 0:
                ends = ends + first_bias
            if j == n_pairs - 1:
                ends = ends + last_bias
            mid = s_buf[j, BLK : 3 * BLK]
            peak = jnp.max(jnp.maximum(ends, jnp.maximum(mid[:BLK], mid[BLK:])), axis=0, keepdims=True)
            e_ends = jnp.exp2((ends - peak) * scale2)
            e_mid = jnp.exp2((mid - peak) * scale2)
            zero = jnp.zeros_like(e_ends)
            e_buf[j, :BLK] = jnp.where(left, e_ends, zero).astype(jnp.bfloat16)
            e_buf[j, BLK : 3 * BLK] = e_mid.astype(jnp.bfloat16)
            e_buf[j, 3 * BLK :] = jnp.where(left, zero, e_ends).astype(jnp.bfloat16)
            peaks.append(peak)
            totals.append(jnp.sum(e_ends + e_mid[:BLK] + e_mid[BLK:], axis=0, keepdims=True))
        stat_ref[head, 0] = jnp.concatenate(peaks, axis=0)
        stat_ref[head, 1] = jnp.concatenate(totals, axis=0)
        turned = jnp.transpose(jnp.concatenate([edges[0, BLK:, cols], edges[1, BLK:, cols]], axis=0))
        for j in range(n_pairs):
            v_0 = v_t_ref[cols, j * LANES : (j + 1) * LANES]
            v_1 = v_t_ref[cols, (j + 1) * LANES : (j + 2) * LANES]
            if j == 0:
                v_0 = jnp.where(wide_left, turned, v_0)
            if j == n_pairs - 1:
                v_1 = jnp.where(wide_left, v_1, turned)
            acc_ref[head, j] = dot_n(jnp.concatenate([v_0, v_1], axis=1), e_buf[j])
        return carry

    lax.fori_loop(0, half // LANES, one_head, 0)


def far_kernel(
    scale2, q_t_ref, acc_ref, stat_ref, kv_a_ref, kv_b_ref, w_ref, pos_ref, out_ref, s_buf, e_buf, bias, w_cols
):
    half, tokens = q_t_ref.shape
    glob = pos_ref.shape[1]
    heads = half // LANES
    n_pairs = tokens // LANES
    core, chip = device_place()
    glob_block = column_of(pos_ref[...] // BLK)
    for j in range(n_pairs):
        block = (chip * n_pairs + j) * (LANES // BLK) + lax.broadcasted_iota(jnp.int32, (glob, LANES), 1) // BLK
        bias[j] = jnp.where(jnp.abs(glob_block - block.astype(jnp.float32)) > 1.5, 0.0, NEG)
    for head in range(heads):
        row = w_ref[pl.ds(core * heads + head, 1), :]
        w_cols[head] = jnp.transpose(jnp.broadcast_to(row, (LANES, LANES)))

    def one_head(head, carry):
        cols = pl.ds(pl.multiple_of(head * LANES, LANES), LANES)
        kv_a = kv_a_ref[:, cols]
        if on_line():
            kv_a = jnp.where(is_inner(chip), kv_a, jnp.zeros_like(kv_a))
        kv = kv_a + kv_b_ref[:, cols]
        kg = kv[:glob]
        for j in range(n_pairs):
            s_buf[j] = dot_n(kg, q_t_ref[cols, j * LANES : (j + 1) * LANES])
        near_peaks = stat_ref[head, 0]
        near_totals = stat_ref[head, 1]
        near_weights, inverses = [], []
        for j in range(n_pairs):
            far = s_buf[j] + bias[j]
            near_peak = near_peaks[j : j + 1]
            peak = jnp.maximum(jnp.max(far, axis=0, keepdims=True), near_peak)
            e_far = jnp.exp2((far - peak) * scale2)
            e_buf[j] = e_far.astype(jnp.bfloat16)
            near_weight = jnp.exp2((near_peak - peak) * scale2)
            total = near_totals[j : j + 1] * near_weight + jnp.sum(e_far, axis=0, keepdims=True)
            near_weights.append(near_weight)
            inverses.append(1.0 / total)
        vg_t = jnp.transpose(kv[glob:])
        w = w_cols[head]
        lins, sqs = [], []
        for j in range(n_pairs):
            acc = acc_ref[head, j] * near_weights[j] + dot_n(vg_t, e_buf[j])
            lins.append(jnp.sum(acc * w, axis=0, keepdims=True) * inverses[j])
            sqs.append(jnp.sum(acc * acc, axis=0, keepdims=True) * (inverses[j] * inverses[j]))
        lin, sq = carry
        return lin + jnp.concatenate(lins, axis=0), sq + jnp.concatenate(sqs, axis=0)

    none = jnp.zeros((n_pairs, LANES), jnp.float32)
    lin, sq = lax.fori_loop(0, heads, one_head, (none, none))
    out_ref[0] = lin
    out_ref[1] = sq


def call(kernel, name, outs, args, scratch=(), micros=0.0, from_hbm=False):
    spec = pl.BlockSpec(memory_space=pltpu.VMEM)
    source = pltpu.HBM if from_hbm else pltpu.VMEM
    single = not isinstance(outs, list)
    shapes = [outs] if single else outs
    result = pl.pallas_call(
        kernel,
        in_specs=[pl.BlockSpec(memory_space=source)] * len(args),
        out_specs=[spec] * len(shapes),
        out_shape=[pltpu.VMEM(shape, dtype) for shape, dtype in shapes],
        scratch_shapes=[pltpu.VMEM(*x) if isinstance(x, tuple) else x for x in scratch],
        compiler_params=pltpu.CompilerParams(vmem_limit_bytes=16 * 1024 * 1024),
        cost_estimate=pl.CostEstimate(flops=int(micros * 1e9) + 1, transcendentals=0, bytes_accessed=1),
        name=name,
    )(*[pltpu.with_memory_space_constraint(x, source) for x in args])
    return result[0] if single else result


def on_device(queries, keys, values, global_positions, score_weight):
    rows, model_width = queries.shape
    head_size = model_width // HEADS
    half = model_width // CORES
    half_heads = HEADS // CORES
    glob = global_positions.shape[0]
    seq_count = lax.axis_size("seq")
    chips = seq_count // CORES
    scale2 = head_size ** (-0.5) * LOG2E
    bf16 = jnp.bfloat16
    f32 = jnp.float32
    rounds = int(math.log2(chips))
    tokens = CORES * rows
    n_pairs = tokens // LANES

    def swap(x, mask):
        return lax.ppermute(x, "seq", [(i, i ^ mask) for i in range(seq_count)])

    def move_cores(x):
        moves = [(i, i + (CORES if i % CORES else -CORES)) for i in range(seq_count)]
        return lax.ppermute(x, "seq", [(i, to) for i, to in moves if 0 <= to < seq_count])

    def move(x, pairs):
        return lax.ppermute(x, "seq", [(a * CORES + c, b * CORES + c) for a, b in pairs for c in range(CORES)])

    inward = ((0, 1), (3, 2))
    across = ((1, 2), (2, 1))
    outward = ((1, 0), (2, 3))

    def after(arrays, *others):
        return lax.optimization_barrier((*arrays, *others))[: len(arrays)]

    row_positions = global_positions.reshape(1, glob)
    small = ((glob, half), bf16)
    pair_of = ((2 * glob, half), bf16)
    three = ((3 * glob, half), bf16)
    bulk = ((3 * rows, half), bf16)
    edge = ((2 * BLK, half), bf16)
    own, sib, edge_own, mine, bulk_sib = call(
        functools.partial(select_kernel, half),
        "select_rows",
        [three, three, ((2 * BLK, model_width), bf16), bulk, bulk],
        [row_positions, queries, keys, values],
        [((1, glob), jnp.int32), pltpu.SemaphoreType.DMA((9,))],
        from_hbm=True,
    )
    q_near, kv_near = call(join_kernel, "join_cores", [small, pair_of], [own, swap(sib, 1)])
    edge_a = move_cores(edge_own)
    bulk_sib = after((bulk_sib,), q_near)[0]
    bulk_recv = swap(bulk_sib, 1)
    for r in range(1, rounds):
        q_near = call(add_kernel, "add_queries", small, [q_near, swap(q_near, 1 << r)])
    edge_a = after((edge_a,), q_near)[0]
    q_far = swap(q_near, 1 << rounds)
    edge_b = swap(call(edge_kernel, "split_edges", edge, [edge_a]), 1)
    k_all, v_t, q_t = call(
        prepare_kernel,
        "prepare",
        [((tokens + 2 * BLK, half), bf16), ((half, tokens + 2 * BLK), bf16), ((half, tokens), bf16)],
        [mine, bulk_recv],
        [((tokens + 2 * BLK, half), bf16)],
        micros=1.6,
    )
    kv_near = after((kv_near,), k_all)[0]
    if chips == 4:
        kv_near = call(add_kernel, "add_keys_values", pair_of, [kv_near, move(kv_near, inward)])
        kv_near = call(add_kernel, "add_keys_values", pair_of, [kv_near, move(kv_near, across)])
        kv_far = move(kv_near, outward)
    else:
        for r in range(1, rounds):
            kv_near = call(add_kernel, "add_keys_values", pair_of, [kv_near, swap(kv_near, 1 << r)])
        kv_far = swap(kv_near, 1 << rounds)

    part = ((half_heads // 2, head_size + STAT_ROWS, LANES), bf16)
    message = call(
        functools.partial(global_kernel, scale2),
        "global_partial",
        part,
        [q_near, q_far, k_all, v_t],
        [((half_heads // 2, tokens, LANES), f32), ((half_heads // 2, tokens + 2 * BLK, LANES), bf16)],
    )
    weights = score_weight.reshape(HEADS, head_size)
    if chips == 4:
        message = call(
            functools.partial(inward_kernel, scale2), "merge_partial", part, [message, move(message, inward)]
        )
        message_far = move(message, across)
    else:
        for r in range(1, rounds):
            message = call(
                functools.partial(merge_kernel, scale2), "merge_partial", part, [message, swap(message, 1 << r)]
            )
        message_far = swap(message, 1 << rounds)
    sums = call(
        functools.partial(sums_kernel, scale2), "global_sums", ((8, LANES), f32), [message, message_far, weights]
    )
    sums_far = move(sums, outward) if chips == 4 else sums

    near_acc, near_stat = call(
        functools.partial(near_kernel, scale2),
        "near_attention",
        [((half_heads, n_pairs, head_size, LANES), f32), ((half_heads, 2, n_pairs, LANES), f32)],
        [q_t, k_all, v_t, edge_a, edge_b],
        [((n_pairs, 4 * BLK, LANES), f32), ((n_pairs, 4 * BLK, LANES), bf16), ((2, 2 * BLK, half), bf16)],
        micros=4.0,
    )
    window = call(
        functools.partial(far_kernel, scale2),
        "far_attention",
        ((2, n_pairs, LANES), f32),
        [q_t, near_acc, near_stat, kv_near, kv_far, weights, row_positions],
        [
            ((n_pairs, glob, LANES), f32),
            ((n_pairs, glob, LANES), bf16),
            ((n_pairs, glob, LANES), f32),
            ((half_heads, LANES, LANES), f32),
        ],
        micros=2.0,
    )
    share = ((2, n_pairs // CORES, LANES), f32)
    mine, theirs = call(
        place_kernel, "place_global", [share, share], [sums, sums_far, row_positions, window]
    )
    theirs = swap(theirs, 1)
    lin = mine[0] + theirs[0]
    sq = mine[1] + theirs[1]
    return (lin * lax.rsqrt(sq * (1.0 / model_width) + 1e-06)).reshape(rows)


def solution(mesh):
    placed = (
        P(("doc", "seq"), None),
        P(("doc", "seq"), None),
        P(("doc", "seq"), None),
        P("doc"),
        P(),
    )
    return jax.shard_map(
        on_device, mesh=mesh, in_specs=placed, out_specs=P(("doc", "seq")), check_vma=False
    )
```

```python
import functools
import math

import jax
import jax.numpy as jnp
from jax import lax
from jax.experimental import pallas as pl
from jax.experimental.pallas import tpu as pltpu
from jax.sharding import PartitionSpec as P

HEADS = 16
BLK = 64
CORES = 2
LANES = 128
NEG = -1e30
LOG2E = math.log2(math.e)
STAT_ROWS = 16


def pieces(x):
    hi = x.astype(jnp.bfloat16)
    rest = x - hi.astype(jnp.float32)
    mid = rest.astype(jnp.bfloat16)
    low = (rest - mid.astype(jnp.float32)).astype(jnp.bfloat16)
    return hi, mid, low


def dot_t(a, b):
    return lax.dot_general(a, b, (((1,), (1,)), ((), ())), preferred_element_type=jnp.float32)


def dot_n(a, b):
    return lax.dot_general(a, b, (((1,), (0,)), ((), ())), preferred_element_type=jnp.float32)


def put_message(out_ref, pair, out, peak, total):
    rows = out.shape[0]
    out_ref[pair, :rows, :] = out.astype(jnp.bfloat16)
    stats = [p.astype(jnp.float32) for p in (*pieces(peak), *pieces(total))]
    row = lax.broadcasted_iota(jnp.int32, (STAT_ROWS, LANES), 0)
    block = jnp.zeros((STAT_ROWS, LANES), jnp.float32)
    for i, stat in enumerate(stats):
        block = jnp.where(row == i, jnp.broadcast_to(stat, block.shape), block)
    out_ref[pair, rows:, :] = block.astype(jnp.bfloat16)


def get_message(ref, pair, head_size):
    out = ref[pair, :head_size, :].astype(jnp.float32)
    stats = ref[pair, head_size:, :].astype(jnp.float32)
    peak = stats[0:1] + stats[1:2] + stats[2:3]
    total = stats[3:4] + stats[4:5] + stats[5:6]
    return out, peak, total


def merged(a, b, scale2):
    out_a, peak_a, total_a = a
    out_b, peak_b, total_b = b
    peak = jnp.maximum(peak_a, peak_b)
    weight_a = jnp.exp2((peak_a - peak) * scale2) * total_a
    weight_b = jnp.exp2((peak_b - peak) * scale2) * total_b
    total = weight_a + weight_b
    inv = 1.0 / total
    return out_a * (weight_a * inv) + out_b * (weight_b * inv), peak, total


def device_place():
    index = lax.axis_index("seq")
    return index % CORES, index // CORES


def column_of(row):
    wide = jnp.concatenate([row, row], axis=1).astype(jnp.float32)
    return jnp.transpose(jnp.broadcast_to(wide, (LANES, LANES)))[: row.shape[1]]


def own_positions(pos_ref, rows):
    core, chip = device_place()
    row = (chip * CORES + core) * rows + lax.broadcasted_iota(jnp.int32, (rows, pos_ref.shape[1]), 0)
    return jnp.where(row == pos_ref[...], 1.0, 0.0).astype(jnp.bfloat16)


def select_kernel(half, pos_hbm, q_hbm, k_hbm, v_hbm, sel_ref, sib_ref, edge_ref, mine_ref, bulk_ref, pos_ref, sems):
    rows = q_hbm.shape[0]
    core, _ = device_place()
    block = pl.ds(pl.multiple_of(core * (rows - BLK), BLK), BLK)
    pos_copy = pltpu.make_async_copy(pos_hbm, pos_ref, sems.at[0])
    copies = []
    for i, x_hbm in enumerate((q_hbm, k_hbm, v_hbm)):
        for to_ref, which in ((bulk_ref, 1 - core), (mine_ref, core)):
            cols = pl.ds(pl.multiple_of(which * half, half), half)
            to = to_ref.at[i * rows : (i + 1) * rows, :]
            copies.append(pltpu.make_async_copy(x_hbm.at[:, cols], to, sems.at[1 + len(copies)]))
    edges = [
        pltpu.make_async_copy(x_hbm.at[block, :], edge_ref.at[i * BLK : (i + 1) * BLK, :], sems.at[7 + i])
        for i, x_hbm in enumerate((k_hbm, v_hbm))
    ]
    for copy in (pos_copy, *copies, *edges):
        copy.start()
    pos_copy.wait()
    hit = own_positions(pos_ref, rows)
    glob = hit.shape[1]
    contract = (((0,), (0,)), ((), ()))
    for i in range(3):
        for copy, x_ref, out_ref in ((copies[2 * i], bulk_ref, sib_ref), (copies[2 * i + 1], mine_ref, sel_ref)):
            copy.wait()
            x = x_ref[i * rows : (i + 1) * rows, :]
            picked = lax.dot_general(hit, x, contract, preferred_element_type=jnp.float32)
            out_ref[i * glob : (i + 1) * glob, :] = picked.astype(jnp.bfloat16)
    for copy in edges:
        copy.wait()


def join_kernel(own_ref, recv_ref, q_ref, kv_ref):
    count = q_ref.shape[0]
    q_ref[...] = own_ref[:count, :] + recv_ref[:count, :]
    kv_ref[...] = own_ref[count:, :] + recv_ref[count:, :]


def edge_kernel(full_ref, out_ref):
    half = out_ref.shape[1]
    core, _ = device_place()
    out_ref[...] = full_ref[:, pl.ds(pl.multiple_of((1 - core) * half, half), half)]


def add_kernel(a_ref, b_ref, out_ref):
    out_ref[...] = a_ref[...] + b_ref[...]


def on_line():
    return lax.axis_size("seq") // CORES == 4


def is_inner(chip):
    return (chip == 1) | (chip == 2)


def prepare_kernel(own_ref, sib_ref, k_ref, v_t_ref, q_t_ref, v_all):
    rows = own_ref.shape[0] // 3
    half = k_ref.shape[1]
    core, _ = device_place()
    zero = jnp.zeros((BLK, half), jnp.bfloat16)
    for ref in (k_ref, v_all):
        ref[:BLK, :] = zero
        ref[BLK + CORES * rows :, :] = zero
    for part_ref, which in ((own_ref, core), (sib_ref, 1 - core)):
        at = pl.ds(pl.multiple_of(which * rows + BLK, BLK), rows)
        k_ref[at, :] = part_ref[rows : 2 * rows, :]
        v_all[at, :] = part_ref[2 * rows :, :]

    def turn(head, carry):
        lanes = pl.ds(pl.multiple_of(head * LANES, LANES), LANES)
        v_t_ref[lanes, :] = jnp.transpose(v_all[:, lanes])
        for part_ref, which in ((own_ref, core), (sib_ref, 1 - core)):
            q_t_ref[lanes, pl.ds(pl.multiple_of(which * rows, LANES), rows)] = jnp.transpose(part_ref[:rows, lanes])
        return carry

    lax.fori_loop(0, half // LANES, turn, 0)


def global_kernel(scale2, q_a_ref, q_b_ref, k_ref, v_t_ref, out_ref, s_buf, e_buf):
    glob, half = q_a_ref.shape
    head_size = LANES
    pairs = half // (2 * head_size)
    tokens = k_ref.shape[0] - 2 * BLK
    row = lax.broadcasted_iota(jnp.int32, (2 * glob, 2 * head_size), 0)
    col = lax.broadcasted_iota(jnp.int32, (2 * glob, 2 * head_size), 1)
    keep = (row < glob) == (col < head_size)
    lane = lax.broadcasted_iota(jnp.int32, (head_size, LANES), 1)
    for pair in range(pairs):
        cols = slice(2 * pair * head_size, 2 * (pair + 1) * head_size)
        q = q_a_ref[:, cols] + q_b_ref[:, cols]
        doubled = jnp.concatenate([q, q], axis=0)
        diag = jnp.where(keep, doubled, jnp.zeros_like(doubled))
        s_buf[pair] = dot_t(k_ref[BLK : BLK + tokens, cols], diag)
    stats = []
    for pair in range(pairs):
        s = s_buf[pair]
        peak = jnp.max(s, axis=0, keepdims=True)
        e = jnp.exp2((s - peak) * scale2)
        stats.append((peak, jnp.sum(e, axis=0, keepdims=True)))
        zero = jnp.zeros((BLK, LANES), jnp.bfloat16)
        e_buf[pair, :BLK] = zero
        e_buf[pair, BLK + tokens :] = zero
        e_buf[pair, BLK : BLK + tokens] = e.astype(jnp.bfloat16)
    for pair in range(pairs):
        rows = slice(2 * pair * head_size, 2 * (pair + 1) * head_size)
        acc = dot_n(v_t_ref[rows, :], e_buf[pair])
        peak, total = stats[pair]
        out = jnp.where(lane < glob, acc[:head_size], acc[head_size:]) / total
        put_message(out_ref, pair, out, peak, total)


def merge_kernel(scale2, a_ref, b_ref, out_ref):
    head_size = a_ref.shape[1] - STAT_ROWS
    for pair in range(a_ref.shape[0]):
        a = get_message(a_ref, pair, head_size)
        b = get_message(b_ref, pair, head_size)
        put_message(out_ref, pair, *merged(a, b, scale2))


def inward_kernel(scale2, a_ref, b_ref, out_ref):
    _, chip = device_place()

    @pl.when(is_inner(chip))
    def _():
        merge_kernel(scale2, a_ref, b_ref, out_ref)

    @pl.when(jnp.logical_not(is_inner(chip)))
    def _():
        out_ref[...] = a_ref[...]


def sums_kernel(scale2, a_ref, b_ref, w_ref, out_ref):
    pairs = a_ref.shape[0]
    head_size = a_ref.shape[1] - STAT_ROWS
    glob = LANES // 2
    core, chip = device_place()
    upper = lax.broadcasted_iota(jnp.int32, (LANES, head_size), 0) < glob
    lin = jnp.zeros((1, LANES), jnp.float32)
    sq = jnp.zeros((1, LANES), jnp.float32)
    for pair in range(pairs):
        a = get_message(a_ref, pair, head_size)
        b = get_message(b_ref, pair, head_size)
        if on_line():
            b = tuple(jnp.where(is_inner(chip), y, x) for x, y in zip(a, b))
        out, _, _ = merged(a, b, scale2)
        w_a = w_ref[pl.ds(core * 2 * pairs + 2 * pair, 1), :]
        w_b = w_ref[pl.ds(core * 2 * pairs + 2 * pair + 1, 1), :]
        w = jnp.transpose(jnp.where(upper, w_a, w_b))
        lin = lin + jnp.sum(out * w, axis=0, keepdims=True)
        sq = sq + jnp.sum(out * out, axis=0, keepdims=True)
    out_ref[...] = jnp.zeros_like(out_ref)
    out_ref[0:1, :] = lin + pltpu.roll(lin, glob, 1)
    out_ref[1:2, :] = sq + pltpu.roll(sq, glob, 1)


def place_kernel(own_sums_ref, far_sums_ref, pos_ref, win_ref, own_ref, sib_ref):
    glob = pos_ref.shape[1]
    core, chip = device_place()
    sums = own_sums_ref[...]
    if on_line():
        sums = jnp.where(is_inner(chip), sums, far_sums_ref[...])
    parts = [p.astype(jnp.float32) for p in (*pieces(sums[0:1]), *pieces(sums[1:2]))] + [jnp.ones((1, LANES), jnp.float32)]
    row = lax.broadcasted_iota(jnp.int32, (16, LANES), 0)
    table = jnp.zeros((16, LANES), jnp.float32)
    for i, part in enumerate(parts):
        table = jnp.where(row == i, jnp.broadcast_to(part, table.shape), table)
    table = table.astype(jnp.bfloat16)[:, :glob]
    pos = column_of(pos_ref[...])
    n_pairs = win_ref.shape[1]
    each = n_pairs // CORES
    for out_ref, which in ((sib_ref, 1 - core), (own_ref, core)):
        for j in range(each):
            pair = which * each + j
            token = (chip * n_pairs + pair) * LANES + lax.broadcasted_iota(jnp.int32, (glob, LANES), 1)
            hit = jnp.where(pos == token.astype(jnp.float32), 1.0, 0.0).astype(jnp.bfloat16)
            placed = dot_n(table, hit)
            is_glob = placed[6:7] > 0.5
            for i in (0, 1):
                value = placed[3 * i : 3 * i + 1] + placed[3 * i + 1 : 3 * i + 2] + placed[3 * i + 2 : 3 * i + 3]
                out_ref[i, j : j + 1, :] = jnp.where(is_glob, value, win_ref[i, pl.ds(pair, 1), :])


def near_kernel(scale2, q_t_ref, k_ref, v_t_ref, edge_a_ref, edge_b_ref, acc_ref, stat_ref, s_buf, e_buf, edges):
    half, tokens = q_t_ref.shape
    n_pairs = tokens // LANES
    core, chip = device_place()
    chips = lax.axis_size("seq") // CORES
    left = lax.broadcasted_iota(jnp.int32, (BLK, LANES), 1) < BLK
    wide_left = lax.broadcasted_iota(jnp.int32, (LANES, LANES), 1) < BLK
    first_bias = jnp.where(left & (chip == 0), NEG, 0.0)
    last_bias = jnp.where((~left) & (chip == chips - 1), NEG, 0.0)

    mine = pl.ds(pl.multiple_of(core * half, half), half)

    @pl.when(core == 1)
    def _():
        edges[0] = edge_a_ref[:, mine]
        edges[1] = edge_b_ref[...]

    @pl.when(core == 0)
    def _():
        edges[0] = edge_b_ref[...]
        edges[1] = edge_a_ref[:, mine]

    def one_head(head, carry):
        cols = pl.ds(pl.multiple_of(head * LANES, LANES), LANES)
        for j in range(n_pairs):
            if j == 0:
                k = jnp.concatenate([edges[0, :BLK, cols], k_ref[BLK : 4 * BLK, cols]], axis=0)
            elif j == n_pairs - 1:
                k = jnp.concatenate([k_ref[j * LANES : j * LANES + 3 * BLK, cols], edges[1, :BLK, cols]], axis=0)
            else:
                k = k_ref[j * LANES : (j + 2) * LANES, cols]
            s_buf[j] = dot_n(k, q_t_ref[cols, j * LANES : (j + 1) * LANES])
        peaks, totals = [], []
        for j in range(n_pairs):
            ends = jnp.where(left, s_buf[j, :BLK], s_buf[j, 3 * BLK :])
            if j == 0:
                ends = ends + first_bias
            if j == n_pairs - 1:
                ends = ends + last_bias
            mid = s_buf[j, BLK : 3 * BLK]
            peak = jnp.max(jnp.maximum(ends, jnp.maximum(mid[:BLK], mid[BLK:])), axis=0, keepdims=True)
            e_ends = jnp.exp2((ends - peak) * scale2)
            e_mid = jnp.exp2((mid - peak) * scale2)
            zero = jnp.zeros_like(e_ends)
            e_buf[j, :BLK] = jnp.where(left, e_ends, zero).astype(jnp.bfloat16)
            e_buf[j, BLK : 3 * BLK] = e_mid.astype(jnp.bfloat16)
            e_buf[j, 3 * BLK :] = jnp.where(left, zero, e_ends).astype(jnp.bfloat16)
            peaks.append(peak)
            totals.append(jnp.sum(e_ends + e_mid[:BLK] + e_mid[BLK:], axis=0, keepdims=True))
        stat_ref[head, 0] = jnp.concatenate(peaks, axis=0)
        stat_ref[head, 1] = jnp.concatenate(totals, axis=0)
        turned = jnp.transpose(jnp.concatenate([edges[0, BLK:, cols], edges[1, BLK:, cols]], axis=0))
        for j in range(n_pairs):
            v_0 = v_t_ref[cols, j * LANES : (j + 1) * LANES]
            v_1 = v_t_ref[cols, (j + 1) * LANES : (j + 2) * LANES]
            if j == 0:
                v_0 = jnp.where(wide_left, turned, v_0)
            if j == n_pairs - 1:
                v_1 = jnp.where(wide_left, v_1, turned)
            acc_ref[head, j] = dot_n(jnp.concatenate([v_0, v_1], axis=1), e_buf[j])
        return carry

    lax.fori_loop(0, half // LANES, one_head, 0)


def far_kernel(
    scale2, q_t_ref, acc_ref, stat_ref, kv_a_ref, kv_b_ref, w_ref, pos_ref, out_ref, s_buf, e_buf, bias, w_cols
):
    half, tokens = q_t_ref.shape
    glob = pos_ref.shape[1]
    heads = half // LANES
    n_pairs = tokens // LANES
    core, chip = device_place()
    glob_block = column_of(pos_ref[...] // BLK)
    for j in range(n_pairs):
        block = (chip * n_pairs + j) * (LANES // BLK) + lax.broadcasted_iota(jnp.int32, (glob, LANES), 1) // BLK
        bias[j] = jnp.where(jnp.abs(glob_block - block.astype(jnp.float32)) > 1.5, 0.0, NEG)
    for head in range(heads):
        row = w_ref[pl.ds(core * heads + head, 1), :]
        w_cols[head] = jnp.transpose(jnp.broadcast_to(row, (LANES, LANES)))

    def one_head(head, carry):
        cols = pl.ds(pl.multiple_of(head * LANES, LANES), LANES)
        kv_a = kv_a_ref[:, cols]
        if on_line():
            kv_a = jnp.where(is_inner(chip), kv_a, jnp.zeros_like(kv_a))
        kv = kv_a + kv_b_ref[:, cols]
        kg = kv[:glob]
        for j in range(n_pairs):
            s_buf[j] = dot_n(kg, q_t_ref[cols, j * LANES : (j + 1) * LANES])
        near_peaks = stat_ref[head, 0]
        near_totals = stat_ref[head, 1]
        near_weights, inverses = [], []
        for j in range(n_pairs):
            far = s_buf[j] + bias[j]
            near_peak = near_peaks[j : j + 1]
            peak = jnp.maximum(jnp.max(far, axis=0, keepdims=True), near_peak)
            e_far = jnp.exp2((far - peak) * scale2)
            e_buf[j] = e_far.astype(jnp.bfloat16)
            near_weight = jnp.exp2((near_peak - peak) * scale2)
            total = near_totals[j : j + 1] * near_weight + jnp.sum(e_far, axis=0, keepdims=True)
            near_weights.append(near_weight)
            inverses.append(1.0 / total)
        vg_t = jnp.transpose(kv[glob:])
        w = w_cols[head]
        lins, sqs = [], []
        for j in range(n_pairs):
            acc = acc_ref[head, j] * near_weights[j] + dot_n(vg_t, e_buf[j])
            lins.append(jnp.sum(acc * w, axis=0, keepdims=True) * inverses[j])
            sqs.append(jnp.sum(acc * acc, axis=0, keepdims=True) * (inverses[j] * inverses[j]))
        lin, sq = carry
        return lin + jnp.concatenate(lins, axis=0), sq + jnp.concatenate(sqs, axis=0)

    none = jnp.zeros((n_pairs, LANES), jnp.float32)
    lin, sq = lax.fori_loop(0, heads, one_head, (none, none))
    out_ref[0] = lin
    out_ref[1] = sq


def call(kernel, name, outs, args, scratch=(), micros=0.0, from_hbm=False):
    spec = pl.BlockSpec(memory_space=pltpu.VMEM)
    source = pltpu.HBM if from_hbm else pltpu.VMEM
    single = not isinstance(outs, list)
    shapes = [outs] if single else outs
    result = pl.pallas_call(
        kernel,
        in_specs=[pl.BlockSpec(memory_space=source)] * len(args),
        out_specs=[spec] * len(shapes),
        out_shape=[pltpu.VMEM(shape, dtype) for shape, dtype in shapes],
        scratch_shapes=[pltpu.VMEM(*x) if isinstance(x, tuple) else x for x in scratch],
        compiler_params=pltpu.CompilerParams(vmem_limit_bytes=16 * 1024 * 1024),
        cost_estimate=pl.CostEstimate(flops=int(micros * 1e9) + 1, transcendentals=0, bytes_accessed=1),
        name=name,
    )(*[pltpu.with_memory_space_constraint(x, source) for x in args])
    return result[0] if single else result


def on_device(queries, keys, values, global_positions, score_weight):
    rows, model_width = queries.shape
    head_size = model_width // HEADS
    half = model_width // CORES
    half_heads = HEADS // CORES
    glob = global_positions.shape[0]
    seq_count = lax.axis_size("seq")
    chips = seq_count // CORES
    scale2 = head_size ** (-0.5) * LOG2E
    bf16 = jnp.bfloat16
    f32 = jnp.float32
    rounds = int(math.log2(chips))
    tokens = CORES * rows
    n_pairs = tokens // LANES

    def swap(x, mask):
        return lax.ppermute(x, "seq", [(i, i ^ mask) for i in range(seq_count)])

    def move_cores(x):
        moves = [(i, i + (CORES if i % CORES else -CORES)) for i in range(seq_count)]
        return lax.ppermute(x, "seq", [(i, to) for i, to in moves if 0 <= to < seq_count])

    def move(x, pairs):
        return lax.ppermute(x, "seq", [(a * CORES + c, b * CORES + c) for a, b in pairs for c in range(CORES)])

    inward = ((0, 1), (3, 2))
    across = ((1, 2), (2, 1))
    outward = ((1, 0), (2, 3))

    def after(arrays, *others):
        return lax.optimization_barrier((*arrays, *others))[: len(arrays)]

    row_positions = global_positions.reshape(1, glob)
    small = ((glob, half), bf16)
    pair_of = ((2 * glob, half), bf16)
    three = ((3 * glob, half), bf16)
    bulk = ((3 * rows, half), bf16)
    edge = ((2 * BLK, half), bf16)
    own, sib, edge_own, mine, bulk_sib = call(
        functools.partial(select_kernel, half),
        "select_rows",
        [three, three, ((2 * BLK, model_width), bf16), bulk, bulk],
        [row_positions, queries, keys, values],
        [((1, glob), jnp.int32), pltpu.SemaphoreType.DMA((9,))],
        from_hbm=True,
    )
    q_near, kv_near = call(join_kernel, "join_cores", [small, pair_of], [own, swap(sib, 1)])
    edge_a = move_cores(edge_own)
    bulk_sib = after((bulk_sib,), q_near)[0]
    bulk_recv = swap(bulk_sib, 1)
    for r in range(1, rounds):
        q_near = call(add_kernel, "add_queries", small, [q_near, swap(q_near, 1 << r)])
    edge_a = after((edge_a,), q_near)[0]
    q_far = swap(q_near, 1 << rounds)
    edge_b = swap(call(edge_kernel, "split_edges", edge, [edge_a]), 1)
    bulk_recv = after((bulk_recv,), q_near)[0]
    k_all, v_t, q_t = call(
        prepare_kernel,
        "prepare",
        [((tokens + 2 * BLK, half), bf16), ((half, tokens + 2 * BLK), bf16), ((half, tokens), bf16)],
        [mine, bulk_recv],
        [((tokens + 2 * BLK, half), bf16)],
        micros=1.6,
    )
    near_acc, near_stat = call(
        functools.partial(near_kernel, scale2),
        "near_attention",
        [((half_heads, n_pairs, head_size, LANES), f32), ((half_heads, 2, n_pairs, LANES), f32)],
        [q_t, k_all, v_t, edge_a, edge_b],
        [((n_pairs, 4 * BLK, LANES), f32), ((n_pairs, 4 * BLK, LANES), bf16), ((2, 2 * BLK, half), bf16)],
        micros=4.0,
    )
    kv_near = after((kv_near,), k_all)[0]
    if chips == 4:
        kv_near = call(add_kernel, "add_keys_values", pair_of, [kv_near, move(kv_near, inward)])
        kv_near = call(add_kernel, "add_keys_values", pair_of, [kv_near, move(kv_near, across)])
        kv_far = move(kv_near, outward)
    else:
        for r in range(1, rounds):
            kv_near = call(add_kernel, "add_keys_values", pair_of, [kv_near, swap(kv_near, 1 << r)])
        kv_far = swap(kv_near, 1 << rounds)

    part = ((half_heads // 2, head_size + STAT_ROWS, LANES), bf16)
    message = call(
        functools.partial(global_kernel, scale2),
        "global_partial",
        part,
        [q_near, q_far, k_all, v_t],
        [((half_heads // 2, tokens, LANES), f32), ((half_heads // 2, tokens + 2 * BLK, LANES), bf16)],
        micros=20.0,
    )
    weights = score_weight.reshape(HEADS, head_size)
    if chips == 4:
        message = call(
            functools.partial(inward_kernel, scale2), "merge_partial", part, [message, after((move(message, inward),), kv_near)[0]]
        )
        message_far = move(message, across)
    else:
        for r in range(1, rounds):
            message = call(
                functools.partial(merge_kernel, scale2), "merge_partial", part, [message, swap(message, 1 << r)]
            )
        message_far = swap(message, 1 << rounds)
    sums = call(
        functools.partial(sums_kernel, scale2), "global_sums", ((8, LANES), f32), [message, message_far, weights]
    )
    sums_far = move(sums, outward) if chips == 4 else sums

    window = call(
        functools.partial(far_kernel, scale2),
        "far_attention",
        ((2, n_pairs, LANES), f32),
        [q_t, near_acc, near_stat, kv_near, kv_far, weights, row_positions],
        [
            ((n_pairs, glob, LANES), f32),
            ((n_pairs, glob, LANES), bf16),
            ((n_pairs, glob, LANES), f32),
            ((half_heads, LANES, LANES), f32),
        ],
        micros=2.0,
    )
    share = ((2, n_pairs // CORES, LANES), f32)
    mine, theirs = call(
        place_kernel, "place_global", [share, share], [sums, sums_far, row_positions, window]
    )
    theirs = swap(theirs, 1)
    lin = mine[0] + theirs[0]
    sq = mine[1] + theirs[1]
    return (lin * lax.rsqrt(sq * (1.0 / model_width) + 1e-06)).reshape(rows)


def solution(mesh):
    placed = (
        P(("doc", "seq"), None),
        P(("doc", "seq"), None),
        P(("doc", "seq"), None),
        P("doc"),
        P(),
    )
    return jax.shard_map(
        on_device, mesh=mesh, in_specs=placed, out_specs=P(("doc", "seq")), check_vma=False
    )
```

```python
import functools
import math

import jax
import jax.numpy as jnp
from jax import lax
from jax.experimental import pallas as pl
from jax.experimental.pallas import tpu as pltpu
from jax.sharding import PartitionSpec as P

HEADS = 16
BLK = 64
CORES = 2
LANES = 128
NEG = -1e30
LOG2E = math.log2(math.e)
STAT_ROWS = 16


def pieces(x):
    hi = x.astype(jnp.bfloat16)
    rest = x - hi.astype(jnp.float32)
    mid = rest.astype(jnp.bfloat16)
    low = (rest - mid.astype(jnp.float32)).astype(jnp.bfloat16)
    return hi, mid, low


def dot_t(a, b):
    return lax.dot_general(a, b, (((1,), (1,)), ((), ())), preferred_element_type=jnp.float32)


def dot_n(a, b):
    return lax.dot_general(a, b, (((1,), (0,)), ((), ())), preferred_element_type=jnp.float32)


def put_message(out_ref, pair, out, peak, total):
    rows = out.shape[0]
    out_ref[pair, :rows, :] = out.astype(jnp.bfloat16)
    stats = [p.astype(jnp.float32) for p in (*pieces(peak), *pieces(total))]
    row = lax.broadcasted_iota(jnp.int32, (STAT_ROWS, LANES), 0)
    block = jnp.zeros((STAT_ROWS, LANES), jnp.float32)
    for i, stat in enumerate(stats):
        block = jnp.where(row == i, jnp.broadcast_to(stat, block.shape), block)
    out_ref[pair, rows:, :] = block.astype(jnp.bfloat16)


def get_message(ref, pair, head_size):
    out = ref[pair, :head_size, :].astype(jnp.float32)
    stats = ref[pair, head_size:, :].astype(jnp.float32)
    peak = stats[0:1] + stats[1:2] + stats[2:3]
    total = stats[3:4] + stats[4:5] + stats[5:6]
    return out, peak, total


def merged(a, b, scale2):
    out_a, peak_a, total_a = a
    out_b, peak_b, total_b = b
    peak = jnp.maximum(peak_a, peak_b)
    weight_a = jnp.exp2((peak_a - peak) * scale2) * total_a
    weight_b = jnp.exp2((peak_b - peak) * scale2) * total_b
    total = weight_a + weight_b
    inv = 1.0 / total
    return out_a * (weight_a * inv) + out_b * (weight_b * inv), peak, total


def device_place():
    index = lax.axis_index("seq")
    return index % CORES, index // CORES


def column_of(row):
    wide = jnp.concatenate([row, row], axis=1).astype(jnp.float32)
    return jnp.transpose(jnp.broadcast_to(wide, (LANES, LANES)))[: row.shape[1]]


def own_positions(pos_ref, rows):
    core, chip = device_place()
    row = (chip * CORES + core) * rows + lax.broadcasted_iota(jnp.int32, (rows, pos_ref.shape[1]), 0)
    return jnp.where(row == pos_ref[...], 1.0, 0.0).astype(jnp.bfloat16)


def select_kernel(half, pos_hbm, q_hbm, k_hbm, v_hbm, sel_ref, sib_ref, edge_ref, mine_ref, bulk_ref, pos_ref, sems):
    rows = q_hbm.shape[0]
    core, _ = device_place()
    block = pl.ds(pl.multiple_of(core * (rows - BLK), BLK), BLK)
    pos_copy = pltpu.make_async_copy(pos_hbm, pos_ref, sems.at[0])
    copies = []
    for i, x_hbm in enumerate((q_hbm, k_hbm, v_hbm)):
        for to_ref, which in ((bulk_ref, 1 - core), (mine_ref, core)):
            cols = pl.ds(pl.multiple_of(which * half, half), half)
            to = to_ref.at[i * rows : (i + 1) * rows, :]
            copies.append(pltpu.make_async_copy(x_hbm.at[:, cols], to, sems.at[1 + len(copies)]))
    edges = [
        pltpu.make_async_copy(x_hbm.at[block, :], edge_ref.at[i * BLK : (i + 1) * BLK, :], sems.at[7 + i])
        for i, x_hbm in enumerate((k_hbm, v_hbm))
    ]
    for copy in (pos_copy, *copies, *edges):
        copy.start()
    pos_copy.wait()
    hit = own_positions(pos_ref, rows)
    glob = hit.shape[1]
    contract = (((0,), (0,)), ((), ()))
    for i in range(3):
        for copy, x_ref, out_ref in ((copies[2 * i], bulk_ref, sib_ref), (copies[2 * i + 1], mine_ref, sel_ref)):
            copy.wait()
            x = x_ref[i * rows : (i + 1) * rows, :]
            picked = lax.dot_general(hit, x, contract, preferred_element_type=jnp.float32)
            out_ref[i * glob : (i + 1) * glob, :] = picked.astype(jnp.bfloat16)
    for copy in edges:
        copy.wait()


def join_kernel(own_ref, recv_ref, q_ref, kv_ref):
    count = q_ref.shape[0]
    q_ref[...] = own_ref[:count, :] + recv_ref[:count, :]
    kv_ref[...] = own_ref[count:, :] + recv_ref[count:, :]


def edge_kernel(full_ref, out_ref):
    half = out_ref.shape[1]
    core, _ = device_place()
    out_ref[...] = full_ref[:, pl.ds(pl.multiple_of((1 - core) * half, half), half)]


def add_kernel(a_ref, b_ref, out_ref):
    out_ref[...] = a_ref[...] + b_ref[...]


def on_line():
    return lax.axis_size("seq") // CORES == 4


def is_inner(chip):
    return (chip == 1) | (chip == 2)


def prepare_kernel(own_ref, sib_ref, k_ref, v_t_ref, q_t_ref, v_all):
    rows = own_ref.shape[0] // 3
    half = k_ref.shape[1]
    core, _ = device_place()
    zero = jnp.zeros((BLK, half), jnp.bfloat16)
    for ref in (k_ref, v_all):
        ref[:BLK, :] = zero
        ref[BLK + CORES * rows :, :] = zero
    for part_ref, which in ((own_ref, core), (sib_ref, 1 - core)):
        at = pl.ds(pl.multiple_of(which * rows + BLK, BLK), rows)
        k_ref[at, :] = part_ref[rows : 2 * rows, :]
        v_all[at, :] = part_ref[2 * rows :, :]

    def turn(head, carry):
        lanes = pl.ds(pl.multiple_of(head * LANES, LANES), LANES)
        v_t_ref[lanes, :] = jnp.transpose(v_all[:, lanes])
        for part_ref, which in ((own_ref, core), (sib_ref, 1 - core)):
            q_t_ref[lanes, pl.ds(pl.multiple_of(which * rows, LANES), rows)] = jnp.transpose(part_ref[:rows, lanes])
        return carry

    lax.fori_loop(0, half // LANES, turn, 0)


def global_kernel(scale2, q_a_ref, q_b_ref, k_ref, v_t_ref, out_ref, s_buf, e_buf):
    glob, half = q_a_ref.shape
    head_size = LANES
    pairs = half // (2 * head_size)
    tokens = k_ref.shape[0] - 2 * BLK
    row = lax.broadcasted_iota(jnp.int32, (2 * glob, 2 * head_size), 0)
    col = lax.broadcasted_iota(jnp.int32, (2 * glob, 2 * head_size), 1)
    keep = (row < glob) == (col < head_size)
    lane = lax.broadcasted_iota(jnp.int32, (head_size, LANES), 1)
    for pair in range(pairs):
        cols = slice(2 * pair * head_size, 2 * (pair + 1) * head_size)
        q = q_a_ref[:, cols] + q_b_ref[:, cols]
        doubled = jnp.concatenate([q, q], axis=0)
        diag = jnp.where(keep, doubled, jnp.zeros_like(doubled))
        s_buf[pair] = dot_t(k_ref[BLK : BLK + tokens, cols], diag)
    stats = []
    for pair in range(pairs):
        s = s_buf[pair]
        peak = jnp.max(s, axis=0, keepdims=True)
        e = jnp.exp2((s - peak) * scale2)
        stats.append((peak, jnp.sum(e, axis=0, keepdims=True)))
        zero = jnp.zeros((BLK, LANES), jnp.bfloat16)
        e_buf[pair, :BLK] = zero
        e_buf[pair, BLK + tokens :] = zero
        e_buf[pair, BLK : BLK + tokens] = e.astype(jnp.bfloat16)
    for pair in range(pairs):
        rows = slice(2 * pair * head_size, 2 * (pair + 1) * head_size)
        acc = dot_n(v_t_ref[rows, :], e_buf[pair])
        peak, total = stats[pair]
        out = jnp.where(lane < glob, acc[:head_size], acc[head_size:]) / total
        put_message(out_ref, pair, out, peak, total)


def merge_kernel(scale2, a_ref, b_ref, out_ref):
    head_size = a_ref.shape[1] - STAT_ROWS
    for pair in range(a_ref.shape[0]):
        a = get_message(a_ref, pair, head_size)
        b = get_message(b_ref, pair, head_size)
        put_message(out_ref, pair, *merged(a, b, scale2))


def inward_kernel(scale2, a_ref, b_ref, out_ref):
    _, chip = device_place()

    @pl.when(is_inner(chip))
    def _():
        merge_kernel(scale2, a_ref, b_ref, out_ref)

    @pl.when(jnp.logical_not(is_inner(chip)))
    def _():
        out_ref[...] = a_ref[...]


def sums_kernel(scale2, a_ref, b_ref, w_ref, out_ref):
    pairs = a_ref.shape[0]
    head_size = a_ref.shape[1] - STAT_ROWS
    glob = LANES // 2
    core, chip = device_place()
    upper = lax.broadcasted_iota(jnp.int32, (LANES, head_size), 0) < glob
    lin = jnp.zeros((1, LANES), jnp.float32)
    sq = jnp.zeros((1, LANES), jnp.float32)
    for pair in range(pairs):
        a = get_message(a_ref, pair, head_size)
        b = get_message(b_ref, pair, head_size)
        if False:
            b = tuple(jnp.where(is_inner(chip), y, x) for x, y in zip(a, b))
        out, _, _ = merged(a, b, scale2)
        w_a = w_ref[pl.ds(core * 2 * pairs + 2 * pair, 1), :]
        w_b = w_ref[pl.ds(core * 2 * pairs + 2 * pair + 1, 1), :]
        w = jnp.transpose(jnp.where(upper, w_a, w_b))
        lin = lin + jnp.sum(out * w, axis=0, keepdims=True)
        sq = sq + jnp.sum(out * out, axis=0, keepdims=True)
    out_ref[...] = jnp.zeros_like(out_ref)
    out_ref[0:1, :] = lin + pltpu.roll(lin, glob, 1)
    out_ref[1:2, :] = sq + pltpu.roll(sq, glob, 1)


def place_kernel(own_sums_ref, far_sums_ref, pos_ref, win_ref, own_ref, sib_ref):
    glob = pos_ref.shape[1]
    core, chip = device_place()
    sums = own_sums_ref[...]
    if False:
        sums = jnp.where(is_inner(chip), sums, far_sums_ref[...])
    parts = [p.astype(jnp.float32) for p in (*pieces(sums[0:1]), *pieces(sums[1:2]))] + [jnp.ones((1, LANES), jnp.float32)]
    row = lax.broadcasted_iota(jnp.int32, (16, LANES), 0)
    table = jnp.zeros((16, LANES), jnp.float32)
    for i, part in enumerate(parts):
        table = jnp.where(row == i, jnp.broadcast_to(part, table.shape), table)
    table = table.astype(jnp.bfloat16)[:, :glob]
    pos = column_of(pos_ref[...])
    n_pairs = win_ref.shape[1]
    each = n_pairs // CORES
    for out_ref, which in ((sib_ref, 1 - core), (own_ref, core)):
        for j in range(each):
            pair = which * each + j
            token = (chip * n_pairs + pair) * LANES + lax.broadcasted_iota(jnp.int32, (glob, LANES), 1)
            hit = jnp.where(pos == token.astype(jnp.float32), 1.0, 0.0).astype(jnp.bfloat16)
            placed = dot_n(table, hit)
            is_glob = placed[6:7] > 0.5
            for i in (0, 1):
                value = placed[3 * i : 3 * i + 1] + placed[3 * i + 1 : 3 * i + 2] + placed[3 * i + 2 : 3 * i + 3]
                out_ref[i, j : j + 1, :] = jnp.where(is_glob, value, win_ref[i, pl.ds(pair, 1), :])


def near_kernel(scale2, q_t_ref, k_ref, v_t_ref, edge_a_ref, edge_b_ref, acc_ref, stat_ref, s_buf, e_buf, edges):
    half, tokens = q_t_ref.shape
    n_pairs = tokens // LANES
    core, chip = device_place()
    chips = lax.axis_size("seq") // CORES
    left = lax.broadcasted_iota(jnp.int32, (BLK, LANES), 1) < BLK
    wide_left = lax.broadcasted_iota(jnp.int32, (LANES, LANES), 1) < BLK
    first_bias = jnp.where(left & (chip == 0), NEG, 0.0)
    last_bias = jnp.where((~left) & (chip == chips - 1), NEG, 0.0)

    mine = pl.ds(pl.multiple_of(core * half, half), half)

    @pl.when(core == 1)
    def _():
        edges[0] = edge_a_ref[:, mine]
        edges[1] = edge_b_ref[...]

    @pl.when(core == 0)
    def _():
        edges[0] = edge_b_ref[...]
        edges[1] = edge_a_ref[:, mine]

    def one_head(head, carry):
        cols = pl.ds(pl.multiple_of(head * LANES, LANES), LANES)
        for j in range(n_pairs):
            if j == 0:
                k = jnp.concatenate([edges[0, :BLK, cols], k_ref[BLK : 4 * BLK, cols]], axis=0)
            elif j == n_pairs - 1:
                k = jnp.concatenate([k_ref[j * LANES : j * LANES + 3 * BLK, cols], edges[1, :BLK, cols]], axis=0)
            else:
                k = k_ref[j * LANES : (j + 2) * LANES, cols]
            s_buf[j] = dot_n(k, q_t_ref[cols, j * LANES : (j + 1) * LANES])
        peaks, totals = [], []
        for j in range(n_pairs):
            ends = jnp.where(left, s_buf[j, :BLK], s_buf[j, 3 * BLK :])
            if j == 0:
                ends = ends + first_bias
            if j == n_pairs - 1:
                ends = ends + last_bias
            mid = s_buf[j, BLK : 3 * BLK]
            peak = jnp.max(jnp.maximum(ends, jnp.maximum(mid[:BLK], mid[BLK:])), axis=0, keepdims=True)
            e_ends = jnp.exp2((ends - peak) * scale2)
            e_mid = jnp.exp2((mid - peak) * scale2)
            zero = jnp.zeros_like(e_ends)
            e_buf[j, :BLK] = jnp.where(left, e_ends, zero).astype(jnp.bfloat16)
            e_buf[j, BLK : 3 * BLK] = e_mid.astype(jnp.bfloat16)
            e_buf[j, 3 * BLK :] = jnp.where(left, zero, e_ends).astype(jnp.bfloat16)
            peaks.append(peak)
            totals.append(jnp.sum(e_ends + e_mid[:BLK] + e_mid[BLK:], axis=0, keepdims=True))
        stat_ref[head, 0] = jnp.concatenate(peaks, axis=0)
        stat_ref[head, 1] = jnp.concatenate(totals, axis=0)
        turned = jnp.transpose(jnp.concatenate([edges[0, BLK:, cols], edges[1, BLK:, cols]], axis=0))
        for j in range(n_pairs):
            v_0 = v_t_ref[cols, j * LANES : (j + 1) * LANES]
            v_1 = v_t_ref[cols, (j + 1) * LANES : (j + 2) * LANES]
            if j == 0:
                v_0 = jnp.where(wide_left, turned, v_0)
            if j == n_pairs - 1:
                v_1 = jnp.where(wide_left, v_1, turned)
            acc_ref[head, j] = dot_n(jnp.concatenate([v_0, v_1], axis=1), e_buf[j])
        return carry

    lax.fori_loop(0, half // LANES, one_head, 0)


def far_kernel(
    scale2, q_t_ref, acc_ref, stat_ref, kv_a_ref, kv_b_ref, w_ref, pos_ref, out_ref, s_buf, e_buf, bias, w_cols
):
    half, tokens = q_t_ref.shape
    glob = pos_ref.shape[1]
    heads = half // LANES
    n_pairs = tokens // LANES
    core, chip = device_place()
    glob_block = column_of(pos_ref[...] // BLK)
    for j in range(n_pairs):
        block = (chip * n_pairs + j) * (LANES // BLK) + lax.broadcasted_iota(jnp.int32, (glob, LANES), 1) // BLK
        bias[j] = jnp.where(jnp.abs(glob_block - block.astype(jnp.float32)) > 1.5, 0.0, NEG)
    for head in range(heads):
        row = w_ref[pl.ds(core * heads + head, 1), :]
        w_cols[head] = jnp.transpose(jnp.broadcast_to(row, (LANES, LANES)))

    def one_head(head, carry):
        cols = pl.ds(pl.multiple_of(head * LANES, LANES), LANES)
        kv_a = kv_a_ref[:, cols]
        if on_line():
            kv_a = jnp.where(is_inner(chip), kv_a, jnp.zeros_like(kv_a))
        kv = kv_a + kv_b_ref[:, cols]
        kg = kv[:glob]
        for j in range(n_pairs):
            s_buf[j] = dot_n(kg, q_t_ref[cols, j * LANES : (j + 1) * LANES])
        near_peaks = stat_ref[head, 0]
        near_totals = stat_ref[head, 1]
        near_weights, inverses = [], []
        for j in range(n_pairs):
            far = s_buf[j] + bias[j]
            near_peak = near_peaks[j : j + 1]
            peak = jnp.maximum(jnp.max(far, axis=0, keepdims=True), near_peak)
            e_far = jnp.exp2((far - peak) * scale2)
            e_buf[j] = e_far.astype(jnp.bfloat16)
            near_weight = jnp.exp2((near_peak - peak) * scale2)
            total = near_totals[j : j + 1] * near_weight + jnp.sum(e_far, axis=0, keepdims=True)
            near_weights.append(near_weight)
            inverses.append(1.0 / total)
        vg_t = jnp.transpose(kv[glob:])
        w = w_cols[head]
        lins, sqs = [], []
        for j in range(n_pairs):
            acc = acc_ref[head, j] * near_weights[j] + dot_n(vg_t, e_buf[j])
            lins.append(jnp.sum(acc * w, axis=0, keepdims=True) * inverses[j])
            sqs.append(jnp.sum(acc * acc, axis=0, keepdims=True) * (inverses[j] * inverses[j]))
        lin, sq = carry
        return lin + jnp.concatenate(lins, axis=0), sq + jnp.concatenate(sqs, axis=0)

    none = jnp.zeros((n_pairs, LANES), jnp.float32)
    lin, sq = lax.fori_loop(0, heads, one_head, (none, none))
    out_ref[0] = lin
    out_ref[1] = sq


def call(kernel, name, outs, args, scratch=(), micros=0.0, from_hbm=False):
    spec = pl.BlockSpec(memory_space=pltpu.VMEM)
    source = pltpu.HBM if from_hbm else pltpu.VMEM
    single = not isinstance(outs, list)
    shapes = [outs] if single else outs
    result = pl.pallas_call(
        kernel,
        in_specs=[pl.BlockSpec(memory_space=source)] * len(args),
        out_specs=[spec] * len(shapes),
        out_shape=[pltpu.VMEM(shape, dtype) for shape, dtype in shapes],
        scratch_shapes=[pltpu.VMEM(*x) if isinstance(x, tuple) else x for x in scratch],
        compiler_params=pltpu.CompilerParams(vmem_limit_bytes=16 * 1024 * 1024),
        cost_estimate=pl.CostEstimate(flops=int(micros * 1e9) + 1, transcendentals=0, bytes_accessed=1),
        name=name,
    )(*[pltpu.with_memory_space_constraint(x, source) for x in args])
    return result[0] if single else result


def on_device(queries, keys, values, global_positions, score_weight):
    rows, model_width = queries.shape
    head_size = model_width // HEADS
    half = model_width // CORES
    half_heads = HEADS // CORES
    glob = global_positions.shape[0]
    seq_count = lax.axis_size("seq")
    chips = seq_count // CORES
    scale2 = head_size ** (-0.5) * LOG2E
    bf16 = jnp.bfloat16
    f32 = jnp.float32
    rounds = int(math.log2(chips))
    tokens = CORES * rows
    n_pairs = tokens // LANES

    def swap(x, mask):
        return lax.ppermute(x, "seq", [(i, i ^ mask) for i in range(seq_count)])

    def move_cores(x):
        moves = [(i, i + (CORES if i % CORES else -CORES)) for i in range(seq_count)]
        return lax.ppermute(x, "seq", [(i, to) for i, to in moves if 0 <= to < seq_count])

    def move(x, pairs):
        return lax.ppermute(x, "seq", [(a * CORES + c, b * CORES + c) for a, b in pairs for c in range(CORES)])

    inward = ((0, 1), (3, 2))
    across = ((1, 2), (2, 1))
    outward = ((1, 0), (2, 3))

    def after(arrays, *others):
        return lax.optimization_barrier((*arrays, *others))[: len(arrays)]

    row_positions = global_positions.reshape(1, glob)
    small = ((glob, half), bf16)
    pair_of = ((2 * glob, half), bf16)
    three = ((3 * glob, half), bf16)
    bulk = ((3 * rows, half), bf16)
    edge = ((2 * BLK, half), bf16)
    own, sib, edge_own, mine, bulk_sib = call(
        functools.partial(select_kernel, half),
        "select_rows",
        [three, three, ((2 * BLK, model_width), bf16), bulk, bulk],
        [row_positions, queries, keys, values],
        [((1, glob), jnp.int32), pltpu.SemaphoreType.DMA((9,))],
        from_hbm=True,
    )
    q_near, kv_near = call(join_kernel, "join_cores", [small, pair_of], [own, swap(sib, 1)])
    edge_a = move_cores(edge_own)
    bulk_sib = after((bulk_sib,), q_near)[0]
    bulk_recv = swap(bulk_sib, 1)
    for r in range(1, rounds):
        q_near = call(add_kernel, "add_queries", small, [q_near, swap(q_near, 1 << r)])
    edge_a = after((edge_a,), q_near)[0]
    q_far = swap(q_near, 1 << rounds)
    edge_b = swap(call(edge_kernel, "split_edges", edge, [edge_a]), 1)
    bulk_recv = after((bulk_recv,), q_near)[0]
    k_all, v_t, q_t = call(
        prepare_kernel,
        "prepare",
        [((tokens + 2 * BLK, half), bf16), ((half, tokens + 2 * BLK), bf16), ((half, tokens), bf16)],
        [mine, bulk_recv],
        [((tokens + 2 * BLK, half), bf16)],
        micros=1.6,
    )
    near_acc, near_stat = call(
        functools.partial(near_kernel, scale2),
        "near_attention",
        [((half_heads, n_pairs, head_size, LANES), f32), ((half_heads, 2, n_pairs, LANES), f32)],
        [q_t, k_all, v_t, edge_a, edge_b],
        [((n_pairs, 4 * BLK, LANES), f32), ((n_pairs, 4 * BLK, LANES), bf16), ((2, 2 * BLK, half), bf16)],
        micros=4.0,
    )
    kv_near = after((kv_near,), k_all)[0]
    if chips == 4:
        kv_near = call(add_kernel, "add_keys_values", pair_of, [kv_near, move(kv_near, inward)])
        kv_near = call(add_kernel, "add_keys_values", pair_of, [kv_near, move(kv_near, across)])
        kv_far = move(kv_near, outward)
    else:
        for r in range(1, rounds):
            kv_near = call(add_kernel, "add_keys_values", pair_of, [kv_near, swap(kv_near, 1 << r)])
        kv_far = swap(kv_near, 1 << rounds)

    part = ((half_heads // 2, head_size + STAT_ROWS, LANES), bf16)
    message = call(
        functools.partial(global_kernel, scale2),
        "global_partial",
        part,
        [q_near, q_far, k_all, v_t],
        [((half_heads // 2, tokens, LANES), f32), ((half_heads // 2, tokens + 2 * BLK, LANES), bf16)],
        micros=20.0,
    )
    weights = score_weight.reshape(HEADS, head_size)
    if chips == 3:
        message = call(
            functools.partial(inward_kernel, scale2), "merge_partial", part, [message, after((move(message, inward),), kv_near)[0]]
        )
        message_far = move(message, across)
    else:
        for r in range(1, rounds):
            message = call(
                functools.partial(merge_kernel, scale2), "merge_partial", part, [message, after((swap(message, 1 << r),), kv_near)[0]]
            )
        message_far = swap(message, 1 << rounds)
    sums = call(
        functools.partial(sums_kernel, scale2), "global_sums", ((8, LANES), f32), [message, message_far, weights]
    )
    sums_far = sums

    window = call(
        functools.partial(far_kernel, scale2),
        "far_attention",
        ((2, n_pairs, LANES), f32),
        [q_t, near_acc, near_stat, kv_near, kv_far, weights, row_positions],
        [
            ((n_pairs, glob, LANES), f32),
            ((n_pairs, glob, LANES), bf16),
            ((n_pairs, glob, LANES), f32),
            ((half_heads, LANES, LANES), f32),
        ],
        micros=2.0,
    )
    share = ((2, n_pairs // CORES, LANES), f32)
    mine, theirs = call(
        place_kernel, "place_global", [share, share], [sums, sums_far, row_positions, window]
    )
    theirs = swap(theirs, 1)
    lin = mine[0] + theirs[0]
    sq = mine[1] + theirs[1]
    return (lin * lax.rsqrt(sq * (1.0 / model_width) + 1e-06)).reshape(rows)


def solution(mesh):
    placed = (
        P(("doc", "seq"), None),
        P(("doc", "seq"), None),
        P(("doc", "seq"), None),
        P("doc"),
        P(),
    )
    return jax.shard_map(
        on_device, mesh=mesh, in_specs=placed, out_specs=P(("doc", "seq")), check_vma=False
    )
```

```python
import functools
import math

import jax
import jax.numpy as jnp
from jax import lax
from jax.experimental import pallas as pl
from jax.experimental.pallas import tpu as pltpu
from jax.sharding import PartitionSpec as P

HEADS = 16
BLK = 64
CORES = 2
LANES = 128
NEG = -1e30
LOG2E = math.log2(math.e)
STAT_ROWS = 16


def pieces(x):
    hi = x.astype(jnp.bfloat16)
    rest = x - hi.astype(jnp.float32)
    mid = rest.astype(jnp.bfloat16)
    low = (rest - mid.astype(jnp.float32)).astype(jnp.bfloat16)
    return hi, mid, low


def dot_t(a, b):
    return lax.dot_general(a, b, (((1,), (1,)), ((), ())), preferred_element_type=jnp.float32)


def dot_n(a, b):
    return lax.dot_general(a, b, (((1,), (0,)), ((), ())), preferred_element_type=jnp.float32)


def put_message(out_ref, pair, out, peak, total):
    rows = out.shape[0]
    out_ref[pair, :rows, :] = out.astype(jnp.bfloat16)
    stats = [p.astype(jnp.float32) for p in (*pieces(peak), *pieces(total))]
    row = lax.broadcasted_iota(jnp.int32, (STAT_ROWS, LANES), 0)
    block = jnp.zeros((STAT_ROWS, LANES), jnp.float32)
    for i, stat in enumerate(stats):
        block = jnp.where(row == i, jnp.broadcast_to(stat, block.shape), block)
    out_ref[pair, rows:, :] = block.astype(jnp.bfloat16)


def get_message(ref, pair, head_size):
    out = ref[pair, :head_size, :].astype(jnp.float32)
    stats = ref[pair, head_size:, :].astype(jnp.float32)
    peak = stats[0:1] + stats[1:2] + stats[2:3]
    total = stats[3:4] + stats[4:5] + stats[5:6]
    return out, peak, total


def merged(a, b, scale2):
    out_a, peak_a, total_a = a
    out_b, peak_b, total_b = b
    peak = jnp.maximum(peak_a, peak_b)
    weight_a = jnp.exp2((peak_a - peak) * scale2) * total_a
    weight_b = jnp.exp2((peak_b - peak) * scale2) * total_b
    total = weight_a + weight_b
    inv = 1.0 / total
    return out_a * (weight_a * inv) + out_b * (weight_b * inv), peak, total


def device_place():
    index = lax.axis_index("seq")
    return index % CORES, index // CORES


def column_of(row):
    wide = jnp.concatenate([row, row], axis=1).astype(jnp.float32)
    return jnp.transpose(jnp.broadcast_to(wide, (LANES, LANES)))[: row.shape[1]]


def own_positions(pos_ref, rows):
    core, chip = device_place()
    row = (chip * CORES + core) * rows + lax.broadcasted_iota(jnp.int32, (rows, pos_ref.shape[1]), 0)
    return jnp.where(row == pos_ref[...], 1.0, 0.0).astype(jnp.bfloat16)


def select_kernel(half, pos_hbm, q_hbm, k_hbm, v_hbm, sel_ref, sib_ref, edge_ref, mine_ref, bulk_ref, pos_ref, sems):
    rows = q_hbm.shape[0]
    core, _ = device_place()
    block = pl.ds(pl.multiple_of(core * (rows - BLK), BLK), BLK)
    pos_copy = pltpu.make_async_copy(pos_hbm, pos_ref, sems.at[0])
    copies = []
    for i, x_hbm in enumerate((q_hbm, k_hbm, v_hbm)):
        for to_ref, which in ((bulk_ref, 1 - core), (mine_ref, core)):
            cols = pl.ds(pl.multiple_of(which * half, half), half)
            to = to_ref.at[i * rows : (i + 1) * rows, :]
            copies.append(pltpu.make_async_copy(x_hbm.at[:, cols], to, sems.at[1 + len(copies)]))
    edges = [
        pltpu.make_async_copy(x_hbm.at[block, :], edge_ref.at[i * BLK : (i + 1) * BLK, :], sems.at[7 + i])
        for i, x_hbm in enumerate((k_hbm, v_hbm))
    ]
    for copy in (pos_copy, *copies, *edges):
        copy.start()
    pos_copy.wait()
    hit = own_positions(pos_ref, rows)
    glob = hit.shape[1]
    contract = (((0,), (0,)), ((), ()))
    for i in range(3):
        for copy, x_ref, out_ref in ((copies[2 * i], bulk_ref, sib_ref), (copies[2 * i + 1], mine_ref, sel_ref)):
            copy.wait()
            x = x_ref[i * rows : (i + 1) * rows, :]
            picked = lax.dot_general(hit, x, contract, preferred_element_type=jnp.float32)
            out_ref[i * glob : (i + 1) * glob, :] = picked.astype(jnp.bfloat16)
    for copy in edges:
        copy.wait()


def join_kernel(own_ref, recv_ref, q_ref, kv_ref):
    count = q_ref.shape[0]
    q_ref[...] = own_ref[:count, :] + recv_ref[:count, :]
    kv_ref[...] = own_ref[count:, :] + recv_ref[count:, :]


def edge_kernel(full_ref, out_ref):
    half = out_ref.shape[1]
    core, _ = device_place()
    out_ref[...] = full_ref[:, pl.ds(pl.multiple_of((1 - core) * half, half), half)]


def add_kernel(a_ref, b_ref, out_ref):
    out_ref[...] = a_ref[...] + b_ref[...]


def on_line():
    return lax.axis_size("seq") // CORES == 4


def is_inner(chip):
    return (chip == 1) | (chip == 2)


def prepare_kernel(own_ref, sib_ref, k_ref, v_t_ref, q_t_ref, v_all):
    rows = own_ref.shape[0] // 3
    half = k_ref.shape[1]
    core, _ = device_place()
    zero = jnp.zeros((BLK, half), jnp.bfloat16)
    for ref in (k_ref, v_all):
        ref[:BLK, :] = zero
        ref[BLK + CORES * rows :, :] = zero
    for part_ref, which in ((own_ref, core), (sib_ref, 1 - core)):
        at = pl.ds(pl.multiple_of(which * rows + BLK, BLK), rows)
        k_ref[at, :] = part_ref[rows : 2 * rows, :]
        v_all[at, :] = part_ref[2 * rows :, :]

    def turn(head, carry):
        lanes = pl.ds(pl.multiple_of(head * LANES, LANES), LANES)
        v_t_ref[lanes, :] = jnp.transpose(v_all[:, lanes])
        for part_ref, which in ((own_ref, core), (sib_ref, 1 - core)):
            q_t_ref[lanes, pl.ds(pl.multiple_of(which * rows, LANES), rows)] = jnp.transpose(part_ref[:rows, lanes])
        return carry

    lax.fori_loop(0, half // LANES, turn, 0)


def global_kernel(scale2, q_a_ref, q_b_ref, k_ref, v_t_ref, out_ref, s_buf, e_buf):
    glob, half = q_a_ref.shape
    head_size = LANES
    pairs = half // (2 * head_size)
    tokens = k_ref.shape[0] - 2 * BLK
    row = lax.broadcasted_iota(jnp.int32, (2 * glob, 2 * head_size), 0)
    col = lax.broadcasted_iota(jnp.int32, (2 * glob, 2 * head_size), 1)
    keep = (row < glob) == (col < head_size)
    lane = lax.broadcasted_iota(jnp.int32, (head_size, LANES), 1)
    for pair in range(pairs):
        cols = slice(2 * pair * head_size, 2 * (pair + 1) * head_size)
        q = q_a_ref[:, cols] + q_b_ref[:, cols]
        doubled = jnp.concatenate([q, q], axis=0)
        diag = jnp.where(keep, doubled, jnp.zeros_like(doubled))
        s_buf[pair] = dot_t(k_ref[BLK : BLK + tokens, cols], diag)
    stats = []
    for pair in range(pairs):
        s = s_buf[pair]
        peak = jnp.max(s, axis=0, keepdims=True)
        e = jnp.exp2((s - peak) * scale2)
        stats.append((peak, jnp.sum(e, axis=0, keepdims=True)))
        zero = jnp.zeros((BLK, LANES), jnp.bfloat16)
        e_buf[pair, :BLK] = zero
        e_buf[pair, BLK + tokens :] = zero
        e_buf[pair, BLK : BLK + tokens] = e.astype(jnp.bfloat16)
    for pair in range(pairs):
        rows = slice(2 * pair * head_size, 2 * (pair + 1) * head_size)
        acc = dot_n(v_t_ref[rows, :], e_buf[pair])
        peak, total = stats[pair]
        out = jnp.where(lane < glob, acc[:head_size], acc[head_size:]) / total
        put_message(out_ref, pair, out, peak, total)


def merge_kernel(scale2, a_ref, b_ref, out_ref):
    head_size = a_ref.shape[1] - STAT_ROWS
    for pair in range(a_ref.shape[0]):
        a = get_message(a_ref, pair, head_size)
        b = get_message(b_ref, pair, head_size)
        put_message(out_ref, pair, *merged(a, b, scale2))


def inward_kernel(scale2, a_ref, b_ref, out_ref):
    _, chip = device_place()

    @pl.when(is_inner(chip))
    def _():
        merge_kernel(scale2, a_ref, b_ref, out_ref)

    @pl.when(jnp.logical_not(is_inner(chip)))
    def _():
        out_ref[...] = a_ref[...]


def sums_kernel(scale2, a_ref, b_ref, w_ref, out_ref):
    pairs = a_ref.shape[0]
    head_size = a_ref.shape[1] - STAT_ROWS
    glob = LANES // 2
    core, chip = device_place()
    upper = lax.broadcasted_iota(jnp.int32, (LANES, head_size), 0) < glob
    lin = jnp.zeros((1, LANES), jnp.float32)
    sq = jnp.zeros((1, LANES), jnp.float32)
    for pair in range(pairs):
        a = get_message(a_ref, pair, head_size)
        b = get_message(b_ref, pair, head_size)
        if False:
            b = tuple(jnp.where(is_inner(chip), y, x) for x, y in zip(a, b))
        out, _, _ = merged(a, b, scale2)
        w_a = w_ref[pl.ds(core * 2 * pairs + 2 * pair, 1), :]
        w_b = w_ref[pl.ds(core * 2 * pairs + 2 * pair + 1, 1), :]
        w = jnp.transpose(jnp.where(upper, w_a, w_b))
        lin = lin + jnp.sum(out * w, axis=0, keepdims=True)
        sq = sq + jnp.sum(out * out, axis=0, keepdims=True)
    out_ref[...] = jnp.zeros_like(out_ref)
    out_ref[0:1, :] = lin + pltpu.roll(lin, glob, 1)
    out_ref[1:2, :] = sq + pltpu.roll(sq, glob, 1)


def place_kernel(own_sums_ref, far_sums_ref, pos_ref, win_ref, own_ref, sib_ref):
    glob = pos_ref.shape[1]
    core, chip = device_place()
    sums = own_sums_ref[...]
    if False:
        sums = jnp.where(is_inner(chip), sums, far_sums_ref[...])
    parts = [p.astype(jnp.float32) for p in (*pieces(sums[0:1]), *pieces(sums[1:2]))] + [jnp.ones((1, LANES), jnp.float32)]
    row = lax.broadcasted_iota(jnp.int32, (16, LANES), 0)
    table = jnp.zeros((16, LANES), jnp.float32)
    for i, part in enumerate(parts):
        table = jnp.where(row == i, jnp.broadcast_to(part, table.shape), table)
    table = table.astype(jnp.bfloat16)[:, :glob]
    pos = column_of(pos_ref[...])
    n_pairs = win_ref.shape[1]
    each = n_pairs // CORES
    for out_ref, which in ((sib_ref, 1 - core), (own_ref, core)):
        for j in range(each):
            pair = which * each + j
            token = (chip * n_pairs + pair) * LANES + lax.broadcasted_iota(jnp.int32, (glob, LANES), 1)
            hit = jnp.where(pos == token.astype(jnp.float32), 1.0, 0.0).astype(jnp.bfloat16)
            placed = dot_n(table, hit)
            is_glob = placed[6:7] > 0.5
            for i in (0, 1):
                value = placed[3 * i : 3 * i + 1] + placed[3 * i + 1 : 3 * i + 2] + placed[3 * i + 2 : 3 * i + 3]
                out_ref[i, j : j + 1, :] = jnp.where(is_glob, value, win_ref[i, pl.ds(pair, 1), :])


def near_kernel(
    scale2,
    q_t_ref,
    k_ref,
    v_t_ref,
    edge_a_ref,
    edge_b_ref,
    w_ref,
    pos_ref,
    acc_ref,
    stat_ref,
    bias,
    w_cols,
    s_buf,
    e_buf,
    edges,
):
    half, tokens = q_t_ref.shape
    n_pairs = tokens // LANES
    core, chip = device_place()
    chips = lax.axis_size("seq") // CORES
    left = lax.broadcasted_iota(jnp.int32, (BLK, LANES), 1) < BLK
    wide_left = lax.broadcasted_iota(jnp.int32, (LANES, LANES), 1) < BLK
    first_bias = jnp.where(left & (chip == 0), NEG, 0.0)
    last_bias = jnp.where((~left) & (chip == chips - 1), NEG, 0.0)

    mine = pl.ds(pl.multiple_of(core * half, half), half)

    @pl.when(core == 1)
    def _():
        edges[0] = edge_a_ref[:, mine]
        edges[1] = edge_b_ref[...]

    @pl.when(core == 0)
    def _():
        edges[0] = edge_b_ref[...]
        edges[1] = edge_a_ref[:, mine]

    glob = pos_ref.shape[1]
    heads = half // LANES
    glob_block = column_of(pos_ref[...] // BLK)
    for j in range(n_pairs):
        block = (chip * n_pairs + j) * (LANES // BLK) + lax.broadcasted_iota(jnp.int32, (glob, LANES), 1) // BLK
        bias[j] = jnp.where(jnp.abs(glob_block - block.astype(jnp.float32)) > 1.5, 0.0, NEG)
    for head in range(heads):
        row = w_ref[pl.ds(core * heads + head, 1), :]
        w_cols[head] = jnp.transpose(jnp.broadcast_to(row, (LANES, LANES)))

    def one_head(head, carry):
        cols = pl.ds(pl.multiple_of(head * LANES, LANES), LANES)
        for j in range(n_pairs):
            if j == 0:
                k = jnp.concatenate([edges[0, :BLK, cols], k_ref[BLK : 4 * BLK, cols]], axis=0)
            elif j == n_pairs - 1:
                k = jnp.concatenate([k_ref[j * LANES : j * LANES + 3 * BLK, cols], edges[1, :BLK, cols]], axis=0)
            else:
                k = k_ref[j * LANES : (j + 2) * LANES, cols]
            s_buf[j] = dot_n(k, q_t_ref[cols, j * LANES : (j + 1) * LANES])
        peaks, totals = [], []
        for j in range(n_pairs):
            ends = jnp.where(left, s_buf[j, :BLK], s_buf[j, 3 * BLK :])
            if j == 0:
                ends = ends + first_bias
            if j == n_pairs - 1:
                ends = ends + last_bias
            mid = s_buf[j, BLK : 3 * BLK]
            peak = jnp.max(jnp.maximum(ends, jnp.maximum(mid[:BLK], mid[BLK:])), axis=0, keepdims=True)
            e_ends = jnp.exp2((ends - peak) * scale2)
            e_mid = jnp.exp2((mid - peak) * scale2)
            zero = jnp.zeros_like(e_ends)
            e_buf[j, :BLK] = jnp.where(left, e_ends, zero).astype(jnp.bfloat16)
            e_buf[j, BLK : 3 * BLK] = e_mid.astype(jnp.bfloat16)
            e_buf[j, 3 * BLK :] = jnp.where(left, zero, e_ends).astype(jnp.bfloat16)
            peaks.append(peak)
            totals.append(jnp.sum(e_ends + e_mid[:BLK] + e_mid[BLK:], axis=0, keepdims=True))
        stat_ref[head, 0] = jnp.concatenate(peaks, axis=0)
        stat_ref[head, 1] = jnp.concatenate(totals, axis=0)
        turned = jnp.transpose(jnp.concatenate([edges[0, BLK:, cols], edges[1, BLK:, cols]], axis=0))
        for j in range(n_pairs):
            v_0 = v_t_ref[cols, j * LANES : (j + 1) * LANES]
            v_1 = v_t_ref[cols, (j + 1) * LANES : (j + 2) * LANES]
            if j == 0:
                v_0 = jnp.where(wide_left, turned, v_0)
            if j == n_pairs - 1:
                v_1 = jnp.where(wide_left, v_1, turned)
            acc_ref[head, j] = dot_n(jnp.concatenate([v_0, v_1], axis=1), e_buf[j])
        return carry

    lax.fori_loop(0, half // LANES, one_head, 0, unroll=1)


def far_kernel(
    scale2, q_t_ref, acc_ref, stat_ref, kv_a_ref, kv_b_ref, bias, w_cols, out_ref, s_buf, e_buf
):
    half, tokens = q_t_ref.shape
    glob = bias.shape[1]
    heads = half // LANES
    n_pairs = tokens // LANES
    core, chip = device_place()
    def one_head(head, carry):
        cols = pl.ds(pl.multiple_of(head * LANES, LANES), LANES)
        kv_a = kv_a_ref[:, cols]
        if on_line():
            kv_a = jnp.where(is_inner(chip), kv_a, jnp.zeros_like(kv_a))
        kv = kv_a + kv_b_ref[:, cols]
        kg = kv[:glob]
        for j in range(n_pairs):
            s_buf[head, j] = dot_n(kg, q_t_ref[cols, j * LANES : (j + 1) * LANES])
        near_peaks = stat_ref[head, 0]
        near_totals = stat_ref[head, 1]
        near_weights, inverses = [], []
        for j in range(n_pairs):
            far = s_buf[head, j] + bias[j]
            near_peak = near_peaks[j : j + 1]
            peak = jnp.maximum(jnp.max(far, axis=0, keepdims=True), near_peak)
            e_far = jnp.exp2((far - peak) * scale2)
            e_buf[head, j] = e_far.astype(jnp.bfloat16)
            near_weight = jnp.exp2((near_peak - peak) * scale2)
            total = near_totals[j : j + 1] * near_weight + jnp.sum(e_far, axis=0, keepdims=True)
            near_weights.append(near_weight)
            inverses.append(1.0 / total)
        vg_t = jnp.transpose(kv[glob:])
        w = w_cols[head]
        lins, sqs = [], []
        for j in range(n_pairs):
            acc = acc_ref[head, j] * near_weights[j] + dot_n(vg_t, e_buf[head, j])
            lins.append(jnp.sum(acc * w, axis=0, keepdims=True) * inverses[j])
            sqs.append(jnp.sum(acc * acc, axis=0, keepdims=True) * (inverses[j] * inverses[j]))
        lin, sq = carry
        return lin + jnp.concatenate(lins, axis=0), sq + jnp.concatenate(sqs, axis=0)

    none = jnp.zeros((n_pairs, LANES), jnp.float32)
    lin, sq = lax.fori_loop(0, heads, one_head, (none, none), unroll=8)
    out_ref[0] = lin
    out_ref[1] = sq


def call(kernel, name, outs, args, scratch=(), micros=0.0, from_hbm=False):
    spec = pl.BlockSpec(memory_space=pltpu.VMEM)
    source = pltpu.HBM if from_hbm else pltpu.VMEM
    single = not isinstance(outs, list)
    shapes = [outs] if single else outs
    result = pl.pallas_call(
        kernel,
        in_specs=[pl.BlockSpec(memory_space=source)] * len(args),
        out_specs=[spec] * len(shapes),
        out_shape=[pltpu.VMEM(shape, dtype) for shape, dtype in shapes],
        scratch_shapes=[pltpu.VMEM(*x) if isinstance(x, tuple) else x for x in scratch],
        compiler_params=pltpu.CompilerParams(vmem_limit_bytes=16 * 1024 * 1024),
        cost_estimate=pl.CostEstimate(flops=int(micros * 1e9) + 1, transcendentals=0, bytes_accessed=1),
        name=name,
    )(*[pltpu.with_memory_space_constraint(x, source) for x in args])
    return result[0] if single else result


def on_device(queries, keys, values, global_positions, score_weight):
    rows, model_width = queries.shape
    head_size = model_width // HEADS
    half = model_width // CORES
    half_heads = HEADS // CORES
    glob = global_positions.shape[0]
    seq_count = lax.axis_size("seq")
    chips = seq_count // CORES
    scale2 = head_size ** (-0.5) * LOG2E
    bf16 = jnp.bfloat16
    f32 = jnp.float32
    rounds = int(math.log2(chips))
    tokens = CORES * rows
    n_pairs = tokens // LANES

    def swap(x, mask):
        return lax.ppermute(x, "seq", [(i, i ^ mask) for i in range(seq_count)])

    def move_cores(x):
        moves = [(i, i + (CORES if i % CORES else -CORES)) for i in range(seq_count)]
        return lax.ppermute(x, "seq", [(i, to) for i, to in moves if 0 <= to < seq_count])

    def move(x, pairs):
        return lax.ppermute(x, "seq", [(a * CORES + c, b * CORES + c) for a, b in pairs for c in range(CORES)])

    inward = ((0, 1), (3, 2))
    across = ((1, 2), (2, 1))
    outward = ((1, 0), (2, 3))

    def after(arrays, *others):
        return lax.optimization_barrier((*arrays, *others))[: len(arrays)]

    row_positions = global_positions.reshape(1, glob)
    weights = score_weight.reshape(HEADS, head_size)
    small = ((glob, half), bf16)
    pair_of = ((2 * glob, half), bf16)
    three = ((3 * glob, half), bf16)
    bulk = ((3 * rows, half), bf16)
    edge = ((2 * BLK, half), bf16)
    own, sib, edge_own, mine, bulk_sib = call(
        functools.partial(select_kernel, half),
        "select_rows",
        [three, three, ((2 * BLK, model_width), bf16), bulk, bulk],
        [row_positions, queries, keys, values],
        [((1, glob), jnp.int32), pltpu.SemaphoreType.DMA((9,))],
        from_hbm=True,
    )
    q_near, kv_near = call(join_kernel, "join_cores", [small, pair_of], [own, swap(sib, 1)])
    edge_a = move_cores(edge_own)
    bulk_sib = after((bulk_sib,), q_near)[0]
    bulk_recv = swap(bulk_sib, 1)
    for r in range(1, rounds):
        q_near = call(add_kernel, "add_queries", small, [q_near, swap(q_near, 1 << r)])
    edge_a = after((edge_a,), q_near)[0]
    q_far = swap(q_near, 1 << rounds)
    edge_b = swap(call(edge_kernel, "split_edges", edge, [edge_a]), 1)
    bulk_recv = after((bulk_recv,), q_near)[0]
    k_all, v_t, q_t = call(
        prepare_kernel,
        "prepare",
        [((tokens + 2 * BLK, half), bf16), ((half, tokens + 2 * BLK), bf16), ((half, tokens), bf16)],
        [mine, bulk_recv],
        [((tokens + 2 * BLK, half), bf16)],
        micros=1.6,
    )
    near_acc, near_stat, bias, weight_cols = call(
        functools.partial(near_kernel, scale2),
        "near_attention",
        [
            ((half_heads, n_pairs, head_size, LANES), f32),
            ((half_heads, 2, n_pairs, LANES), f32),
            ((n_pairs, glob, LANES), f32),
            ((half_heads, LANES, LANES), f32),
        ],
        [q_t, k_all, v_t, edge_a, edge_b, weights, row_positions],
        [((n_pairs, 4 * BLK, LANES), f32), ((n_pairs, 4 * BLK, LANES), bf16), ((2, 2 * BLK, half), bf16)],
        micros=4.0,
    )
    kv_near = after((kv_near,), k_all)[0]
    if chips == 4:
        kv_near = call(add_kernel, "add_keys_values", pair_of, [kv_near, move(kv_near, inward)])
        kv_near = call(add_kernel, "add_keys_values", pair_of, [kv_near, move(kv_near, across)])
        kv_far = move(kv_near, outward)
    else:
        for r in range(1, rounds):
            kv_near = call(add_kernel, "add_keys_values", pair_of, [kv_near, swap(kv_near, 1 << r)])
        kv_far = swap(kv_near, 1 << rounds)

    part = ((half_heads // 2, head_size + STAT_ROWS, LANES), bf16)
    message = call(
        functools.partial(global_kernel, scale2),
        "global_partial",
        part,
        [q_near, q_far, k_all, v_t],
        [((half_heads // 2, tokens, LANES), f32), ((half_heads // 2, tokens + 2 * BLK, LANES), bf16)],
        micros=20.0,
    )
    if chips == 3:
        message = call(
            functools.partial(inward_kernel, scale2), "merge_partial", part, [message, after((move(message, inward),), kv_near)[0]]
        )
        message_far = move(message, across)
    else:
        for r in range(1, rounds):
            message = call(
                functools.partial(merge_kernel, scale2), "merge_partial", part, [message, after((swap(message, 1 << r),), kv_near)[0]]
            )
        message_far = swap(message, 1 << rounds)
    sums = call(
        functools.partial(sums_kernel, scale2), "global_sums", ((8, LANES), f32), [message, message_far, weights]
    )
    sums_far = sums

    window = call(
        functools.partial(far_kernel, scale2),
        "far_attention",
        ((2, n_pairs, LANES), f32),
        [q_t, near_acc, near_stat, kv_near, kv_far, bias, weight_cols],
        [
            ((half_heads, n_pairs, glob, LANES), f32),
            ((half_heads, n_pairs, glob, LANES), bf16),
        ],
        micros=2.0,
    )
    share = ((2, n_pairs // CORES, LANES), f32)
    mine, theirs = call(
        place_kernel, "place_global", [share, share], [sums, sums_far, row_positions, window]
    )
    theirs = swap(theirs, 1)
    lin = mine[0] + theirs[0]
    sq = mine[1] + theirs[1]
    return (lin * lax.rsqrt(sq * (1.0 / model_width) + 1e-06)).reshape(rows)


def solution(mesh):
    placed = (
        P(("doc", "seq"), None),
        P(("doc", "seq"), None),
        P(("doc", "seq"), None),
        P("doc"),
        P(),
    )
    return jax.shard_map(
        on_device, mesh=mesh, in_specs=placed, out_specs=P(("doc", "seq")), check_vma=False
    )
```
